128 devices in a mesh: lat: 8 (over y_hi, x), lon: 16 (over z, y_lo, core).
Axes of the slice: x: 4, y: 4 (y_hi: 2, y_lo: 2; y = y_hi * 2 + y_lo), z: 4, core: 2. Of those that a mesh axis runs over, the one named last changes fastest.
Arguments:
- state: bfloat16 [64, 512, 128], P('lat', 'lon'), may hold values from -6 to 6
- kernel_in: bfloat16 [3, 3, 3, 32, 32], replicated, may hold values from -0.21875 to 0.21875
- kernel_mid: bfloat16 [3, 3, 3, 32, 64], replicated, may hold values from -0.21875 to 0.21875
- kernel_out: bfloat16 [3, 3, 3, 32, 32], replicated, may hold values from -0.21875 to 0.21875
- lift: bfloat16 [64, 32], replicated, may hold values from -0.75 to 0.75
- obs_cells: int32 [8, 256, 256, 4], P('lat', 'lon'), may hold values from 0 to 255, as said below
- obs_chan: int32 [8, 256, 256], P('lat', 'lon'), may hold values from 0 to 127
- obs_weights: float32 [8, 256, 256, 4], P('lat', 'lon'), may hold values from 0 to 1
- obs_value: float32 [8, 256, 256], P('lat', 'lon'), may hold values from -6 to 6
- obs_count: int32 [8, 256], P('lat', 'lon'), may hold values from 0 to 256, as said below
Outputs:
- gradient: float32 [64, 512, 128], P('lat', 'lon')
- innovation: float32 [8, 256, 256], P('lat', 'lon')
The draws below stay inside these ranges and needn't reach their ends.
Inputs may be any that keep to these rules, and one draw needn't show every extreme that they name: `obs_cells`: each slot's four cells are a base cell, the next column, the next row and the cell diagonal to it, all inside one tile. `obs_count`: in every latitude tile row some destination tile receives 256 live slots from every owner.
All inputs are finite; a program needn't handle non-finite values.
Results may differ from the reference program's by a relative error of at most 0.0075.
Values may be sent and summed in bfloat16 or wider, within the bound.
A program may use at most 64 MiB of HBM per device.

```python
import jax
import jax.numpy as jnp

C = 32
C2 = 64
LEV = 4
LAT_DEV = 8
LON_DEV = 32
CAP = 256
LAT_TILES = 8
LON_TILES = 16
PAIRS = 256
NLAT = 64
NLON = 512


def draw_obs_cells(key, part):
    key_row = jax.random.fold_in(key, 11)
    key_col = jax.random.fold_in(key, 12)
    cell_row = jax.random.randint(key_row, (LAT_TILES, PAIRS, CAP), 0, LAT_DEV - 1)
    cell_col = jax.random.randint(key_col, (LAT_TILES, PAIRS, CAP), 0, LON_DEV - 1)
    cell_row = cell_row.at[0, 0, 0].set(LAT_DEV - 2).at[0, 0, 1].set(0)
    cell_col = cell_col.at[0, 0, 0].set(LON_DEV - 2).at[0, 0, 1].set(0)
    base = cell_row * LON_DEV + cell_col
    return jnp.stack([base, base + 1, base + LON_DEV, base + LON_DEV + 1], axis=-1).astype(jnp.int32)


def draw_obs_count(key, part):
    key_hot = jax.random.fold_in(key, 21)
    key_pick = jax.random.fold_in(key, 22)
    key_base = jax.random.fold_in(key, 23)
    hot = jax.random.randint(key_hot, (LAT_TILES, LON_TILES), 0, 4) == 0
    picked = jax.random.randint(key_pick, (LAT_TILES, 1), 0, LON_TILES)
    hot = jnp.logical_or(hot, jnp.arange(LON_TILES, dtype=jnp.int32)[None, :] == picked)
    base = jax.random.randint(key_base, (LAT_TILES, LON_TILES, LON_TILES), 0, CAP // 2 + 1)
    counts = jnp.where(hot[:, None, :], CAP, base)
    return counts.reshape(LAT_TILES, PAIRS).astype(jnp.int32)


def with_ends(entries, stream_key, low, top_value):
    longest = entries.shape.index(max(entries.shape))
    spots = []
    for shift in (0, 1):
        where = [jax.random.randint(jax.random.fold_in(stream_key, axis), (), 0, length) for axis, length in enumerate(entries.shape)]
        where[longest] = (where[longest] + shift) % entries.shape[longest]
        spots.append(tuple(where))
    return entries.at[spots[0]].set(low).at[spots[1]].set(top_value)


def shard_levels(stream_key, shape, shards, smallest, high):
    loudness, own = 1.0, jax.random.fold_in(stream_key, 6)
    for axis_at, parts in shards:
        draws = jnp.exp(jax.random.uniform(jax.random.fold_in(own, axis_at), (parts,), jnp.float32, smallest / len(shards), high / len(shards)))
        loudness = loudness * jnp.repeat(draws, shape[axis_at] // parts).reshape([-1 if axis == axis_at else 1 for axis in range(len(shape))])
    return loudness


def centred(rng, extent, scale, most, split=(), kind=jnp.bfloat16):
    drawn = scale * jax.random.normal(rng, extent, jnp.float32)
    if split:
        drawn = drawn * shard_levels(rng, extent, split, -0.22, 0.18)
    return jnp.clip(drawn, -most, most).astype(kind)


def setup_inputs(seed: int = 0) -> dict:
    splits = jax.random.split(jax.random.key(seed), 11)
    state = centred(splits[0], (NLAT, NLON, LEV * C), 1.0, 6.0, ((0, 8), (1, 16)))
    kernel_in = centred(splits[1], (3, 3, 3, C, C), (27 * C) ** -0.5, 0.21875)
    kernel_mid = centred(splits[2], (3, 3, 3, C, C2), (27 * C) ** -0.5, 0.21875)
    kernel_out = centred(splits[3], (3, 3, 3, C, C), (27 * C) ** -0.5, 0.21875)
    lift = centred(splits[4], (C2, C), C2 ** -0.5, 0.75)
    obs_cells = draw_obs_cells(jax.random.fold_in(splits[10], 71), 0)
    obs_chan = with_ends(jax.random.randint(splits[6], (LAT_TILES, PAIRS, CAP), 0, LEV * C), jax.random.fold_in(splits[6], 1), 0, (LEV * C) - 1).astype(jnp.int32)
    obs_weights = jnp.clip(1.0 * jax.random.uniform(splits[7], (LAT_TILES, PAIRS, CAP, 4), jnp.float32) ** shard_levels(splits[7], (LAT_TILES, PAIRS, CAP, 4), ((0, 8), (1, 16)), -0.2, 0.2), 0.0, 1.0)
    obs_value = centred(splits[8], (LAT_TILES, PAIRS, CAP), 1.0, 6.0, ((0, 8), (1, 16)), jnp.float32)
    obs_count = draw_obs_count(jax.random.fold_in(splits[10], 71), 0)
    return {"state": state, "kernel_in": kernel_in, "kernel_mid": kernel_mid, "kernel_out": kernel_out, "lift": lift, "obs_cells": obs_cells, "obs_chan": obs_chan, "obs_weights": obs_weights, "obs_value": obs_value, "obs_count": obs_count}


def banded(kernel, levels):
    lin = jnp.arange(levels, dtype=jnp.int32)
    taps = jnp.arange(3, dtype=jnp.int32)
    select = (lin[:, None, None] - lin[None, :, None] + 1 == taps[None, None, :]).astype(jnp.float32)
    full = jnp.einsum("pqt,abtcg->abpcqg", select, kernel.astype(jnp.float32))
    cin = kernel.shape[3]
    cout = kernel.shape[4]
    return full.reshape(9, levels * cin, levels * cout).astype(jnp.bfloat16)


def gelu_slope(value):
    inner = 0.7978845608 * (value + 0.044715 * value ** 3)
    tval = jnp.tanh(inner)
    return 0.5 * (1.0 + tval) + 0.5 * value * (1.0 - tval * tval) * 0.7978845608 * (1.0 + 0.134145 * value * value)


def extend_global(field):
    wide = jnp.concatenate([field[:, -1:], field, field[:, :1]], axis=1)
    return jnp.pad(wide, ((1, 1), (0, 0), (0, 0)))


def convolve(field, matrices):
    rows, cols = field.shape[0], field.shape[1]
    padded = extend_global(field)
    total = jnp.zeros((rows, cols, matrices.shape[2]), jnp.float32)
    for row_off in range(3):
        for col_off in range(3):
            piece = padded[row_off:row_off + rows, col_off:col_off + cols]
            total = total + jnp.einsum("ijf,fg->ijg", piece, matrices[row_off * 3 + col_off], preferred_element_type=jnp.float32)
    return total


def convolve_adjoint(grads, matrices):
    rows, cols = grads.shape[0], grads.shape[1]
    padded = extend_global(grads)
    total = jnp.zeros((rows, cols, matrices.shape[1]), jnp.float32)
    for row_off in range(3):
        for col_off in range(3):
            piece = padded[2 - row_off:2 - row_off + rows, 2 - col_off:2 - col_off + cols]
            total = total + jnp.einsum("ijg,fg->ijf", piece, matrices[row_off * 3 + col_off], preferred_element_type=jnp.float32)
    return total


def widen(coarse):
    rows, cols, feats = coarse.shape
    return jnp.broadcast_to(coarse[:, None, :, None, :], (rows, 2, cols, 2, feats)).reshape(rows * 2, cols * 2, feats)


def block_sum(fine):
    rows, cols, feats = fine.shape
    return fine.reshape(rows // 2, 2, cols // 2, 2, feats).sum(axis=(1, 3))


def reference(state, kernel_in, kernel_mid, kernel_out, lift, obs_cells, obs_chan, obs_weights, obs_value, obs_count):
    feats = LEV * C
    mat_in = banded(kernel_in, LEV)
    mat_mid = banded(kernel_mid, LEV)
    mat_out = banded(kernel_out, LEV)
    lift_full = jnp.einsum("pq,cg->pcqg", jnp.eye(LEV, dtype=jnp.float32), lift.astype(jnp.float32)).reshape(LEV * C2, feats).astype(jnp.bfloat16)
    pre_first = convolve(state, mat_in)
    act_first = jax.nn.gelu(pre_first, approximate=True).astype(jnp.bfloat16)
    pooled = (block_sum(act_first.astype(jnp.float32)) * 0.25).astype(jnp.bfloat16)
    pre_mid = convolve(pooled, mat_mid)
    act_mid = jax.nn.gelu(pre_mid, approximate=True).astype(jnp.bfloat16)
    lifted = jnp.einsum("ijg,gf->ijf", act_mid, lift_full, preferred_element_type=jnp.float32)
    merged = (act_first.astype(jnp.float32) + widen(lifted)).astype(jnp.bfloat16)
    pre_last = convolve(merged, mat_out)
    output = state.astype(jnp.float32) + jax.nn.gelu(pre_last, approximate=True)
    slots = jnp.arange(CAP, dtype=jnp.int32)
    live = (slots[None, None, :] < obs_count[:, :, None]).astype(jnp.float32)
    weights = obs_weights * live[..., None]
    values = obs_value * live
    tile_row = jnp.arange(LAT_TILES, dtype=jnp.int32)[:, None, None, None]
    target = (jnp.arange(PAIRS, dtype=jnp.int32) % LON_TILES)[None, :, None, None]
    cell_row = obs_cells // LON_DEV
    cell_col = obs_cells % LON_DEV
    where_flat = ((tile_row * LAT_DEV + cell_row) * NLON + target * LON_DEV + cell_col) * feats + obs_chan[..., None]
    flat_out = output.reshape(-1)
    samples = flat_out[where_flat]
    innovation = jnp.sum(weights * samples, axis=-1) - values
    terms = (weights * innovation[..., None]).reshape(-1)
    grad_out = jnp.zeros((NLAT * NLON * feats,), jnp.float32).at[where_flat.reshape(-1)].add(terms).reshape(NLAT, NLON, feats)
    grad_pre_last = (grad_out * gelu_slope(pre_last)).astype(jnp.bfloat16)
    grad_merged = convolve_adjoint(grad_pre_last, mat_out)
    grad_coarse = block_sum(grad_merged).astype(jnp.bfloat16)
    back_mid = jnp.einsum("ijf,gf->ijg", grad_coarse, lift_full, preferred_element_type=jnp.float32)
    grad_mid = (back_mid * gelu_slope(pre_mid)).astype(jnp.bfloat16)
    grad_pooled = convolve_adjoint(grad_mid, mat_mid)
    grad_first = ((grad_merged + widen(grad_pooled) * 0.25) * gelu_slope(pre_first)).astype(jnp.bfloat16)
    gradient = grad_out + convolve_adjoint(grad_first, mat_in)
    return gradient, innovation
```

```python
import jax
import jax.numpy as jnp
from jax import lax
from jax.sharding import PartitionSpec as P

C = 32
C2 = 64
LEV = 4


def with_halo(block, sides, width, periodic):
    for axis, dim in sides:
        count = lax.axis_size(axis)
        forward = [(i, i + 1) for i in range(count - 1)]
        if periodic:
            forward.append((count - 1, 0))
        backward = [(target, source) for source, target in forward]
        low = lax.ppermute(
            lax.slice_in_dim(block, block.shape[dim] - width, None, axis=dim), axis, forward
        )
        high = lax.ppermute(lax.slice_in_dim(block, 0, width, axis=dim), axis, backward)
        block = jnp.concatenate([low, block, high], axis=dim)
    return block


def banded(kernel, levels):
    lin = jnp.arange(levels, dtype=jnp.int32)
    taps = jnp.arange(3, dtype=jnp.int32)
    select = (lin[:, None, None] - lin[None, :, None] + 1 == taps[None, None, :]).astype(
        jnp.float32
    )
    full = jnp.einsum("pqt,abtcg->abpcqg", select, kernel.astype(jnp.float32))
    cin = kernel.shape[3]
    cout = kernel.shape[4]
    return full.reshape(9, levels * cin, levels * cout).astype(jnp.bfloat16)


def gelu_slope(value):
    inner = 0.7978845608 * (value + 0.044715 * value**3)
    tval = jnp.tanh(inner)
    return 0.5 * (1.0 + tval) + 0.5 * value * (1.0 - tval * tval) * 0.7978845608 * (
        1.0 + 0.134145 * value * value
    )


def extend(field):
    wide = with_halo(field, (("lon", 1),), 1, True)
    return with_halo(wide, (("lat", 0),), 1, False)


def conv_valid(padded, matrices, rows, cols):
    total = jnp.zeros((rows, cols, matrices.shape[2]), jnp.float32)
    for row_off in range(3):
        for col_off in range(3):
            piece = padded[row_off : row_off + rows, col_off : col_off + cols]
            total = total + jnp.einsum(
                "ijf,fg->ijg",
                piece,
                matrices[row_off * 3 + col_off],
                preferred_element_type=jnp.float32,
            )
    return total


def adjoint_valid(padded, matrices, rows, cols):
    total = jnp.zeros((rows, cols, matrices.shape[1]), jnp.float32)
    for row_off in range(3):
        for col_off in range(3):
            piece = padded[2 - row_off : 2 - row_off + rows, 2 - col_off : 2 - col_off + cols]
            total = total + jnp.einsum(
                "ijg,fg->ijf",
                piece,
                matrices[row_off * 3 + col_off],
                preferred_element_type=jnp.float32,
            )
    return total


def convolve(field, matrices):
    return conv_valid(extend(field), matrices, field.shape[0], field.shape[1])


def convolve_adjoint(grads, matrices):
    return adjoint_valid(extend(grads), matrices, grads.shape[0], grads.shape[1])


def widen(coarse):
    rows, cols, feats = coarse.shape
    return jnp.broadcast_to(coarse[:, None, :, None, :], (rows, 2, cols, 2, feats)).reshape(
        rows * 2, cols * 2, feats
    )


def block_sum(fine):
    rows, cols, feats = fine.shape
    return fine.reshape(rows // 2, 2, cols // 2, 2, feats).sum(axis=(1, 3))


def split_bf16(value):
    high = value.astype(jnp.bfloat16)
    low = (value - high.astype(jnp.float32)).astype(jnp.bfloat16)
    return high, low


def observe(output, obs_cells, obs_chan, obs_weights, obs_value, obs_count):
    rows, cols, feats = output.shape
    ncell = rows * cols
    slots = lax.broadcasted_iota(jnp.int32, obs_chan.shape, 2)
    live = (slots < obs_count[:, :, None]).astype(jnp.float32)
    weights = obs_weights * live[..., None]
    values = obs_value * live
    packed = jnp.concatenate(
        [
            obs_cells.astype(jnp.float32),
            obs_chan[..., None].astype(jnp.float32),
            weights,
            values[..., None],
        ],
        axis=-1,
    )
    got = lax.all_to_all(packed, "lon", split_axis=1, concat_axis=1, tiled=True)
    got = got.reshape(-1, packed.shape[-1])
    cells = got[:, 0:4].astype(jnp.int32)
    chan = got[:, 4:5].astype(jnp.int32)
    wts = got[:, 5:9]
    vals = got[:, 9]
    count = got.shape[0]
    cell_ids = lax.broadcasted_iota(jnp.int32, (count, ncell), 1)
    table = jnp.zeros((count, ncell), jnp.float32)
    for j in range(4):
        table = table + jnp.where(cell_ids == cells[:, j : j + 1], wts[:, j : j + 1], 0.0)
    t_hi, t_lo = split_bf16(table)
    o_hi, o_lo = split_bf16(output.reshape(ncell, feats))
    both = jnp.dot(t_hi, jnp.concatenate([o_hi, o_lo], axis=1), preferred_element_type=jnp.float32)
    picked = both[:, :feats] + both[:, feats:] + jnp.dot(
        t_lo, o_hi, preferred_element_type=jnp.float32
    )
    pick = lax.broadcasted_iota(jnp.int32, (count, feats), 1) == chan
    innov = jnp.sum(jnp.where(pick, picked, 0.0), axis=1) - vals
    spread = jnp.where(pick, innov[:, None], 0.0)
    s_hi, s_lo = split_bf16(spread)
    dims = (((0,), (0,)), ((), ()))
    back = lax.dot_general(
        t_hi, jnp.concatenate([s_hi, s_lo], axis=1), dims, preferred_element_type=jnp.float32
    )
    grad = back[:, :feats] + back[:, feats:] + lax.dot_general(
        t_lo, s_hi, dims, preferred_element_type=jnp.float32
    )
    innovation = lax.all_to_all(
        innov.reshape(obs_value.shape), "lon", split_axis=1, concat_axis=1, tiled=True
    )
    return grad.reshape(rows, cols, feats), innovation


def shards(
    state,
    kernel_in,
    kernel_mid,
    kernel_out,
    lift,
    obs_cells,
    obs_chan,
    obs_weights,
    obs_value,
    obs_count,
):
    feats = LEV * C
    rows, cols = (state.shape[0], state.shape[1])
    mat_in = banded(kernel_in, LEV)
    mat_mid = banded(kernel_mid, LEV)
    mat_out = banded(kernel_out, LEV)
    lift_full = (
        jnp.einsum("pq,cg->pcqg", jnp.eye(LEV, dtype=jnp.float32), lift.astype(jnp.float32))
        .reshape(LEV * C2, feats)
        .astype(jnp.bfloat16)
    )
    pre_first = convolve(state, mat_in)
    act_first = jax.nn.gelu(pre_first, approximate=True).astype(jnp.bfloat16)
    pooled = (block_sum(act_first.astype(jnp.float32)) * 0.25).astype(jnp.bfloat16)
    pre_mid = convolve(pooled, mat_mid)
    act_mid = jax.nn.gelu(pre_mid, approximate=True).astype(jnp.bfloat16)
    lifted = jnp.einsum("ijg,gf->ijf", act_mid, lift_full, preferred_element_type=jnp.float32)
    merged = (act_first.astype(jnp.float32) + widen(lifted)).astype(jnp.bfloat16)
    pre_last = convolve(merged, mat_out)
    slope_first = gelu_slope(pre_first)
    slope_mid = gelu_slope(pre_mid)
    output = state.astype(jnp.float32) + jax.nn.gelu(pre_last, approximate=True)
    grad_out, innovation = observe(
        output, obs_cells, obs_chan, obs_weights, obs_value, obs_count
    )
    grad_pre_last = (grad_out * gelu_slope(pre_last)).astype(jnp.bfloat16)
    grad_merged = convolve_adjoint(grad_pre_last, mat_out)
    grad_coarse = block_sum(grad_merged).astype(jnp.bfloat16)
    back_mid = jnp.einsum("ijf,gf->ijg", grad_coarse, lift_full, preferred_element_type=jnp.float32)
    grad_mid = (back_mid * slope_mid).astype(jnp.bfloat16)
    grad_pooled = convolve_adjoint(grad_mid, mat_mid)
    grad_first = ((grad_merged + widen(grad_pooled) * 0.25) * slope_first).astype(jnp.bfloat16)
    gradient = grad_out + convolve_adjoint(grad_first, mat_in)
    return (gradient, innovation)


def solution(mesh):
    placed = (
        P("lat", "lon", None),
        P(),
        P(),
        P(),
        P(),
        P("lat", "lon", None, None),
        P("lat", "lon", None),
        P("lat", "lon", None, None),
        P("lat", "lon", None),
        P("lat", "lon"),
    )
    return jax.shard_map(
        shards,
        mesh=mesh,
        in_specs=placed,
        out_specs=(P("lat", "lon", None), P("lat", "lon", None)),
        check_vma=False,
    )
```

```python
import jax
import jax.numpy as jnp
from jax import lax
from jax.sharding import PartitionSpec as P

C = 32
C2 = 64
LEV = 4


def with_halo(block, sides, width, periodic):
    for axis, dim in sides:
        count = lax.axis_size(axis)
        forward = [(i, i + 1) for i in range(count - 1)]
        if periodic:
            forward.append((count - 1, 0))
        backward = [(target, source) for source, target in forward]
        low = lax.ppermute(
            lax.slice_in_dim(block, block.shape[dim] - width, None, axis=dim), axis, forward
        )
        high = lax.ppermute(lax.slice_in_dim(block, 0, width, axis=dim), axis, backward)
        block = jnp.concatenate([low, block, high], axis=dim)
    return block


def banded(kernel, levels):
    zero = jnp.zeros(kernel.shape[:2] + kernel.shape[3:], kernel.dtype)
    rows = []
    for p in range(levels):
        blocks = [kernel[:, :, p - q + 1] if 0 <= p - q + 1 < 3 else zero for q in range(levels)]
        rows.append(jnp.concatenate(blocks, axis=-1))
    full = jnp.concatenate(rows, axis=-2)
    return full.reshape(9, full.shape[2], full.shape[3])


def block_diagonal(matrix, levels):
    zero = jnp.zeros_like(matrix)
    rows = [
        jnp.concatenate([matrix if p == q else zero for q in range(levels)], axis=1)
        for p in range(levels)
    ]
    return jnp.concatenate(rows, axis=0)


def gelu_slope(value):
    inner = 0.7978845608 * (value + 0.044715 * value**3)
    tval = jnp.tanh(inner)
    return 0.5 * (1.0 + tval) + 0.5 * value * (1.0 - tval * tval) * 0.7978845608 * (
        1.0 + 0.134145 * value * value
    )


def extend(field):
    wide = with_halo(field, (("lon", 1),), 1, True)
    return with_halo(wide, (("lat", 0),), 1, False)


def conv_valid(padded, matrices, rows, cols):
    total = jnp.zeros((rows, cols, matrices.shape[2]), jnp.float32)
    for row_off in range(3):
        for col_off in range(3):
            piece = padded[row_off : row_off + rows, col_off : col_off + cols]
            total = total + jnp.einsum(
                "ijf,fg->ijg",
                piece,
                matrices[row_off * 3 + col_off],
                preferred_element_type=jnp.float32,
            )
    return total


def adjoint_valid(padded, matrices, rows, cols):
    total = jnp.zeros((rows, cols, matrices.shape[1]), jnp.float32)
    for row_off in range(3):
        for col_off in range(3):
            piece = padded[2 - row_off : 2 - row_off + rows, 2 - col_off : 2 - col_off + cols]
            total = total + jnp.einsum(
                "ijg,fg->ijf",
                piece,
                matrices[row_off * 3 + col_off],
                preferred_element_type=jnp.float32,
            )
    return total


def convolve(field, matrices):
    return conv_valid(extend(field), matrices, field.shape[0], field.shape[1])


def convolve_adjoint(grads, matrices):
    return adjoint_valid(extend(grads), matrices, grads.shape[0], grads.shape[1])


def widen(coarse):
    rows, cols, feats = coarse.shape
    return jnp.broadcast_to(coarse[:, None, :, None, :], (rows, 2, cols, 2, feats)).reshape(
        rows * 2, cols * 2, feats
    )


def block_sum(fine):
    rows, cols, feats = fine.shape
    return fine.reshape(rows // 2, 2, cols // 2, 2, feats).sum(axis=(1, 3))


def split_bf16(value):
    high = lax.reduce_precision(value, exponent_bits=8, mantissa_bits=7)
    return high.astype(jnp.bfloat16), (value - high).astype(jnp.bfloat16)


def observe(output, obs_cells, obs_chan, obs_weights, obs_value, obs_count):
    rows, cols, feats = output.shape
    ncell = rows * cols
    slots = lax.broadcasted_iota(jnp.int32, obs_chan.shape, 2)
    live = (slots < obs_count[:, :, None]).astype(jnp.float32)
    weights = obs_weights * live[..., None]
    values = obs_value * live
    packed = jnp.concatenate(
        [
            obs_cells.astype(jnp.float32),
            obs_chan[..., None].astype(jnp.float32),
            weights,
            values[..., None],
        ],
        axis=-1,
    )
    got = lax.all_to_all(packed, "lon", split_axis=1, concat_axis=1, tiled=True)
    got = got.reshape(-1, packed.shape[-1])
    cells = got[:, 0:4].astype(jnp.int32)
    chan = got[:, 4:5].astype(jnp.int32)
    wts = got[:, 5:9]
    vals = got[:, 9]
    count = got.shape[0]
    cell_ids = lax.broadcasted_iota(jnp.int32, (count, ncell), 1)
    table = jnp.zeros((count, ncell), jnp.float32)
    for j in range(4):
        table = table + jnp.where(cell_ids == cells[:, j : j + 1], wts[:, j : j + 1], 0.0)
    t_hi, t_lo = split_bf16(table)
    o_hi, o_lo = split_bf16(output.reshape(ncell, feats))
    both = jnp.dot(t_hi, jnp.concatenate([o_hi, o_lo], axis=1), preferred_element_type=jnp.float32)
    picked = both[:, :feats] + both[:, feats:] + jnp.dot(
        t_lo, o_hi, preferred_element_type=jnp.float32
    )
    pick = lax.broadcasted_iota(jnp.int32, (count, feats), 1) == chan
    innov = jnp.sum(jnp.where(pick, picked, 0.0), axis=1) - vals
    spread = jnp.where(pick, innov[:, None], 0.0)
    s_hi, s_lo = split_bf16(spread)
    dims = (((0,), (0,)), ((), ()))
    back = lax.dot_general(
        t_hi, jnp.concatenate([s_hi, s_lo], axis=1), dims, preferred_element_type=jnp.float32
    )
    grad = back[:, :feats] + back[:, feats:] + lax.dot_general(
        t_lo, s_hi, dims, preferred_element_type=jnp.float32
    )
    innovation = lax.all_to_all(
        innov.reshape(obs_value.shape), "lon", split_axis=1, concat_axis=1, tiled=True
    )
    return grad.reshape(rows, cols, feats), innovation


def exchange(block, width):
    wide = with_halo(block, (("lon", 1),), width, True)
    return with_halo(wide, (("lat", 0),), width, False)


def inside(field, tile_rows, halo):
    rows = field.shape[0]
    first = lax.axis_index("lat") * tile_rows - halo
    where = first + lax.broadcasted_iota(jnp.int32, (rows, 1, 1), 0)
    keep = (where >= 0) & (where < lax.axis_size("lat") * tile_rows)
    return jnp.where(keep, field, jnp.zeros_like(field))


def trim(field, width):
    return field[width : field.shape[0] - width, width : field.shape[1] - width]


def shards(
    state,
    kernel_in,
    kernel_mid,
    kernel_out,
    lift,
    obs_cells,
    obs_chan,
    obs_weights,
    obs_value,
    obs_count,
):
    rows, cols = (state.shape[0], state.shape[1])
    crows = rows // 2
    mat_in = banded(kernel_in, LEV)
    mat_mid = banded(kernel_mid, LEV)
    mat_out = banded(kernel_out, LEV)
    lift_full = block_diagonal(lift, LEV)
    padded = exchange(state, 7)
    pre_first = conv_valid(padded, mat_in, rows + 12, cols + 12)
    act_first = jax.nn.gelu(pre_first, approximate=True).astype(jnp.bfloat16)
    pooled = (block_sum(act_first.astype(jnp.float32)) * 0.25).astype(jnp.bfloat16)
    pooled = inside(pooled, crows, 3)
    pre_mid = conv_valid(pooled, mat_mid, crows + 4, cols // 2 + 4)
    act_mid = jax.nn.gelu(trim(pre_mid, 1), approximate=True).astype(jnp.bfloat16)
    lifted = jnp.einsum("ijg,gf->ijf", act_mid, lift_full, preferred_element_type=jnp.float32)
    merged = (trim(act_first, 5).astype(jnp.float32) + trim(widen(lifted), 1)).astype(jnp.bfloat16)
    merged = inside(merged, rows, 1)
    pre_last = conv_valid(merged, mat_out, rows, cols)
    slope_first = gelu_slope(trim(pre_first, 5))
    slope_mid = gelu_slope(pre_mid)
    output = state.astype(jnp.float32) + jax.nn.gelu(pre_last, approximate=True)
    grad_out, innovation = observe(
        output, obs_cells, obs_chan, obs_weights, obs_value, obs_count
    )
    grad_pre_last = (grad_out * gelu_slope(pre_last)).astype(jnp.bfloat16)
    grads = exchange(grad_pre_last, 5)
    grad_merged = adjoint_valid(grads, mat_out, rows + 8, cols + 8)
    grad_coarse = block_sum(grad_merged).astype(jnp.bfloat16)
    back_mid = jnp.einsum("ijf,gf->ijg", grad_coarse, lift_full, preferred_element_type=jnp.float32)
    grad_mid = inside((back_mid * slope_mid).astype(jnp.bfloat16), crows, 2)
    grad_pooled = adjoint_valid(grad_mid, mat_mid, crows + 2, cols // 2 + 2)
    grad_first = (
        (trim(grad_merged, 3) + trim(widen(grad_pooled), 1) * 0.25) * slope_first
    ).astype(jnp.bfloat16)
    grad_first = inside(grad_first, rows, 1)
    gradient = grad_out + adjoint_valid(grad_first, mat_in, rows, cols)
    return (gradient, innovation)


def solution(mesh):
    placed = (
        P("lat", "lon", None),
        P(),
        P(),
        P(),
        P(),
        P("lat", "lon", None, None),
        P("lat", "lon", None),
        P("lat", "lon", None, None),
        P("lat", "lon", None),
        P("lat", "lon"),
    )
    return jax.shard_map(
        shards,
        mesh=mesh,
        in_specs=placed,
        out_specs=(P("lat", "lon", None), P("lat", "lon", None)),
        check_vma=False,
    )
```

```python
import jax
import jax.numpy as jnp
from jax import lax
from jax.sharding import PartitionSpec as P

C = 32
C2 = 64
LEV = 4


def with_halo(block, sides, width, periodic):
    for axis, dim in sides:
        count = lax.axis_size(axis)
        forward = [(i, i + 1) for i in range(count - 1)]
        if periodic:
            forward.append((count - 1, 0))
        backward = [(target, source) for source, target in forward]
        low = lax.ppermute(
            lax.slice_in_dim(block, block.shape[dim] - width, None, axis=dim), axis, forward
        )
        high = lax.ppermute(lax.slice_in_dim(block, 0, width, axis=dim), axis, backward)
        block = jnp.concatenate([low, block, high], axis=dim)
    return block


def banded(kernel, levels):
    zero = jnp.zeros(kernel.shape[:2] + kernel.shape[3:], kernel.dtype)
    rows = []
    for p in range(levels):
        blocks = [kernel[:, :, p - q + 1] if 0 <= p - q + 1 < 3 else zero for q in range(levels)]
        rows.append(jnp.concatenate(blocks, axis=-1))
    full = jnp.concatenate(rows, axis=-2)
    return full.reshape(9, full.shape[2], full.shape[3])


def block_diagonal(matrix, levels):
    zero = jnp.zeros_like(matrix)
    rows = [
        jnp.concatenate([matrix if p == q else zero for q in range(levels)], axis=1)
        for p in range(levels)
    ]
    return jnp.concatenate(rows, axis=0)


def gelu_slope(value):
    inner = 0.7978845608 * (value + 0.044715 * value**3)
    tval = jnp.tanh(inner)
    return 0.5 * (1.0 + tval) + 0.5 * value * (1.0 - tval * tval) * 0.7978845608 * (
        1.0 + 0.134145 * value * value
    )


def extend(field):
    wide = with_halo(field, (("lon", 1),), 1, True)
    return with_halo(wide, (("lat", 0),), 1, False)


def conv_valid(padded, matrices, rows, cols):
    total = jnp.zeros((rows, cols, matrices.shape[2]), jnp.float32)
    for row_off in range(3):
        for col_off in range(3):
            piece = padded[row_off : row_off + rows, col_off : col_off + cols]
            total = total + jnp.einsum(
                "ijf,fg->ijg",
                piece,
                matrices[row_off * 3 + col_off],
                preferred_element_type=jnp.float32,
            )
    return total


def adjoint_valid(padded, matrices, rows, cols):
    total = jnp.zeros((rows, cols, matrices.shape[1]), jnp.float32)
    for row_off in range(3):
        for col_off in range(3):
            piece = padded[2 - row_off : 2 - row_off + rows, 2 - col_off : 2 - col_off + cols]
            total = total + jnp.einsum(
                "ijg,fg->ijf",
                piece,
                matrices[row_off * 3 + col_off],
                preferred_element_type=jnp.float32,
            )
    return total


def convolve(field, matrices):
    return conv_valid(extend(field), matrices, field.shape[0], field.shape[1])


def convolve_adjoint(grads, matrices):
    return adjoint_valid(extend(grads), matrices, grads.shape[0], grads.shape[1])


def widen(coarse):
    rows, cols, feats = coarse.shape
    return jnp.broadcast_to(coarse[:, None, :, None, :], (rows, 2, cols, 2, feats)).reshape(
        rows * 2, cols * 2, feats
    )


def block_sum(fine):
    rows, cols, feats = fine.shape
    return fine.reshape(rows // 2, 2, cols // 2, 2, feats).sum(axis=(1, 3))


def split_bf16(value):
    high = lax.reduce_precision(value, exponent_bits=8, mantissa_bits=7)
    return high.astype(jnp.bfloat16), (value - high).astype(jnp.bfloat16)


def observe(output, obs_cells, obs_chan, obs_weights, obs_value, obs_count):
    rows, cols, feats = output.shape
    ncell = rows * cols
    slots = lax.broadcasted_iota(jnp.int32, obs_chan.shape, 2)
    live = (slots < obs_count[:, :, None]).astype(jnp.float32)
    weights = obs_weights * live[..., None]
    values = obs_value * live
    packed = jnp.concatenate(
        [
            obs_cells.astype(jnp.float32),
            obs_chan[..., None].astype(jnp.float32),
            weights,
            values[..., None],
        ],
        axis=-1,
    )
    got = lax.all_to_all(packed, "lon", split_axis=1, concat_axis=1, tiled=True)
    got = got.reshape(-1, packed.shape[-1])
    cells = got[:, 0:4].astype(jnp.int32)
    chan = got[:, 4:5].astype(jnp.int32)
    wts = got[:, 5:9]
    vals = got[:, 9]
    count = got.shape[0]
    cell_ids = lax.broadcasted_iota(jnp.int32, (count, ncell), 1)
    table = jnp.zeros((count, ncell), jnp.float32)
    for j in range(4):
        table = table + jnp.where(cell_ids == cells[:, j : j + 1], wts[:, j : j + 1], 0.0)
    t_hi, t_lo = split_bf16(table)
    o_hi, o_lo = split_bf16(output.reshape(ncell, feats))
    both = jnp.dot(t_hi, jnp.concatenate([o_hi, o_lo], axis=1), preferred_element_type=jnp.float32)
    picked = both[:, :feats] + both[:, feats:] + jnp.dot(
        t_lo, o_hi, preferred_element_type=jnp.float32
    )
    pick = lax.broadcasted_iota(jnp.int32, (count, feats), 1) == chan
    innov = jnp.sum(jnp.where(pick, picked, 0.0), axis=1) - vals
    spread = jnp.where(pick, innov[:, None], 0.0)
    s_hi, s_lo = split_bf16(spread)
    dims = (((0,), (0,)), ((), ()))
    back = lax.dot_general(
        t_hi, jnp.concatenate([s_hi, s_lo], axis=1), dims, preferred_element_type=jnp.float32
    )
    grad = back[:, :feats] + back[:, feats:] + lax.dot_general(
        t_lo, s_hi, dims, preferred_element_type=jnp.float32
    )
    innovation = lax.all_to_all(
        innov.reshape(obs_value.shape), "lon", split_axis=1, concat_axis=1, tiled=True
    )
    return grad.reshape(rows, cols, feats), innovation


def exchange(block, width):
    nlat = lax.axis_size("lat")
    nlon = lax.axis_size("lon")
    rows, cols = block.shape[0], block.shape[1]
    row_part = {-1: slice(rows - width, rows), 0: slice(0, rows), 1: slice(0, width)}
    col_part = {-1: slice(cols - width, cols), 0: slice(0, cols), 1: slice(0, width)}
    got = {}
    for a in (-1, 0, 1):
        for b in (-1, 0, 1):
            if a == 0 and b == 0:
                got[a, b] = block
                continue
            pairs = [
                (i * nlon + j, (i - a) * nlon + (j - b) % nlon)
                for i in range(nlat)
                for j in range(nlon)
                if 0 <= i - a < nlat
            ]
            got[a, b] = lax.ppermute(block[row_part[a], col_part[b]], ("lat", "lon"), pairs)
    bands = [jnp.concatenate([got[a, b] for b in (-1, 0, 1)], axis=1) for a in (-1, 0, 1)]
    return jnp.concatenate(bands, axis=0)


def inside(field, tile_rows, halo):
    rows = field.shape[0]
    first = lax.axis_index("lat") * tile_rows - halo
    where = first + lax.broadcasted_iota(jnp.int32, (rows, 1, 1), 0)
    keep = (where >= 0) & (where < lax.axis_size("lat") * tile_rows)
    return jnp.where(keep, field, jnp.zeros_like(field))


def trim(field, width):
    return field[width : field.shape[0] - width, width : field.shape[1] - width]


def shards(
    state,
    kernel_in,
    kernel_mid,
    kernel_out,
    lift,
    obs_cells,
    obs_chan,
    obs_weights,
    obs_value,
    obs_count,
):
    rows, cols = (state.shape[0], state.shape[1])
    crows = rows // 2
    mat_in = banded(kernel_in, LEV)
    mat_mid = banded(kernel_mid, LEV)
    mat_out = banded(kernel_out, LEV)
    lift_full = block_diagonal(lift, LEV)
    padded = exchange(state, 7)
    pre_first = conv_valid(padded, mat_in, rows + 12, cols + 12)
    act_first = jax.nn.gelu(pre_first, approximate=True).astype(jnp.bfloat16)
    pooled = (block_sum(act_first.astype(jnp.float32)) * 0.25).astype(jnp.bfloat16)
    pooled = inside(pooled, crows, 3)
    pre_mid = conv_valid(pooled, mat_mid, crows + 4, cols // 2 + 4)
    act_mid = jax.nn.gelu(trim(pre_mid, 1), approximate=True).astype(jnp.bfloat16)
    lifted = jnp.einsum("ijg,gf->ijf", act_mid, lift_full, preferred_element_type=jnp.float32)
    merged = (trim(act_first, 5).astype(jnp.float32) + trim(widen(lifted), 1)).astype(jnp.bfloat16)
    merged = inside(merged, rows, 1)
    pre_last = conv_valid(merged, mat_out, rows, cols)
    slope_first = gelu_slope(trim(pre_first, 5))
    slope_mid = gelu_slope(pre_mid)
    output = state.astype(jnp.float32) + jax.nn.gelu(pre_last, approximate=True)
    grad_out, innovation = observe(
        output, obs_cells, obs_chan, obs_weights, obs_value, obs_count
    )
    grad_pre_last = (grad_out * gelu_slope(pre_last)).astype(jnp.bfloat16)
    grads = exchange(grad_pre_last, 5)
    grad_merged = adjoint_valid(grads, mat_out, rows + 8, cols + 8)
    grad_coarse = block_sum(grad_merged).astype(jnp.bfloat16)
    back_mid = jnp.einsum("ijf,gf->ijg", grad_coarse, lift_full, preferred_element_type=jnp.float32)
    grad_mid = inside((back_mid * slope_mid).astype(jnp.bfloat16), crows, 2)
    grad_pooled = adjoint_valid(grad_mid, mat_mid, crows + 2, cols // 2 + 2)
    grad_first = (
        (trim(grad_merged, 3) + trim(widen(grad_pooled), 1) * 0.25) * slope_first
    ).astype(jnp.bfloat16)
    grad_first = inside(grad_first, rows, 1)
    gradient = grad_out + adjoint_valid(grad_first, mat_in, rows, cols)
    return (gradient, innovation)


def solution(mesh):
    placed = (
        P("lat", "lon", None),
        P(),
        P(),
        P(),
        P(),
        P("lat", "lon", None, None),
        P("lat", "lon", None),
        P("lat", "lon", None, None),
        P("lat", "lon", None),
        P("lat", "lon"),
    )
    return jax.shard_map(
        shards,
        mesh=mesh,
        in_specs=placed,
        out_specs=(P("lat", "lon", None), P("lat", "lon", None)),
        check_vma=False,
    )
```

```python
import jax
import jax.numpy as jnp
from jax import lax
from jax.experimental import pallas as pl
from jax.sharding import PartitionSpec as P

C = 32
C2 = 64
LEV = 4


def with_halo(block, sides, width, periodic):
    for axis, dim in sides:
        count = lax.axis_size(axis)
        forward = [(i, i + 1) for i in range(count - 1)]
        if periodic:
            forward.append((count - 1, 0))
        backward = [(target, source) for source, target in forward]
        low = lax.ppermute(
            lax.slice_in_dim(block, block.shape[dim] - width, None, axis=dim), axis, forward
        )
        high = lax.ppermute(lax.slice_in_dim(block, 0, width, axis=dim), axis, backward)
        block = jnp.concatenate([low, block, high], axis=dim)
    return block


def banded(kernel, levels):
    zero = jnp.zeros(kernel.shape[:2] + kernel.shape[3:], kernel.dtype)
    rows = []
    for p in range(levels):
        blocks = [kernel[:, :, p - q + 1] if 0 <= p - q + 1 < 3 else zero for q in range(levels)]
        rows.append(jnp.concatenate(blocks, axis=-1))
    full = jnp.concatenate(rows, axis=-2)
    return full.reshape(9, full.shape[2], full.shape[3])


def block_diagonal(matrix, levels):
    zero = jnp.zeros_like(matrix)
    rows = [
        jnp.concatenate([matrix if p == q else zero for q in range(levels)], axis=1)
        for p in range(levels)
    ]
    return jnp.concatenate(rows, axis=0)


def gelu_slope(value):
    inner = 0.7978845608 * (value + 0.044715 * value**3)
    tval = jnp.tanh(inner)
    return 0.5 * (1.0 + tval) + 0.5 * value * (1.0 - tval * tval) * 0.7978845608 * (
        1.0 + 0.134145 * value * value
    )


def extend(field):
    wide = with_halo(field, (("lon", 1),), 1, True)
    return with_halo(wide, (("lat", 0),), 1, False)


def conv_valid(padded, matrices, rows, cols):
    total = jnp.zeros((rows, cols, matrices.shape[2]), jnp.float32)
    for row_off in range(3):
        for col_off in range(3):
            piece = padded[row_off : row_off + rows, col_off : col_off + cols]
            total = total + jnp.einsum(
                "ijf,fg->ijg",
                piece,
                matrices[row_off * 3 + col_off],
                preferred_element_type=jnp.float32,
            )
    return total


def adjoint_valid(padded, matrices, rows, cols):
    total = jnp.zeros((rows, cols, matrices.shape[1]), jnp.float32)
    for row_off in range(3):
        for col_off in range(3):
            piece = padded[2 - row_off : 2 - row_off + rows, 2 - col_off : 2 - col_off + cols]
            total = total + jnp.einsum(
                "ijg,fg->ijf",
                piece,
                matrices[row_off * 3 + col_off],
                preferred_element_type=jnp.float32,
            )
    return total


def convolve(field, matrices):
    return conv_valid(extend(field), matrices, field.shape[0], field.shape[1])


def convolve_adjoint(grads, matrices):
    return adjoint_valid(extend(grads), matrices, grads.shape[0], grads.shape[1])


def widen(coarse):
    rows, cols, feats = coarse.shape
    return jnp.broadcast_to(coarse[:, None, :, None, :], (rows, 2, cols, 2, feats)).reshape(
        rows * 2, cols * 2, feats
    )


def block_sum(fine):
    rows, cols, feats = fine.shape
    return fine.reshape(rows // 2, 2, cols // 2, 2, feats).sum(axis=(1, 3))


def split_bf16(value):
    high = lax.reduce_precision(value, exponent_bits=8, mantissa_bits=7)
    return high.astype(jnp.bfloat16), (value - high).astype(jnp.bfloat16)


def observe_kernel(got_ref, high_ref, low_ref, innov_ref, grad_ref):
    fields, nslot = got_ref.shape[1], got_ref.shape[2]
    feats, ncell = high_ref.shape
    cell_ids = lax.broadcasted_iota(jnp.int32, (ncell, nslot), 0).astype(jnp.float32)
    feat_ids = lax.broadcasted_iota(jnp.int32, (feats, nslot), 0).astype(jnp.float32)
    high = high_ref[...]
    low = low_ref[...]
    both = jnp.concatenate([high, low], axis=0)
    grad_ref[...] = jnp.zeros(grad_ref.shape, jnp.float32)
    trans = (((1,), (1,)), ((), ()))

    def body(owner, carry):
        block = got_ref[owner]
        table = jnp.zeros((ncell, nslot), jnp.float32)
        for j in range(4):
            table = table + jnp.where(
                cell_ids == block[j : j + 1, :], block[5 + j : 6 + j, :], 0.0
            )
        t_hi = table.astype(jnp.bfloat16)
        t_lo = (table - t_hi.astype(jnp.float32)).astype(jnp.bfloat16)
        two = jnp.dot(both, t_hi, preferred_element_type=jnp.float32)
        picked = two[:feats] + two[feats:] + jnp.dot(high, t_lo, preferred_element_type=jnp.float32)
        pick = feat_ids == block[4:5, :]
        innov = jnp.sum(jnp.where(pick, picked, 0.0), axis=0, keepdims=True) - block[9:10, :]
        innov_ref[pl.ds(owner, 1), :] = innov
        spread = jnp.where(pick, innov, 0.0)
        s_hi = spread.astype(jnp.bfloat16)
        s_lo = (spread - s_hi.astype(jnp.float32)).astype(jnp.bfloat16)
        sums = lax.dot_general(
            t_hi, jnp.concatenate([s_hi, s_lo], axis=0), trans, preferred_element_type=jnp.float32
        )
        grad_ref[...] += (
            sums[:, :feats]
            + sums[:, feats:]
            + lax.dot_general(t_lo, s_hi, trans, preferred_element_type=jnp.float32)
        )
        return carry

    lax.fori_loop(0, got_ref.shape[0], body, 0)


def observe(output, obs_cells, obs_chan, obs_weights, obs_value, obs_count):
    rows, cols, feats = output.shape
    ncell = rows * cols
    slots = lax.broadcasted_iota(jnp.int32, obs_chan.shape, 2)
    live = (slots < obs_count[:, :, None]).astype(jnp.float32)
    weights = obs_weights * live[..., None]
    values = obs_value * live
    packed = jnp.concatenate(
        [
            jnp.swapaxes(obs_cells, 2, 3).astype(jnp.float32),
            obs_chan[:, :, None, :].astype(jnp.float32),
            jnp.swapaxes(weights, 2, 3),
            values[:, :, None, :],
        ],
        axis=2,
    )
    got = lax.all_to_all(packed, "lon", split_axis=1, concat_axis=1, tiled=True)
    got = got.reshape(got.shape[1:])
    owners, nslot = got.shape[0], got.shape[2]
    o_hi, o_lo = split_bf16(output.reshape(ncell, feats).T)
    innov, grad = pl.pallas_call(
        observe_kernel,
        out_shape=(
            jax.ShapeDtypeStruct((owners, nslot), jnp.float32),
            jax.ShapeDtypeStruct((ncell, feats), jnp.float32),
        ),
    )(got, o_hi, o_lo)
    innovation = lax.all_to_all(
        innov.reshape(obs_value.shape), "lon", split_axis=1, concat_axis=1, tiled=True
    )
    return grad.reshape(rows, cols, feats), innovation


def exchange(block, width):
    wide = with_halo(block, (("lon", 1),), width, True)
    return with_halo(wide, (("lat", 0),), width, False)


def inside(field, tile_rows, halo):
    rows = field.shape[0]
    first = lax.axis_index("lat") * tile_rows - halo
    where = first + lax.broadcasted_iota(jnp.int32, (rows, 1, 1), 0)
    keep = (where >= 0) & (where < lax.axis_size("lat") * tile_rows)
    return jnp.where(keep, field, jnp.zeros_like(field))


def trim(field, width):
    return field[width : field.shape[0] - width, width : field.shape[1] - width]


def shards(
    state,
    kernel_in,
    kernel_mid,
    kernel_out,
    lift,
    obs_cells,
    obs_chan,
    obs_weights,
    obs_value,
    obs_count,
):
    rows, cols = (state.shape[0], state.shape[1])
    crows = rows // 2
    mat_in = banded(kernel_in, LEV)
    mat_mid = banded(kernel_mid, LEV)
    mat_out = banded(kernel_out, LEV)
    lift_full = block_diagonal(lift, LEV)
    padded = exchange(state, 7)
    pre_first = conv_valid(padded, mat_in, rows + 12, cols + 12)
    act_first = jax.nn.gelu(pre_first, approximate=True).astype(jnp.bfloat16)
    pooled = (block_sum(act_first.astype(jnp.float32)) * 0.25).astype(jnp.bfloat16)
    pooled = inside(pooled, crows, 3)
    pre_mid = conv_valid(pooled, mat_mid, crows + 4, cols // 2 + 4)
    act_mid = jax.nn.gelu(trim(pre_mid, 1), approximate=True).astype(jnp.bfloat16)
    lifted = jnp.einsum("ijg,gf->ijf", act_mid, lift_full, preferred_element_type=jnp.float32)
    merged = (trim(act_first, 5).astype(jnp.float32) + trim(widen(lifted), 1)).astype(jnp.bfloat16)
    merged = inside(merged, rows, 1)
    pre_last = conv_valid(merged, mat_out, rows, cols)
    slope_first = gelu_slope(trim(pre_first, 5))
    slope_mid = gelu_slope(pre_mid)
    output = state.astype(jnp.float32) + jax.nn.gelu(pre_last, approximate=True)
    grad_out, innovation = observe(
        output, obs_cells, obs_chan, obs_weights, obs_value, obs_count
    )
    grad_pre_last = (grad_out * gelu_slope(pre_last)).astype(jnp.bfloat16)
    grads = exchange(grad_pre_last, 5)
    grad_merged = adjoint_valid(grads, mat_out, rows + 8, cols + 8)
    grad_coarse = block_sum(grad_merged).astype(jnp.bfloat16)
    back_mid = jnp.einsum("ijf,gf->ijg", grad_coarse, lift_full, preferred_element_type=jnp.float32)
    grad_mid = inside((back_mid * slope_mid).astype(jnp.bfloat16), crows, 2)
    grad_pooled = adjoint_valid(grad_mid, mat_mid, crows + 2, cols // 2 + 2)
    grad_first = (
        (trim(grad_merged, 3) + trim(widen(grad_pooled), 1) * 0.25) * slope_first
    ).astype(jnp.bfloat16)
    grad_first = inside(grad_first, rows, 1)
    gradient = grad_out + adjoint_valid(grad_first, mat_in, rows, cols)
    return (gradient, innovation)


def solution(mesh):
    placed = (
        P("lat", "lon", None),
        P(),
        P(),
        P(),
        P(),
        P("lat", "lon", None, None),
        P("lat", "lon", None),
        P("lat", "lon", None, None),
        P("lat", "lon", None),
        P("lat", "lon"),
    )
    return jax.shard_map(
        shards,
        mesh=mesh,
        in_specs=placed,
        out_specs=(P("lat", "lon", None), P("lat", "lon", None)),
        check_vma=False,
    )
```

```python
import jax
import jax.numpy as jnp
from jax import lax
import functools

from jax.experimental import pallas as pl
from jax.experimental.pallas import tpu as pltpu
from jax.sharding import PartitionSpec as P

C = 32
C2 = 64
LEV = 4


def with_halo(block, sides, width, periodic):
    for axis, dim in sides:
        count = lax.axis_size(axis)
        forward = [(i, i + 1) for i in range(count - 1)]
        if periodic:
            forward.append((count - 1, 0))
        backward = [(target, source) for source, target in forward]
        low = lax.ppermute(
            lax.slice_in_dim(block, block.shape[dim] - width, None, axis=dim), axis, forward
        )
        high = lax.ppermute(lax.slice_in_dim(block, 0, width, axis=dim), axis, backward)
        block = jnp.concatenate([low, block, high], axis=dim)
    return block


def banded(kernel, levels):
    zero = jnp.zeros(kernel.shape[:2] + kernel.shape[3:], kernel.dtype)
    rows = []
    for p in range(levels):
        blocks = [kernel[:, :, p - q + 1] if 0 <= p - q + 1 < 3 else zero for q in range(levels)]
        rows.append(jnp.concatenate(blocks, axis=-1))
    full = jnp.concatenate(rows, axis=-2)
    return full.reshape(9, full.shape[2], full.shape[3])


def block_diagonal(matrix, levels):
    zero = jnp.zeros_like(matrix)
    rows = [
        jnp.concatenate([matrix if p == q else zero for q in range(levels)], axis=1)
        for p in range(levels)
    ]
    return jnp.concatenate(rows, axis=0)


def gelu_slope(value):
    inner = 0.7978845608 * (value + 0.044715 * value**3)
    tval = jnp.tanh(inner)
    return 0.5 * (1.0 + tval) + 0.5 * value * (1.0 - tval * tval) * 0.7978845608 * (
        1.0 + 0.134145 * value * value
    )


def extend(field):
    wide = with_halo(field, (("lon", 1),), 1, True)
    return with_halo(wide, (("lat", 0),), 1, False)


def conv_valid(padded, matrices, rows, cols):
    total = jnp.zeros((rows, cols, matrices.shape[2]), jnp.float32)
    for row_off in range(3):
        for col_off in range(3):
            piece = padded[row_off : row_off + rows, col_off : col_off + cols]
            total = total + jnp.einsum(
                "ijf,fg->ijg",
                piece,
                matrices[row_off * 3 + col_off],
                preferred_element_type=jnp.float32,
            )
    return total


def adjoint_valid(padded, matrices, rows, cols):
    total = jnp.zeros((rows, cols, matrices.shape[1]), jnp.float32)
    for row_off in range(3):
        for col_off in range(3):
            piece = padded[2 - row_off : 2 - row_off + rows, 2 - col_off : 2 - col_off + cols]
            total = total + jnp.einsum(
                "ijg,fg->ijf",
                piece,
                matrices[row_off * 3 + col_off],
                preferred_element_type=jnp.float32,
            )
    return total


def convolve(field, matrices):
    return conv_valid(extend(field), matrices, field.shape[0], field.shape[1])


def convolve_adjoint(grads, matrices):
    return adjoint_valid(extend(grads), matrices, grads.shape[0], grads.shape[1])


def widen(coarse):
    rows, cols, feats = coarse.shape
    return jnp.broadcast_to(coarse[:, None, :, None, :], (rows, 2, cols, 2, feats)).reshape(
        rows * 2, cols * 2, feats
    )


def block_sum(fine):
    rows, cols, feats = fine.shape
    return fine.reshape(rows // 2, 2, cols // 2, 2, feats).sum(axis=(1, 3))


def split_bf16(value):
    high = lax.reduce_precision(value, exponent_bits=8, mantissa_bits=7)
    return high.astype(jnp.bfloat16), (value - high).astype(jnp.bfloat16)


def observe_kernel(got_ref, high_ref, low_ref, innov_ref, grad_ref):
    fields, nslot = got_ref.shape[1], got_ref.shape[2]
    feats, ncell = high_ref.shape
    cell_ids = lax.broadcasted_iota(jnp.int32, (ncell, nslot), 0).astype(jnp.float32)
    feat_ids = lax.broadcasted_iota(jnp.int32, (feats, nslot), 0).astype(jnp.float32)
    high = high_ref[...]
    low = low_ref[...]
    both = jnp.concatenate([high, low], axis=0)
    grad_ref[...] = jnp.zeros(grad_ref.shape, jnp.float32)
    trans = (((1,), (1,)), ((), ()))

    def body(owner, carry):
        block = got_ref[owner]
        table = jnp.zeros((ncell, nslot), jnp.float32)
        for j in range(4):
            table = table + jnp.where(
                cell_ids == block[j : j + 1, :], block[5 + j : 6 + j, :], 0.0
            )
        t_hi = table.astype(jnp.bfloat16)
        t_lo = (table - t_hi.astype(jnp.float32)).astype(jnp.bfloat16)
        two = jnp.dot(both, t_hi, preferred_element_type=jnp.float32)
        picked = two[:feats] + two[feats:] + jnp.dot(high, t_lo, preferred_element_type=jnp.float32)
        pick = feat_ids == block[4:5, :]
        innov = jnp.sum(jnp.where(pick, picked, 0.0), axis=0, keepdims=True) - block[9:10, :]
        innov_ref[pl.ds(owner, 1), :] = innov
        spread = jnp.where(pick, innov, 0.0)
        s_hi = spread.astype(jnp.bfloat16)
        s_lo = (spread - s_hi.astype(jnp.float32)).astype(jnp.bfloat16)
        sums = lax.dot_general(
            t_hi, jnp.concatenate([s_hi, s_lo], axis=0), trans, preferred_element_type=jnp.float32
        )
        grad_ref[...] += (
            sums[:, :feats]
            + sums[:, feats:]
            + lax.dot_general(t_lo, s_hi, trans, preferred_element_type=jnp.float32)
        )
        return carry

    lax.fori_loop(0, got_ref.shape[0], body, 0)


def observe(output, obs_cells, obs_chan, obs_weights, obs_value, obs_count):
    rows, cols, feats = output.shape
    ncell = rows * cols
    slots = lax.broadcasted_iota(jnp.int32, obs_chan.shape, 2)
    live = (slots < obs_count[:, :, None]).astype(jnp.float32)
    weights = obs_weights * live[..., None]
    values = obs_value * live
    packed = jnp.concatenate(
        [
            jnp.swapaxes(obs_cells, 2, 3).astype(jnp.float32),
            obs_chan[:, :, None, :].astype(jnp.float32),
            jnp.swapaxes(weights, 2, 3),
            values[:, :, None, :],
        ],
        axis=2,
    )
    got = lax.all_to_all(packed, "lon", split_axis=1, concat_axis=1, tiled=True)
    got = got.reshape(got.shape[1:])
    owners, nslot = got.shape[0], got.shape[2]
    o_hi, o_lo = split_bf16(output.reshape(ncell, feats).T)
    innov, grad = pl.pallas_call(
        observe_kernel,
        out_shape=(
            jax.ShapeDtypeStruct((owners, nslot), jnp.float32),
            jax.ShapeDtypeStruct((ncell, feats), jnp.float32),
        ),
    )(got, o_hi, o_lo)
    innovation = lax.all_to_all(
        innov.reshape(obs_value.shape), "lon", split_axis=1, concat_axis=1, tiled=True
    )
    return grad.reshape(rows, cols, feats), innovation


def halo_kernel(width, nlat, nlon, x_ref, o_ref, buf, send_sem, recv_sem):
    rows, cols = x_ref.shape[0], x_ref.shape[1]
    edge = (buf.shape[1] - cols) // 2
    i = lax.axis_index("lat")
    j = lax.axis_index("lon")
    has = {-1: i > 0, 0: i >= 0, 1: i < nlat - 1}
    dirs = [(a, b) for a in (-1, 0, 1) for b in (-1, 0, 1) if (a, b) != (0, 0)]
    buf[...] = jnp.zeros(buf.shape, buf.dtype)
    buf[width : width + rows, edge : edge + cols, :] = x_ref[...]
    barrier = pltpu.get_barrier_semaphore()
    for a, b in dirs:

        @pl.when(has[a])
        def _():
            pl.semaphore_signal(
                barrier,
                inc=1,
                device_id=((i + a) % nlat, (j + b) % nlon),
                device_id_type=pl.DeviceIdType.MESH,
            )

    count = 2 + 3 * has[-1].astype(jnp.int32) + 3 * has[1].astype(jnp.int32)
    pl.semaphore_wait(barrier, count)
    src_rows = {1: pl.ds(rows - width, width), -1: pl.ds(0, width), 0: pl.ds(0, rows)}
    dst_rows = {1: pl.ds(0, width), -1: pl.ds(width + rows, width), 0: pl.ds(width, rows)}
    src_cols = {1: pl.ds(cols - edge, edge), -1: pl.ds(0, edge), 0: pl.ds(0, cols)}
    dst_cols = {1: pl.ds(0, edge), -1: pl.ds(edge + cols, edge), 0: pl.ds(edge, cols)}
    copies = []
    for k, (a, b) in enumerate(dirs):
        copy = pltpu.make_async_remote_copy(
            src_ref=x_ref.at[src_rows[a], src_cols[b]],
            dst_ref=buf.at[dst_rows[a], dst_cols[b]],
            send_sem=send_sem.at[k],
            recv_sem=recv_sem.at[k],
            device_id=((i + a) % nlat, (j + b) % nlon),
            device_id_type=pl.DeviceIdType.MESH,
        )
        copies.append((a, copy))
        pl.when(has[a])(copy.start)
    for a, copy in copies:
        pl.when(has[a])(copy.wait_send)
        pl.when(has[-a])(copy.wait_recv)
    o_ref[...] = buf[...]


EXCHANGE_IDS = {7: 0, 5: 1}


def exchange(block, width):
    rows, cols, feats = block.shape
    edge = 16
    nlat = lax.axis_size("lat")
    nlon = lax.axis_size("lon")
    full = (rows + 2 * width, cols + 2 * edge, feats)
    out = pl.pallas_call(
        functools.partial(halo_kernel, width, nlat, nlon),
        out_shape=jax.ShapeDtypeStruct(full, block.dtype),
        in_specs=[pl.BlockSpec(memory_space=pltpu.VMEM)],
        out_specs=pl.BlockSpec(memory_space=pltpu.VMEM),
        scratch_shapes=[
            pltpu.VMEM(full, block.dtype),
            pltpu.SemaphoreType.DMA((8,)),
            pltpu.SemaphoreType.DMA((8,)),
        ],
        compiler_params=pltpu.CompilerParams(
            collective_id=EXCHANGE_IDS[width], has_side_effects=True
        ),
    )(block)
    return out[:, edge - width : edge + cols + width]


def inside(field, tile_rows, halo):
    rows = field.shape[0]
    first = lax.axis_index("lat") * tile_rows - halo
    where = first + lax.broadcasted_iota(jnp.int32, (rows, 1, 1), 0)
    keep = (where >= 0) & (where < lax.axis_size("lat") * tile_rows)
    return jnp.where(keep, field, jnp.zeros_like(field))


def trim(field, width):
    return field[width : field.shape[0] - width, width : field.shape[1] - width]


def shards(
    state,
    kernel_in,
    kernel_mid,
    kernel_out,
    lift,
    obs_cells,
    obs_chan,
    obs_weights,
    obs_value,
    obs_count,
):
    rows, cols = (state.shape[0], state.shape[1])
    crows = rows // 2
    mat_in = banded(kernel_in, LEV)
    mat_mid = banded(kernel_mid, LEV)
    mat_out = banded(kernel_out, LEV)
    lift_full = block_diagonal(lift, LEV)
    padded = exchange(state, 7)
    pre_first = conv_valid(padded, mat_in, rows + 12, cols + 12)
    act_first = jax.nn.gelu(pre_first, approximate=True).astype(jnp.bfloat16)
    pooled = (block_sum(act_first.astype(jnp.float32)) * 0.25).astype(jnp.bfloat16)
    pooled = inside(pooled, crows, 3)
    pre_mid = conv_valid(pooled, mat_mid, crows + 4, cols // 2 + 4)
    act_mid = jax.nn.gelu(trim(pre_mid, 1), approximate=True).astype(jnp.bfloat16)
    lifted = jnp.einsum("ijg,gf->ijf", act_mid, lift_full, preferred_element_type=jnp.float32)
    merged = (trim(act_first, 5).astype(jnp.float32) + trim(widen(lifted), 1)).astype(jnp.bfloat16)
    merged = inside(merged, rows, 1)
    pre_last = conv_valid(merged, mat_out, rows, cols)
    slope_first = gelu_slope(trim(pre_first, 5))
    slope_mid = gelu_slope(pre_mid)
    output = state.astype(jnp.float32) + jax.nn.gelu(pre_last, approximate=True)
    grad_out, innovation = observe(
        output, obs_cells, obs_chan, obs_weights, obs_value, obs_count
    )
    grad_pre_last = (grad_out * gelu_slope(pre_last)).astype(jnp.bfloat16)
    grads = exchange(grad_pre_last, 5)
    grad_merged = adjoint_valid(grads, mat_out, rows + 8, cols + 8)
    grad_coarse = block_sum(grad_merged).astype(jnp.bfloat16)
    back_mid = jnp.einsum("ijf,gf->ijg", grad_coarse, lift_full, preferred_element_type=jnp.float32)
    grad_mid = inside((back_mid * slope_mid).astype(jnp.bfloat16), crows, 2)
    grad_pooled = adjoint_valid(grad_mid, mat_mid, crows + 2, cols // 2 + 2)
    grad_first = (
        (trim(grad_merged, 3) + trim(widen(grad_pooled), 1) * 0.25) * slope_first
    ).astype(jnp.bfloat16)
    grad_first = inside(grad_first, rows, 1)
    gradient = grad_out + adjoint_valid(grad_first, mat_in, rows, cols)
    return (gradient, innovation)


def solution(mesh):
    placed = (
        P("lat", "lon", None),
        P(),
        P(),
        P(),
        P(),
        P("lat", "lon", None, None),
        P("lat", "lon", None),
        P("lat", "lon", None, None),
        P("lat", "lon", None),
        P("lat", "lon"),
    )
    return jax.shard_map(
        shards,
        mesh=mesh,
        in_specs=placed,
        out_specs=(P("lat", "lon", None), P("lat", "lon", None)),
        check_vma=False,
    )
```

```python
import jax
import jax.numpy as jnp
from jax import lax
import functools

from jax.experimental import pallas as pl
from jax.experimental.pallas import tpu as pltpu
from jax.sharding import PartitionSpec as P

C = 32
C2 = 64
LEV = 4


def with_halo(block, sides, width, periodic):
    for axis, dim in sides:
        count = lax.axis_size(axis)
        forward = [(i, i + 1) for i in range(count - 1)]
        if periodic:
            forward.append((count - 1, 0))
        backward = [(target, source) for source, target in forward]
        low = lax.ppermute(
            lax.slice_in_dim(block, block.shape[dim] - width, None, axis=dim), axis, forward
        )
        high = lax.ppermute(lax.slice_in_dim(block, 0, width, axis=dim), axis, backward)
        block = jnp.concatenate([low, block, high], axis=dim)
    return block


def banded(kernel, levels):
    zero = jnp.zeros(kernel.shape[:2] + kernel.shape[3:], kernel.dtype)
    rows = []
    for p in range(levels):
        blocks = [kernel[:, :, p - q + 1] if 0 <= p - q + 1 < 3 else zero for q in range(levels)]
        rows.append(jnp.concatenate(blocks, axis=-1))
    full = jnp.concatenate(rows, axis=-2)
    return full.reshape(9, full.shape[2], full.shape[3])


def block_diagonal(matrix, levels):
    zero = jnp.zeros_like(matrix)
    rows = [
        jnp.concatenate([matrix if p == q else zero for q in range(levels)], axis=1)
        for p in range(levels)
    ]
    return jnp.concatenate(rows, axis=0)


def gelu_slope(value):
    inner = 0.7978845608 * (value + 0.044715 * value**3)
    tval = jnp.tanh(inner)
    return 0.5 * (1.0 + tval) + 0.5 * value * (1.0 - tval * tval) * 0.7978845608 * (
        1.0 + 0.134145 * value * value
    )


def extend(field):
    wide = with_halo(field, (("lon", 1),), 1, True)
    return with_halo(wide, (("lat", 0),), 1, False)


def conv_valid(padded, matrices, rows, cols):
    total = jnp.zeros((rows, cols, matrices.shape[2]), jnp.float32)
    for row_off in range(3):
        for col_off in range(3):
            piece = padded[row_off : row_off + rows, col_off : col_off + cols]
            total = total + jnp.einsum(
                "ijf,fg->ijg",
                piece,
                matrices[row_off * 3 + col_off],
                preferred_element_type=jnp.float32,
            )
    return total


def adjoint_valid(padded, matrices, rows, cols):
    total = jnp.zeros((rows, cols, matrices.shape[1]), jnp.float32)
    for row_off in range(3):
        for col_off in range(3):
            piece = padded[2 - row_off : 2 - row_off + rows, 2 - col_off : 2 - col_off + cols]
            total = total + jnp.einsum(
                "ijg,fg->ijf",
                piece,
                matrices[row_off * 3 + col_off],
                preferred_element_type=jnp.float32,
            )
    return total


def convolve(field, matrices):
    return conv_valid(extend(field), matrices, field.shape[0], field.shape[1])


def convolve_adjoint(grads, matrices):
    return adjoint_valid(extend(grads), matrices, grads.shape[0], grads.shape[1])


def widen(coarse):
    rows, cols, feats = coarse.shape
    return jnp.broadcast_to(coarse[:, None, :, None, :], (rows, 2, cols, 2, feats)).reshape(
        rows * 2, cols * 2, feats
    )


def block_sum(fine):
    rows, cols, feats = fine.shape
    return fine.reshape(rows // 2, 2, cols // 2, 2, feats).sum(axis=(1, 3))


def split_bf16(value):
    high = lax.reduce_precision(value, exponent_bits=8, mantissa_bits=7)
    return high.astype(jnp.bfloat16), (value - high).astype(jnp.bfloat16)


def observe_kernel(got_ref, high_ref, low_ref, innov_ref, grad_ref):
    fields, nslot = got_ref.shape[1], got_ref.shape[2]
    feats, ncell = high_ref.shape
    cell_ids = lax.broadcasted_iota(jnp.int32, (ncell, nslot), 0).astype(jnp.float32)
    feat_ids = lax.broadcasted_iota(jnp.int32, (feats, nslot), 0).astype(jnp.float32)
    high = high_ref[...]
    low = low_ref[...]
    both = jnp.concatenate([high, low], axis=0)
    grad_ref[...] = jnp.zeros(grad_ref.shape, jnp.float32)
    trans = (((1,), (1,)), ((), ()))

    def body(owner, carry):
        block = got_ref[owner]
        table = jnp.zeros((ncell, nslot), jnp.float32)
        for j in range(4):
            table = table + jnp.where(
                cell_ids == block[j : j + 1, :], block[5 + j : 6 + j, :], 0.0
            )
        t_hi = table.astype(jnp.bfloat16)
        t_lo = (table - t_hi.astype(jnp.float32)).astype(jnp.bfloat16)
        two = jnp.dot(both, t_hi, preferred_element_type=jnp.float32)
        picked = two[:feats] + two[feats:] + jnp.dot(high, t_lo, preferred_element_type=jnp.float32)
        pick = feat_ids == block[4:5, :]
        innov = jnp.sum(jnp.where(pick, picked, 0.0), axis=0, keepdims=True) - block[9:10, :]
        innov_ref[pl.ds(owner, 1), :] = innov
        spread = jnp.where(pick, innov, 0.0)
        s_hi = spread.astype(jnp.bfloat16)
        s_lo = (spread - s_hi.astype(jnp.float32)).astype(jnp.bfloat16)
        sums = lax.dot_general(
            t_hi, jnp.concatenate([s_hi, s_lo], axis=0), trans, preferred_element_type=jnp.float32
        )
        grad_ref[...] += (
            sums[:, :feats]
            + sums[:, feats:]
            + lax.dot_general(t_lo, s_hi, trans, preferred_element_type=jnp.float32)
        )
        return carry

    lax.fori_loop(0, got_ref.shape[0], body, 0)


def pack(obs_cells, obs_chan, obs_weights, obs_value, obs_count):
    slots = lax.broadcasted_iota(jnp.int32, obs_chan.shape, 2)
    live = (slots < obs_count[:, :, None]).astype(jnp.float32)
    weights = obs_weights * live[..., None]
    values = obs_value * live
    packed = jnp.concatenate(
        [
            jnp.swapaxes(obs_cells, 2, 3).astype(jnp.float32),
            obs_chan[:, :, None, :].astype(jnp.float32),
            jnp.swapaxes(weights, 2, 3),
            values[:, :, None, :],
        ],
        axis=2,
    )
    return packed.reshape(packed.shape[1:])


def observe(output, got):
    rows, cols, feats = output.shape
    ncell = rows * cols
    owners, nslot = got.shape[0], got.shape[2]
    o_hi, o_lo = split_bf16(output.reshape(ncell, feats).T)
    innov, grad = pl.pallas_call(
        observe_kernel,
        out_shape=(
            jax.ShapeDtypeStruct((owners, nslot), jnp.float32),
            jax.ShapeDtypeStruct((ncell, feats), jnp.float32),
        ),
    )(got, o_hi, o_lo)
    return grad.reshape(rows, cols, feats), innov


def halo_kernel(
    width, nlat, nlon, x_ref, p_ref, o_ref, q_ref, buf, inbox, send_sem, recv_sem, p_send, p_recv
):
    rows, cols = x_ref.shape[0], x_ref.shape[1]
    edge = (buf.shape[1] - cols) // 2
    i = lax.axis_index("lat")
    j = lax.axis_index("lon")
    has = {-1: i > 0, 0: i >= 0, 1: i < nlat - 1}
    mesh = pl.DeviceIdType.MESH
    dirs = [(a, b) for a in (-1, 0, 1) for b in (-1, 0, 1) if (a, b) != (0, 0)]
    buf[...] = jnp.zeros(buf.shape, buf.dtype)
    buf[width : width + rows, edge : edge + cols, :] = x_ref[...]
    inbox[pl.ds(j, 1)] = p_ref[pl.ds(j, 1)]
    barrier = pltpu.get_barrier_semaphore()
    for a in (-1, 1):
        for b in (-1, 0, 1):

            @pl.when(has[a])
            def _():
                pl.semaphore_signal(
                    barrier, inc=1, device_id=((i + a) % nlat, (j + b) % nlon), device_id_type=mesh
                )

    for t in range(nlon):

        @pl.when(t != j)
        def _():
            pl.semaphore_signal(barrier, inc=1, device_id=(i, t), device_id_type=mesh)

    count = (nlon - 1) + 3 * has[-1].astype(jnp.int32) + 3 * has[1].astype(jnp.int32)
    pl.semaphore_wait(barrier, count)
    src_rows = {1: pl.ds(rows - width, width), -1: pl.ds(0, width), 0: pl.ds(0, rows)}
    dst_rows = {1: pl.ds(0, width), -1: pl.ds(width + rows, width), 0: pl.ds(width, rows)}
    src_cols = {1: pl.ds(cols - edge, edge), -1: pl.ds(0, edge), 0: pl.ds(0, cols)}
    dst_cols = {1: pl.ds(0, edge), -1: pl.ds(edge + cols, edge), 0: pl.ds(edge, cols)}
    copies = []
    for k, (a, b) in enumerate(dirs):
        copy = pltpu.make_async_remote_copy(
            src_ref=x_ref.at[src_rows[a], src_cols[b]],
            dst_ref=buf.at[dst_rows[a], dst_cols[b]],
            send_sem=send_sem.at[k],
            recv_sem=recv_sem.at[k],
            device_id=((i + a) % nlat, (j + b) % nlon),
            device_id_type=mesh,
        )
        copies.append((a, copy))
        pl.when(has[a])(copy.start)
    sends = []
    for t in range(nlon):
        copy = pltpu.make_async_remote_copy(
            src_ref=p_ref.at[pl.ds(t, 1)],
            dst_ref=inbox.at[pl.ds(j, 1)],
            send_sem=p_send.at[t],
            recv_sem=p_recv.at[j],
            device_id=(i, t),
            device_id_type=mesh,
        )
        sends.append(copy)
        pl.when(t != j)(copy.start)
    for a, copy in copies:
        pl.when(has[a])(copy.wait_send)
        pl.when(has[-a])(copy.wait_recv)
    for t in range(nlon):
        arrival = pltpu.make_async_remote_copy(
            src_ref=p_ref.at[pl.ds(t, 1)],
            dst_ref=inbox.at[pl.ds(t, 1)],
            send_sem=p_send.at[t],
            recv_sem=p_recv.at[t],
            device_id=(i, t),
            device_id_type=mesh,
        )
        pl.when(t != j)(sends[t].wait_send)
        pl.when(t != j)(arrival.wait_recv)
    o_ref[...] = buf[...]
    q_ref[...] = inbox[...]


EXCHANGE_IDS = {7: 0, 5: 1}


def exchange(block, width, payload):
    rows, cols, feats = block.shape
    edge = 16
    nlat = lax.axis_size("lat")
    nlon = lax.axis_size("lon")
    full = (rows + 2 * width, cols + 2 * edge, feats)
    vmem = pl.BlockSpec(memory_space=pltpu.VMEM)
    out, got = pl.pallas_call(
        functools.partial(halo_kernel, width, nlat, nlon),
        out_shape=(
            jax.ShapeDtypeStruct(full, block.dtype),
            jax.ShapeDtypeStruct(payload.shape, payload.dtype),
        ),
        in_specs=[vmem, vmem],
        out_specs=(vmem, vmem),
        scratch_shapes=[
            pltpu.VMEM(full, block.dtype),
            pltpu.VMEM(payload.shape, payload.dtype),
            pltpu.SemaphoreType.DMA((8,)),
            pltpu.SemaphoreType.DMA((8,)),
            pltpu.SemaphoreType.DMA((nlon,)),
            pltpu.SemaphoreType.DMA((nlon,)),
        ],
        compiler_params=pltpu.CompilerParams(
            collective_id=EXCHANGE_IDS[width], has_side_effects=True
        ),
    )(block, payload)
    return out[:, edge - width : edge + cols + width], got


def inside(field, tile_rows, halo):
    rows = field.shape[0]
    first = lax.axis_index("lat") * tile_rows - halo
    where = first + lax.broadcasted_iota(jnp.int32, (rows, 1, 1), 0)
    keep = (where >= 0) & (where < lax.axis_size("lat") * tile_rows)
    return jnp.where(keep, field, jnp.zeros_like(field))


def trim(field, width):
    return field[width : field.shape[0] - width, width : field.shape[1] - width]


def shards(
    state,
    kernel_in,
    kernel_mid,
    kernel_out,
    lift,
    obs_cells,
    obs_chan,
    obs_weights,
    obs_value,
    obs_count,
):
    rows, cols = (state.shape[0], state.shape[1])
    crows = rows // 2
    mat_in = banded(kernel_in, LEV)
    mat_mid = banded(kernel_mid, LEV)
    mat_out = banded(kernel_out, LEV)
    lift_full = block_diagonal(lift, LEV)
    packed = pack(obs_cells, obs_chan, obs_weights, obs_value, obs_count)
    padded, got = exchange(state, 7, packed)
    pre_first = conv_valid(padded, mat_in, rows + 12, cols + 12)
    act_first = jax.nn.gelu(pre_first, approximate=True).astype(jnp.bfloat16)
    pooled = (block_sum(act_first.astype(jnp.float32)) * 0.25).astype(jnp.bfloat16)
    pooled = inside(pooled, crows, 3)
    pre_mid = conv_valid(pooled, mat_mid, crows + 4, cols // 2 + 4)
    act_mid = jax.nn.gelu(trim(pre_mid, 1), approximate=True).astype(jnp.bfloat16)
    lifted = jnp.einsum("ijg,gf->ijf", act_mid, lift_full, preferred_element_type=jnp.float32)
    merged = (trim(act_first, 5).astype(jnp.float32) + trim(widen(lifted), 1)).astype(jnp.bfloat16)
    merged = inside(merged, rows, 1)
    pre_last = conv_valid(merged, mat_out, rows, cols)
    slope_first = gelu_slope(trim(pre_first, 5))
    slope_mid = gelu_slope(pre_mid)
    output = state.astype(jnp.float32) + jax.nn.gelu(pre_last, approximate=True)
    grad_out, innov = observe(output, got)
    grad_pre_last = (grad_out * gelu_slope(pre_last)).astype(jnp.bfloat16)
    grads, innovation = exchange(grad_pre_last, 5, innov.reshape(innov.shape[0], 1, innov.shape[1]))
    innovation = innovation.reshape(obs_value.shape)
    grad_merged = adjoint_valid(grads, mat_out, rows + 8, cols + 8)
    grad_coarse = block_sum(grad_merged).astype(jnp.bfloat16)
    back_mid = jnp.einsum("ijf,gf->ijg", grad_coarse, lift_full, preferred_element_type=jnp.float32)
    grad_mid = inside((back_mid * slope_mid).astype(jnp.bfloat16), crows, 2)
    grad_pooled = adjoint_valid(grad_mid, mat_mid, crows + 2, cols // 2 + 2)
    grad_first = (
        (trim(grad_merged, 3) + trim(widen(grad_pooled), 1) * 0.25) * slope_first
    ).astype(jnp.bfloat16)
    grad_first = inside(grad_first, rows, 1)
    gradient = grad_out + adjoint_valid(grad_first, mat_in, rows, cols)
    return (gradient, innovation)


def solution(mesh):
    placed = (
        P("lat", "lon", None),
        P(),
        P(),
        P(),
        P(),
        P("lat", "lon", None, None),
        P("lat", "lon", None),
        P("lat", "lon", None, None),
        P("lat", "lon", None),
        P("lat", "lon"),
    )
    return jax.shard_map(
        shards,
        mesh=mesh,
        in_specs=placed,
        out_specs=(P("lat", "lon", None), P("lat", "lon", None)),
        check_vma=False,
    )
```

```python
import jax
import jax.numpy as jnp
from jax import lax
import functools

from jax.experimental import pallas as pl
from jax.experimental.pallas import tpu as pltpu
from jax.sharding import PartitionSpec as P

C = 32
C2 = 64
LEV = 4


def with_halo(block, sides, width, periodic):
    for axis, dim in sides:
        count = lax.axis_size(axis)
        forward = [(i, i + 1) for i in range(count - 1)]
        if periodic:
            forward.append((count - 1, 0))
        backward = [(target, source) for source, target in forward]
        low = lax.ppermute(
            lax.slice_in_dim(block, block.shape[dim] - width, None, axis=dim), axis, forward
        )
        high = lax.ppermute(lax.slice_in_dim(block, 0, width, axis=dim), axis, backward)
        block = jnp.concatenate([low, block, high], axis=dim)
    return block


def banded(kernel, levels):
    zero = jnp.zeros(kernel.shape[:2] + kernel.shape[3:], kernel.dtype)
    rows = []
    for p in range(levels):
        blocks = [kernel[:, :, p - q + 1] if 0 <= p - q + 1 < 3 else zero for q in range(levels)]
        rows.append(jnp.concatenate(blocks, axis=-1))
    full = jnp.concatenate(rows, axis=-2)
    return full.reshape(9, full.shape[2], full.shape[3])


def block_diagonal(matrix, levels):
    zero = jnp.zeros_like(matrix)
    rows = [
        jnp.concatenate([matrix if p == q else zero for q in range(levels)], axis=1)
        for p in range(levels)
    ]
    return jnp.concatenate(rows, axis=0)


def gelu_slope(value):
    inner = 0.7978845608 * (value + 0.044715 * value**3)
    tval = jnp.tanh(inner)
    return 0.5 * (1.0 + tval) + 0.5 * value * (1.0 - tval * tval) * 0.7978845608 * (
        1.0 + 0.134145 * value * value
    )


def extend(field):
    wide = with_halo(field, (("lon", 1),), 1, True)
    return with_halo(wide, (("lat", 0),), 1, False)


def conv_valid(padded, matrices, rows, cols):
    taps = matrices.reshape(3, 3, matrices.shape[1], matrices.shape[2])
    out = lax.conv_general_dilated(
        padded[None],
        taps,
        (1, 1),
        "VALID",
        dimension_numbers=("NHWC", "HWIO", "NHWC"),
        preferred_element_type=jnp.float32,
    )
    return out[0]


def adjoint_valid(padded, matrices, rows, cols):
    taps = matrices.reshape(3, 3, matrices.shape[1], matrices.shape[2])
    taps = jnp.swapaxes(taps[::-1, ::-1], 2, 3)
    out = lax.conv_general_dilated(
        padded[None],
        taps,
        (1, 1),
        "VALID",
        dimension_numbers=("NHWC", "HWIO", "NHWC"),
        preferred_element_type=jnp.float32,
    )
    return out[0]


def convolve(field, matrices):
    return conv_valid(extend(field), matrices, field.shape[0], field.shape[1])


def convolve_adjoint(grads, matrices):
    return adjoint_valid(extend(grads), matrices, grads.shape[0], grads.shape[1])


def widen(coarse):
    rows, cols, feats = coarse.shape
    return jnp.broadcast_to(coarse[:, None, :, None, :], (rows, 2, cols, 2, feats)).reshape(
        rows * 2, cols * 2, feats
    )


def block_sum(fine):
    rows, cols, feats = fine.shape
    return fine.reshape(rows // 2, 2, cols // 2, 2, feats).sum(axis=(1, 3))


def split_bf16(value):
    high = lax.reduce_precision(value, exponent_bits=8, mantissa_bits=7)
    return high.astype(jnp.bfloat16), (value - high).astype(jnp.bfloat16)


def observe_kernel(got_ref, high_ref, low_ref, innov_ref, grad_ref):
    fields, nslot = got_ref.shape[1], got_ref.shape[2]
    feats, ncell = high_ref.shape
    cell_ids = lax.broadcasted_iota(jnp.int32, (ncell, nslot), 0).astype(jnp.float32)
    feat_ids = lax.broadcasted_iota(jnp.int32, (feats, nslot), 0).astype(jnp.float32)
    high = high_ref[...]
    low = low_ref[...]
    both = jnp.concatenate([high, low], axis=0)
    grad_ref[...] = jnp.zeros(grad_ref.shape, jnp.float32)
    trans = (((1,), (1,)), ((), ()))

    def body(owner, carry):
        block = got_ref[owner]
        table = jnp.zeros((ncell, nslot), jnp.float32)
        for j in range(4):
            table = table + jnp.where(
                cell_ids == block[j : j + 1, :], block[5 + j : 6 + j, :], 0.0
            )
        t_hi = table.astype(jnp.bfloat16)
        t_lo = (table - t_hi.astype(jnp.float32)).astype(jnp.bfloat16)
        two = jnp.dot(both, t_hi, preferred_element_type=jnp.float32)
        picked = two[:feats] + two[feats:] + jnp.dot(high, t_lo, preferred_element_type=jnp.float32)
        pick = feat_ids == block[4:5, :]
        innov = jnp.sum(jnp.where(pick, picked, 0.0), axis=0, keepdims=True) - block[9:10, :]
        innov_ref[owner] = innov
        spread = jnp.where(pick, innov, 0.0)
        s_hi = spread.astype(jnp.bfloat16)
        s_lo = (spread - s_hi.astype(jnp.float32)).astype(jnp.bfloat16)
        sums = lax.dot_general(
            t_hi, jnp.concatenate([s_hi, s_lo], axis=0), trans, preferred_element_type=jnp.float32
        )
        grad_ref[...] += (
            sums[:, :feats]
            + sums[:, feats:]
            + lax.dot_general(t_lo, s_hi, trans, preferred_element_type=jnp.float32)
        )
        return carry

    lax.fori_loop(0, got_ref.shape[0], body, 0)


def pack(obs_cells, obs_chan, obs_weights, obs_value, obs_count):
    slots = lax.broadcasted_iota(jnp.int32, obs_chan.shape, 2)
    live = (slots < obs_count[:, :, None]).astype(jnp.float32)
    weights = obs_weights * live[..., None]
    values = obs_value * live
    packed = jnp.concatenate(
        [
            jnp.swapaxes(obs_cells, 2, 3).astype(jnp.float32),
            obs_chan[:, :, None, :].astype(jnp.float32),
            jnp.swapaxes(weights, 2, 3),
            values[:, :, None, :],
        ],
        axis=2,
    )
    return packed.reshape(packed.shape[1:])


def observe(output, got):
    rows, cols, feats = output.shape
    ncell = rows * cols
    owners, nslot = got.shape[0], got.shape[2]
    o_hi, o_lo = split_bf16(output.reshape(ncell, feats).T)
    innov, grad = pl.pallas_call(
        observe_kernel,
        out_shape=(
            jax.ShapeDtypeStruct((owners, 1, nslot), jnp.float32),
            jax.ShapeDtypeStruct((ncell, feats), jnp.float32),
        ),
    )(got, o_hi, o_lo)
    return grad.reshape(rows, cols, feats), innov


def halo_kernel(
    width, nlat, nlon, x_ref, p_ref, o_ref, q_ref, buf, inbox, send_sem, recv_sem, p_send, p_recv
):
    rows, cols = x_ref.shape[0], x_ref.shape[1]
    edge = (buf.shape[1] - cols) // 2
    i = lax.axis_index("lat")
    j = lax.axis_index("lon")
    has = {-1: i > 0, 0: i >= 0, 1: i < nlat - 1}
    mesh = pl.DeviceIdType.MESH
    dirs = [(a, b) for a in (-1, 0, 1) for b in (-1, 0, 1) if (a, b) != (0, 0)]
    buf[...] = jnp.zeros(buf.shape, buf.dtype)
    buf[width : width + rows, edge : edge + cols, :] = x_ref[...]
    inbox[pl.ds(j, 1)] = p_ref[pl.ds(j, 1)]
    barrier = pltpu.get_barrier_semaphore()
    for a in (-1, 1):
        for b in (-1, 0, 1):

            @pl.when(has[a])
            def _():
                pl.semaphore_signal(
                    barrier, inc=1, device_id=((i + a) % nlat, (j + b) % nlon), device_id_type=mesh
                )

    for t in range(nlon):

        @pl.when(t != j)
        def _():
            pl.semaphore_signal(barrier, inc=1, device_id=(i, t), device_id_type=mesh)

    count = (nlon - 1) + 3 * has[-1].astype(jnp.int32) + 3 * has[1].astype(jnp.int32)
    pl.semaphore_wait(barrier, count)
    src_rows = {1: pl.ds(rows - width, width), -1: pl.ds(0, width), 0: pl.ds(0, rows)}
    dst_rows = {1: pl.ds(0, width), -1: pl.ds(width + rows, width), 0: pl.ds(width, rows)}
    src_cols = {1: pl.ds(cols - edge, edge), -1: pl.ds(0, edge), 0: pl.ds(0, cols)}
    dst_cols = {1: pl.ds(0, edge), -1: pl.ds(edge + cols, edge), 0: pl.ds(edge, cols)}
    copies = []
    for k, (a, b) in enumerate(dirs):
        copy = pltpu.make_async_remote_copy(
            src_ref=x_ref.at[src_rows[a], src_cols[b]],
            dst_ref=buf.at[dst_rows[a], dst_cols[b]],
            send_sem=send_sem.at[k],
            recv_sem=recv_sem.at[k],
            device_id=((i + a) % nlat, (j + b) % nlon),
            device_id_type=mesh,
        )
        copies.append((a, copy))
        pl.when(has[a])(copy.start)
    sends = []
    for t in range(nlon):
        copy = pltpu.make_async_remote_copy(
            src_ref=p_ref.at[pl.ds(t, 1)],
            dst_ref=inbox.at[pl.ds(j, 1)],
            send_sem=p_send.at[t],
            recv_sem=p_recv.at[j],
            device_id=(i, t),
            device_id_type=mesh,
        )
        sends.append(copy)
        pl.when(t != j)(copy.start)
    for a, copy in copies:
        pl.when(has[a])(copy.wait_send)
        pl.when(has[-a])(copy.wait_recv)
    for t in range(nlon):
        arrival = pltpu.make_async_remote_copy(
            src_ref=p_ref.at[pl.ds(t, 1)],
            dst_ref=inbox.at[pl.ds(t, 1)],
            send_sem=p_send.at[t],
            recv_sem=p_recv.at[t],
            device_id=(i, t),
            device_id_type=mesh,
        )
        pl.when(t != j)(sends[t].wait_send)
        pl.when(t != j)(arrival.wait_recv)
    o_ref[...] = buf[...]
    q_ref[...] = inbox[...]


EXCHANGE_IDS = {7: 0, 5: 1}


def exchange(block, width, payload):
    rows, cols, feats = block.shape
    edge = 16
    nlat = lax.axis_size("lat")
    nlon = lax.axis_size("lon")
    full = (rows + 2 * width, cols + 2 * edge, feats)
    vmem = pl.BlockSpec(memory_space=pltpu.VMEM)
    out, got = pl.pallas_call(
        functools.partial(halo_kernel, width, nlat, nlon),
        out_shape=(
            jax.ShapeDtypeStruct(full, block.dtype),
            jax.ShapeDtypeStruct(payload.shape, payload.dtype),
        ),
        in_specs=[vmem, vmem],
        out_specs=(vmem, vmem),
        scratch_shapes=[
            pltpu.VMEM(full, block.dtype),
            pltpu.VMEM(payload.shape, payload.dtype),
            pltpu.SemaphoreType.DMA((8,)),
            pltpu.SemaphoreType.DMA((8,)),
            pltpu.SemaphoreType.DMA((nlon,)),
            pltpu.SemaphoreType.DMA((nlon,)),
        ],
        compiler_params=pltpu.CompilerParams(
            collective_id=EXCHANGE_IDS[width], has_side_effects=True
        ),
    )(block, payload)
    return out[:, edge - width : edge + cols + width], got


def inside(field, tile_rows, halo):
    rows = field.shape[0]
    first = lax.axis_index("lat") * tile_rows - halo
    where = first + lax.broadcasted_iota(jnp.int32, (rows, 1, 1), 0)
    keep = (where >= 0) & (where < lax.axis_size("lat") * tile_rows)
    return jnp.where(keep, field, jnp.zeros_like(field))


def trim(field, width):
    return field[width : field.shape[0] - width, width : field.shape[1] - width]


def shards(
    state,
    kernel_in,
    kernel_mid,
    kernel_out,
    lift,
    obs_cells,
    obs_chan,
    obs_weights,
    obs_value,
    obs_count,
):
    rows, cols = (state.shape[0], state.shape[1])
    crows = rows // 2
    mat_in = banded(kernel_in, LEV)
    mat_mid = banded(kernel_mid, LEV)
    mat_out = banded(kernel_out, LEV)
    lift_full = block_diagonal(lift, LEV)
    packed = pack(obs_cells, obs_chan, obs_weights, obs_value, obs_count)
    padded, got = exchange(state, 7, packed)
    pre_first = conv_valid(padded, mat_in, rows + 12, cols + 12)
    act_first = jax.nn.gelu(pre_first, approximate=True).astype(jnp.bfloat16)
    pooled = (block_sum(act_first.astype(jnp.float32)) * 0.25).astype(jnp.bfloat16)
    pooled = inside(pooled, crows, 3)
    pre_mid = conv_valid(pooled, mat_mid, crows + 4, cols // 2 + 4)
    act_mid = jax.nn.gelu(trim(pre_mid, 1), approximate=True).astype(jnp.bfloat16)
    lifted = jnp.einsum("ijg,gf->ijf", act_mid, lift_full, preferred_element_type=jnp.float32)
    merged = (trim(act_first, 5).astype(jnp.float32) + trim(widen(lifted), 1)).astype(jnp.bfloat16)
    merged = inside(merged, rows, 1)
    pre_last = conv_valid(merged, mat_out, rows, cols)
    slope_first = gelu_slope(trim(pre_first, 5))
    slope_mid = gelu_slope(pre_mid)
    output = state.astype(jnp.float32) + jax.nn.gelu(pre_last, approximate=True)
    grad_out, innov = observe(output, got)
    grad_pre_last = (grad_out * gelu_slope(pre_last)).astype(jnp.bfloat16)
    grads, innovation = exchange(grad_pre_last, 5, innov)
    innovation = innovation.reshape(obs_value.shape)
    grad_merged = adjoint_valid(grads, mat_out, rows + 8, cols + 8)
    grad_coarse = block_sum(grad_merged).astype(jnp.bfloat16)
    back_mid = jnp.einsum("ijf,gf->ijg", grad_coarse, lift_full, preferred_element_type=jnp.float32)
    grad_mid = inside((back_mid * slope_mid).astype(jnp.bfloat16), crows, 2)
    grad_pooled = adjoint_valid(grad_mid, mat_mid, crows + 2, cols // 2 + 2)
    grad_first = (
        (trim(grad_merged, 3) + trim(widen(grad_pooled), 1) * 0.25) * slope_first
    ).astype(jnp.bfloat16)
    grad_first = inside(grad_first, rows, 1)
    gradient = grad_out + adjoint_valid(grad_first, mat_in, rows, cols)
    return (gradient, innovation)


def solution(mesh):
    placed = (
        P("lat", "lon", None),
        P(),
        P(),
        P(),
        P(),
        P("lat", "lon", None, None),
        P("lat", "lon", None),
        P("lat", "lon", None, None),
        P("lat", "lon", None),
        P("lat", "lon"),
    )
    return jax.shard_map(
        shards,
        mesh=mesh,
        in_specs=placed,
        out_specs=(P("lat", "lon", None), P("lat", "lon", None)),
        check_vma=False,
    )
```

```python
import jax
import jax.numpy as jnp
from jax import lax
import functools

from jax.experimental import pallas as pl
from jax.experimental.pallas import tpu as pltpu
from jax.sharding import PartitionSpec as P

C = 32
C2 = 64
LEV = 4


def with_halo(block, sides, width, periodic):
    for axis, dim in sides:
        count = lax.axis_size(axis)
        forward = [(i, i + 1) for i in range(count - 1)]
        if periodic:
            forward.append((count - 1, 0))
        backward = [(target, source) for source, target in forward]
        low = lax.ppermute(
            lax.slice_in_dim(block, block.shape[dim] - width, None, axis=dim), axis, forward
        )
        high = lax.ppermute(lax.slice_in_dim(block, 0, width, axis=dim), axis, backward)
        block = jnp.concatenate([low, block, high], axis=dim)
    return block


def banded(kernel, levels):
    zero = jnp.zeros(kernel.shape[:2] + kernel.shape[3:], kernel.dtype)
    rows = []
    for p in range(levels):
        blocks = [kernel[:, :, p - q + 1] if 0 <= p - q + 1 < 3 else zero for q in range(levels)]
        rows.append(jnp.concatenate(blocks, axis=-1))
    full = jnp.concatenate(rows, axis=-2)
    return full.reshape(9, full.shape[2], full.shape[3])


def block_diagonal(matrix, levels):
    zero = jnp.zeros_like(matrix)
    rows = [
        jnp.concatenate([matrix if p == q else zero for q in range(levels)], axis=1)
        for p in range(levels)
    ]
    return jnp.concatenate(rows, axis=0)


def gelu_slope(value):
    inner = 0.7978845608 * (value + 0.044715 * value**3)
    tval = jnp.tanh(inner)
    return 0.5 * (1.0 + tval) + 0.5 * value * (1.0 - tval * tval) * 0.7978845608 * (
        1.0 + 0.134145 * value * value
    )


def extend(field):
    wide = with_halo(field, (("lon", 1),), 1, True)
    return with_halo(wide, (("lat", 0),), 1, False)


def conv_valid(padded, matrices, rows, cols):
    taps = matrices.reshape(3, 3, matrices.shape[1], matrices.shape[2])
    out = lax.conv_general_dilated(
        padded[None],
        taps,
        (1, 1),
        "VALID",
        dimension_numbers=("NHWC", "HWIO", "NHWC"),
        preferred_element_type=jnp.float32,
    )
    return out[0]


def adjoint_valid(padded, matrices, rows, cols):
    taps = matrices.reshape(3, 3, matrices.shape[1], matrices.shape[2])
    taps = jnp.swapaxes(taps[::-1, ::-1], 2, 3)
    out = lax.conv_general_dilated(
        padded[None],
        taps,
        (1, 1),
        "VALID",
        dimension_numbers=("NHWC", "HWIO", "NHWC"),
        preferred_element_type=jnp.float32,
    )
    return out[0]


def convolve(field, matrices):
    return conv_valid(extend(field), matrices, field.shape[0], field.shape[1])


def convolve_adjoint(grads, matrices):
    return adjoint_valid(extend(grads), matrices, grads.shape[0], grads.shape[1])


def widen(coarse):
    rows, cols, feats = coarse.shape
    return jnp.broadcast_to(coarse[:, None, :, None, :], (rows, 2, cols, 2, feats)).reshape(
        rows * 2, cols * 2, feats
    )


def block_sum(fine):
    rows, cols, feats = fine.shape
    return fine.reshape(rows // 2, 2, cols // 2, 2, feats).sum(axis=(1, 3))


def split_bf16(value):
    high = lax.reduce_precision(value, exponent_bits=8, mantissa_bits=7)
    return high.astype(jnp.bfloat16), (value - high).astype(jnp.bfloat16)


def observe_kernel(got_ref, high_ref, low_ref, innov_ref, grad_ref):
    fields, nslot = got_ref.shape[1], got_ref.shape[2]
    feats, ncell = high_ref.shape
    cell_ids = lax.broadcasted_iota(jnp.int32, (ncell, nslot), 0).astype(jnp.float32)
    feat_ids = lax.broadcasted_iota(jnp.int32, (feats, nslot), 0).astype(jnp.float32)
    high = high_ref[...]
    low = low_ref[...]
    both = jnp.concatenate([high, low], axis=0)
    grad_ref[...] = jnp.zeros(grad_ref.shape, jnp.float32)
    trans = (((1,), (1,)), ((), ()))

    def body(owner, carry):
        block = got_ref[owner]
        table = jnp.zeros((ncell, nslot), jnp.float32)
        for j in range(4):
            table = table + jnp.where(
                cell_ids == block[j : j + 1, :], block[5 + j : 6 + j, :], 0.0
            )
        t_hi = table.astype(jnp.bfloat16)
        t_lo = (table - t_hi.astype(jnp.float32)).astype(jnp.bfloat16)
        two = jnp.dot(both, t_hi, preferred_element_type=jnp.float32)
        picked = two[:feats] + two[feats:] + jnp.dot(high, t_lo, preferred_element_type=jnp.float32)
        pick = feat_ids == block[4:5, :]
        innov = jnp.sum(jnp.where(pick, picked, 0.0), axis=0, keepdims=True) - block[9:10, :]
        innov_ref[owner] = innov
        spread = jnp.where(pick, innov, 0.0)
        s_hi = spread.astype(jnp.bfloat16)
        s_lo = (spread - s_hi.astype(jnp.float32)).astype(jnp.bfloat16)
        sums = lax.dot_general(
            t_hi, jnp.concatenate([s_hi, s_lo], axis=0), trans, preferred_element_type=jnp.float32
        )
        grad_ref[...] += (
            sums[:, :feats]
            + sums[:, feats:]
            + lax.dot_general(t_lo, s_hi, trans, preferred_element_type=jnp.float32)
        )
        return carry

    lax.fori_loop(0, got_ref.shape[0], body, 0)


def pack(obs_cells, obs_chan, obs_weights, obs_value, obs_count):
    slots = lax.broadcasted_iota(jnp.int32, obs_chan.shape, 2)
    live = (slots < obs_count[:, :, None]).astype(jnp.float32)
    weights = obs_weights * live[..., None]
    values = obs_value * live
    packed = jnp.concatenate(
        [
            jnp.swapaxes(obs_cells, 2, 3).astype(jnp.float32),
            obs_chan[:, :, None, :].astype(jnp.float32),
            jnp.swapaxes(weights, 2, 3),
            values[:, :, None, :],
        ],
        axis=2,
    )
    return packed.reshape(packed.shape[1:])


def observe(output, got):
    rows, cols, feats = output.shape
    ncell = rows * cols
    owners, nslot = got.shape[0], got.shape[2]
    o_hi, o_lo = split_bf16(output.reshape(ncell, feats).T)
    innov, grad = pl.pallas_call(
        observe_kernel,
        out_shape=(
            jax.ShapeDtypeStruct((owners, 1, nslot), jnp.float32),
            jax.ShapeDtypeStruct((ncell, feats), jnp.float32),
        ),
    )(got, o_hi, o_lo)
    return grad.reshape(rows, cols, feats), innov


def greet(nlat, nlon):
    i = lax.axis_index("lat")
    j = lax.axis_index("lon")
    has = {-1: i > 0, 0: i >= 0, 1: i < nlat - 1}
    mesh = pl.DeviceIdType.MESH
    barrier = pltpu.get_barrier_semaphore()
    for a in (-1, 1):
        for b in (-1, 0, 1):

            @pl.when(has[a])
            def _():
                pl.semaphore_signal(
                    barrier, inc=1, device_id=((i + a) % nlat, (j + b) % nlon), device_id_type=mesh
                )

    for t in range(nlon):

        @pl.when(t != j)
        def _():
            pl.semaphore_signal(barrier, inc=1, device_id=(i, t), device_id_type=mesh)

    return (nlon - 1) + 3 * has[-1].astype(jnp.int32) + 3 * has[1].astype(jnp.int32)


def trade(width, nlat, nlon, count, x_ref, p_ref, buf, inbox, send_sem, recv_sem, p_send, p_recv):
    rows, cols = x_ref.shape[0], x_ref.shape[1]
    edge = (buf.shape[1] - cols) // 2
    i = lax.axis_index("lat")
    j = lax.axis_index("lon")
    has = {-1: i > 0, 0: i >= 0, 1: i < nlat - 1}
    mesh = pl.DeviceIdType.MESH
    dirs = [(a, b) for a in (-1, 0, 1) for b in (-1, 0, 1) if (a, b) != (0, 0)]
    pl.semaphore_wait(pltpu.get_barrier_semaphore(), count)
    src_rows = {1: pl.ds(rows - width, width), -1: pl.ds(0, width), 0: pl.ds(0, rows)}
    dst_rows = {1: pl.ds(0, width), -1: pl.ds(width + rows, width), 0: pl.ds(width, rows)}
    src_cols = {1: pl.ds(cols - edge, edge), -1: pl.ds(0, edge), 0: pl.ds(0, cols)}
    dst_cols = {1: pl.ds(0, edge), -1: pl.ds(edge + cols, edge), 0: pl.ds(edge, cols)}
    copies = []
    for k, (a, b) in enumerate(dirs):
        copy = pltpu.make_async_remote_copy(
            src_ref=x_ref.at[src_rows[a], src_cols[b]],
            dst_ref=buf.at[dst_rows[a], dst_cols[b]],
            send_sem=send_sem.at[k],
            recv_sem=recv_sem.at[k],
            device_id=((i + a) % nlat, (j + b) % nlon),
            device_id_type=mesh,
        )
        copies.append((a, copy))
        pl.when(has[a])(copy.start)
    sends = []
    for t in range(nlon):
        copy = pltpu.make_async_remote_copy(
            src_ref=p_ref.at[pl.ds(t, 1)],
            dst_ref=inbox.at[pl.ds(j, 1)],
            send_sem=p_send.at[t],
            recv_sem=p_recv.at[j],
            device_id=(i, t),
            device_id_type=mesh,
        )
        sends.append(copy)
        pl.when(t != j)(copy.start)
    for a, copy in copies:
        pl.when(has[a])(copy.wait_send)
        pl.when(has[-a])(copy.wait_recv)
    for t in range(nlon):
        arrival = pltpu.make_async_remote_copy(
            src_ref=p_ref.at[pl.ds(t, 1)],
            dst_ref=inbox.at[pl.ds(t, 1)],
            send_sem=p_send.at[t],
            recv_sem=p_recv.at[t],
            device_id=(i, t),
            device_id_type=mesh,
        )
        pl.when(t != j)(sends[t].wait_send)
        pl.when(t != j)(arrival.wait_recv)


def halo_kernel(width, nlat, nlon, x_ref, p_ref, o_ref, q_ref, buf, inbox, *sems):
    rows, cols = x_ref.shape[0], x_ref.shape[1]
    edge = (buf.shape[1] - cols) // 2
    j = lax.axis_index("lon")
    buf[...] = jnp.zeros(buf.shape, buf.dtype)
    buf[width : width + rows, edge : edge + cols, :] = x_ref[...]
    inbox[pl.ds(j, 1)] = p_ref[pl.ds(j, 1)]
    count = greet(nlat, nlon)
    trade(width, nlat, nlon, count, x_ref, p_ref, buf, inbox, *sems)
    o_ref[...] = buf[...]
    q_ref[...] = inbox[...]


def back_kernel(
    width, nlat, nlon, got_ref, high_ref, low_ref, slope_ref,
    grad_ref, o_ref, q_ref, buf, inbox, innov_ref, x_src, *sems
):
    rows, cols = x_src.shape[0], x_src.shape[1]
    edge = (buf.shape[1] - cols) // 2
    j = lax.axis_index("lon")
    buf[...] = jnp.zeros(buf.shape, buf.dtype)
    count = greet(nlat, nlon)
    observe_kernel(got_ref, high_ref, low_ref, innov_ref, grad_ref)
    grads = (grad_ref[...] * slope_ref[...]).astype(x_src.dtype).reshape(x_src.shape)
    x_src[...] = grads
    trade(width, nlat, nlon, count, x_src, innov_ref, buf, inbox, *sems)
    buf[width : width + rows, edge : edge + cols, :] = x_src[...]
    inbox[pl.ds(j, 1)] = innov_ref[pl.ds(j, 1)]
    o_ref[...] = buf[...]
    q_ref[...] = inbox[...]


def sem_scratch(nlon):
    return [
        pltpu.SemaphoreType.DMA((8,)),
        pltpu.SemaphoreType.DMA((8,)),
        pltpu.SemaphoreType.DMA((nlon,)),
        pltpu.SemaphoreType.DMA((nlon,)),
    ]


def exchange(block, width, payload):
    rows, cols, feats = block.shape
    edge = 16
    nlat = lax.axis_size("lat")
    nlon = lax.axis_size("lon")
    full = (rows + 2 * width, cols + 2 * edge, feats)
    vmem = pl.BlockSpec(memory_space=pltpu.VMEM)
    out, got = pl.pallas_call(
        functools.partial(halo_kernel, width, nlat, nlon),
        out_shape=(
            jax.ShapeDtypeStruct(full, block.dtype),
            jax.ShapeDtypeStruct(payload.shape, payload.dtype),
        ),
        in_specs=[vmem, vmem],
        out_specs=(vmem, vmem),
        scratch_shapes=[
            pltpu.VMEM(full, block.dtype),
            pltpu.VMEM(payload.shape, payload.dtype),
        ]
        + sem_scratch(nlon),
        compiler_params=pltpu.CompilerParams(collective_id=0, has_side_effects=True),
    )(block, payload)
    return out[:, edge - width : edge + cols + width], got


def observe_and_exchange(output, got, slope, width):
    rows, cols, feats = output.shape
    ncell = rows * cols
    edge = 16
    nlat = lax.axis_size("lat")
    nlon = lax.axis_size("lon")
    owners, nslot = got.shape[0], got.shape[2]
    o_hi, o_lo = split_bf16(output.reshape(ncell, feats).T)
    full = (rows + 2 * width, cols + 2 * edge, feats)
    vmem = pl.BlockSpec(memory_space=pltpu.VMEM)
    innov_shape = (owners, 1, nslot)
    grad, out, innovation = pl.pallas_call(
        functools.partial(back_kernel, width, nlat, nlon),
        out_shape=(
            jax.ShapeDtypeStruct((ncell, feats), jnp.float32),
            jax.ShapeDtypeStruct(full, jnp.bfloat16),
            jax.ShapeDtypeStruct(innov_shape, jnp.float32),
        ),
        in_specs=[vmem] * 4,
        out_specs=(vmem, vmem, vmem),
        scratch_shapes=[
            pltpu.VMEM(full, jnp.bfloat16),
            pltpu.VMEM(innov_shape, jnp.float32),
            pltpu.VMEM(innov_shape, jnp.float32),
            pltpu.VMEM((rows, cols, feats), jnp.bfloat16),
        ]
        + sem_scratch(nlon),
        compiler_params=pltpu.CompilerParams(collective_id=1, has_side_effects=True),
    )(got, o_hi, o_lo, slope.reshape(ncell, feats))
    grads = out[:, edge - width : edge + cols + width]
    return grad.reshape(rows, cols, feats), grads, innovation


def inside(field, tile_rows, halo):
    rows = field.shape[0]
    first = lax.axis_index("lat") * tile_rows - halo
    where = first + lax.broadcasted_iota(jnp.int32, (rows, 1, 1), 0)
    keep = (where >= 0) & (where < lax.axis_size("lat") * tile_rows)
    return jnp.where(keep, field, jnp.zeros_like(field))


def trim(field, width):
    return field[width : field.shape[0] - width, width : field.shape[1] - width]


def shards(
    state,
    kernel_in,
    kernel_mid,
    kernel_out,
    lift,
    obs_cells,
    obs_chan,
    obs_weights,
    obs_value,
    obs_count,
):
    rows, cols = (state.shape[0], state.shape[1])
    crows = rows // 2
    mat_in = banded(kernel_in, LEV)
    mat_mid = banded(kernel_mid, LEV)
    mat_out = banded(kernel_out, LEV)
    lift_full = block_diagonal(lift, LEV)
    packed = pack(obs_cells, obs_chan, obs_weights, obs_value, obs_count)
    padded, got = exchange(state, 7, packed)
    pre_first = conv_valid(padded, mat_in, rows + 12, cols + 12)
    act_first = jax.nn.gelu(pre_first, approximate=True).astype(jnp.bfloat16)
    pooled = (block_sum(act_first.astype(jnp.float32)) * 0.25).astype(jnp.bfloat16)
    pooled = inside(pooled, crows, 3)
    pre_mid = conv_valid(pooled, mat_mid, crows + 4, cols // 2 + 4)
    act_mid = jax.nn.gelu(trim(pre_mid, 1), approximate=True).astype(jnp.bfloat16)
    lifted = jnp.einsum("ijg,gf->ijf", act_mid, lift_full, preferred_element_type=jnp.float32)
    merged = (trim(act_first, 5).astype(jnp.float32) + trim(widen(lifted), 1)).astype(jnp.bfloat16)
    merged = inside(merged, rows, 1)
    pre_last = conv_valid(merged, mat_out, rows, cols)
    slope_first = gelu_slope(trim(pre_first, 5))
    slope_mid = gelu_slope(pre_mid)
    output = state.astype(jnp.float32) + jax.nn.gelu(pre_last, approximate=True)
    grad_out, grads, innovation = observe_and_exchange(output, got, gelu_slope(pre_last), 5)
    innovation = innovation.reshape(obs_value.shape)
    grad_merged = adjoint_valid(grads, mat_out, rows + 8, cols + 8)
    grad_coarse = block_sum(grad_merged).astype(jnp.bfloat16)
    back_mid = jnp.einsum("ijf,gf->ijg", grad_coarse, lift_full, preferred_element_type=jnp.float32)
    grad_mid = inside((back_mid * slope_mid).astype(jnp.bfloat16), crows, 2)
    grad_pooled = adjoint_valid(grad_mid, mat_mid, crows + 2, cols // 2 + 2)
    grad_first = (
        (trim(grad_merged, 3) + trim(widen(grad_pooled), 1) * 0.25) * slope_first
    ).astype(jnp.bfloat16)
    grad_first = inside(grad_first, rows, 1)
    gradient = grad_out + adjoint_valid(grad_first, mat_in, rows, cols)
    return (gradient, innovation)


def solution(mesh):
    placed = (
        P("lat", "lon", None),
        P(),
        P(),
        P(),
        P(),
        P("lat", "lon", None, None),
        P("lat", "lon", None),
        P("lat", "lon", None, None),
        P("lat", "lon", None),
        P("lat", "lon"),
    )
    return jax.shard_map(
        shards,
        mesh=mesh,
        in_specs=placed,
        out_specs=(P("lat", "lon", None), P("lat", "lon", None)),
        check_vma=False,
    )
```

```python
import jax
import jax.numpy as jnp
from jax import lax
import functools

from jax.experimental import pallas as pl
from jax.experimental.pallas import tpu as pltpu
from jax.sharding import PartitionSpec as P

C = 32
C2 = 64
LEV = 4


def with_halo(block, sides, width, periodic):
    for axis, dim in sides:
        count = lax.axis_size(axis)
        forward = [(i, i + 1) for i in range(count - 1)]
        if periodic:
            forward.append((count - 1, 0))
        backward = [(target, source) for source, target in forward]
        low = lax.ppermute(
            lax.slice_in_dim(block, block.shape[dim] - width, None, axis=dim), axis, forward
        )
        high = lax.ppermute(lax.slice_in_dim(block, 0, width, axis=dim), axis, backward)
        block = jnp.concatenate([low, block, high], axis=dim)
    return block


def banded(kernel, levels):
    zero = jnp.zeros(kernel.shape[:2] + kernel.shape[3:], kernel.dtype)
    rows = []
    for p in range(levels):
        blocks = [kernel[:, :, p - q + 1] if 0 <= p - q + 1 < 3 else zero for q in range(levels)]
        rows.append(jnp.concatenate(blocks, axis=-1))
    full = jnp.concatenate(rows, axis=-2)
    return full.reshape(9, full.shape[2], full.shape[3])


def block_diagonal(matrix, levels):
    zero = jnp.zeros_like(matrix)
    rows = [
        jnp.concatenate([matrix if p == q else zero for q in range(levels)], axis=1)
        for p in range(levels)
    ]
    return jnp.concatenate(rows, axis=0)


def gelu_slope(value):
    inner = 0.7978845608 * (value + 0.044715 * value**3)
    tval = jnp.tanh(inner)
    return 0.5 * (1.0 + tval) + 0.5 * value * (1.0 - tval * tval) * 0.7978845608 * (
        1.0 + 0.134145 * value * value
    )


def extend(field):
    wide = with_halo(field, (("lon", 1),), 1, True)
    return with_halo(wide, (("lat", 0),), 1, False)


def conv_valid(padded, matrices, rows, cols):
    taps = matrices.reshape(3, 3, matrices.shape[1], matrices.shape[2])
    out = lax.conv_general_dilated(
        padded[None],
        taps,
        (1, 1),
        "VALID",
        dimension_numbers=("NHWC", "HWIO", "NHWC"),
        preferred_element_type=jnp.float32,
    )
    return out[0]


def adjoint_valid(padded, matrices, rows, cols):
    taps = matrices.reshape(3, 3, matrices.shape[1], matrices.shape[2])
    taps = jnp.swapaxes(taps[::-1, ::-1], 2, 3)
    out = lax.conv_general_dilated(
        padded[None],
        taps,
        (1, 1),
        "VALID",
        dimension_numbers=("NHWC", "HWIO", "NHWC"),
        preferred_element_type=jnp.float32,
    )
    return out[0]


def convolve(field, matrices):
    return conv_valid(extend(field), matrices, field.shape[0], field.shape[1])


def convolve_adjoint(grads, matrices):
    return adjoint_valid(extend(grads), matrices, grads.shape[0], grads.shape[1])


def widen(coarse):
    rows, cols, feats = coarse.shape
    return jnp.broadcast_to(coarse[:, None, :, None, :], (rows, 2, cols, 2, feats)).reshape(
        rows * 2, cols * 2, feats
    )


def block_sum(fine):
    rows, cols, feats = fine.shape
    return fine.reshape(rows // 2, 2, cols // 2, 2, feats).sum(axis=(1, 3))


def split_bf16(value):
    high = lax.reduce_precision(value, exponent_bits=8, mantissa_bits=7)
    return high.astype(jnp.bfloat16), (value - high).astype(jnp.bfloat16)


def observe_kernel(got_ref, high_ref, low_ref, innov_ref, grad_ref):
    fields, nslot = got_ref.shape[1], got_ref.shape[2]
    feats, ncell = high_ref.shape
    cell_ids = lax.broadcasted_iota(jnp.int32, (ncell, nslot), 0).astype(jnp.float32)
    feat_ids = lax.broadcasted_iota(jnp.int32, (feats, nslot), 0).astype(jnp.float32)
    high = high_ref[...]
    low = low_ref[...]
    both = jnp.concatenate([high, low], axis=0)
    grad_ref[...] = jnp.zeros(grad_ref.shape, jnp.float32)
    trans = (((1,), (1,)), ((), ()))

    def body(owner, carry):
        block = got_ref[owner]
        table = jnp.zeros((ncell, nslot), jnp.float32)
        for j in range(4):
            table = table + jnp.where(
                cell_ids == block[j : j + 1, :], block[5 + j : 6 + j, :], 0.0
            )
        t_hi = table.astype(jnp.bfloat16)
        t_lo = (table - t_hi.astype(jnp.float32)).astype(jnp.bfloat16)
        two = jnp.dot(both, t_hi, preferred_element_type=jnp.float32)
        picked = two[:feats] + two[feats:] + jnp.dot(high, t_lo, preferred_element_type=jnp.float32)
        pick = feat_ids == block[4:5, :]
        innov = jnp.sum(jnp.where(pick, picked, 0.0), axis=0, keepdims=True) - block[9:10, :]
        innov_ref[owner] = innov
        spread = jnp.where(pick, innov, 0.0)
        s_hi = spread.astype(jnp.bfloat16)
        s_lo = (spread - s_hi.astype(jnp.float32)).astype(jnp.bfloat16)
        sums = lax.dot_general(
            t_hi, jnp.concatenate([s_hi, s_lo], axis=0), trans, preferred_element_type=jnp.float32
        )
        grad_ref[...] += (
            sums[:, :feats]
            + sums[:, feats:]
            + lax.dot_general(t_lo, s_hi, trans, preferred_element_type=jnp.float32)
        )
        return carry

    lax.fori_loop(0, got_ref.shape[0], body, 0)


def pack(obs_cells, obs_chan, obs_weights, obs_value, obs_count):
    slots = lax.broadcasted_iota(jnp.int32, obs_chan.shape, 2)
    live = (slots < obs_count[:, :, None]).astype(jnp.float32)
    weights = obs_weights * live[..., None]
    values = obs_value * live
    packed = jnp.concatenate(
        [
            jnp.swapaxes(obs_cells, 2, 3).astype(jnp.float32),
            obs_chan[:, :, None, :].astype(jnp.float32),
            jnp.swapaxes(weights, 2, 3),
            values[:, :, None, :],
        ],
        axis=2,
    )
    return packed.reshape(packed.shape[1:])


def observe(output, got):
    rows, cols, feats = output.shape
    ncell = rows * cols
    owners, nslot = got.shape[0], got.shape[2]
    o_hi, o_lo = split_bf16(output.reshape(ncell, feats).T)
    innov, grad = pl.pallas_call(
        observe_kernel,
        out_shape=(
            jax.ShapeDtypeStruct((owners, 1, nslot), jnp.float32),
            jax.ShapeDtypeStruct((ncell, feats), jnp.float32),
        ),
    )(got, o_hi, o_lo)
    return grad.reshape(rows, cols, feats), innov


def greet(nlat, nlon):
    i = lax.axis_index("lat")
    j = lax.axis_index("lon")
    has = {-1: i > 0, 0: i >= 0, 1: i < nlat - 1}
    mesh = pl.DeviceIdType.MESH
    barrier = pltpu.get_barrier_semaphore()
    for a in (-1, 1):
        for b in (-1, 0, 1):

            @pl.when(has[a])
            def _():
                pl.semaphore_signal(
                    barrier, inc=1, device_id=((i + a) % nlat, (j + b) % nlon), device_id_type=mesh
                )

    for t in range(nlon):

        @pl.when(t != j)
        def _():
            pl.semaphore_signal(barrier, inc=1, device_id=(i, t), device_id_type=mesh)

    return (nlon - 1) + 3 * has[-1].astype(jnp.int32) + 3 * has[1].astype(jnp.int32)


def trade(width, nlat, nlon, count, x_ref, p_ref, buf, inbox, send_sem, recv_sem, p_send, p_recv):
    rows, cols = x_ref.shape[0], x_ref.shape[1]
    edge = (buf.shape[1] - cols) // 2
    i = lax.axis_index("lat")
    j = lax.axis_index("lon")
    has = {-1: i > 0, 0: i >= 0, 1: i < nlat - 1}
    mesh = pl.DeviceIdType.MESH
    dirs = [(a, b) for a in (-1, 0, 1) for b in (-1, 0, 1) if (a, b) != (0, 0)]
    pl.semaphore_wait(pltpu.get_barrier_semaphore(), count)
    src_rows = {1: pl.ds(rows - width, width), -1: pl.ds(0, width), 0: pl.ds(0, rows)}
    dst_rows = {1: pl.ds(0, width), -1: pl.ds(width + rows, width), 0: pl.ds(width, rows)}
    src_cols = {1: pl.ds(cols - edge, edge), -1: pl.ds(0, edge), 0: pl.ds(0, cols)}
    dst_cols = {1: pl.ds(0, edge), -1: pl.ds(edge + cols, edge), 0: pl.ds(edge, cols)}
    copies = []
    for k, (a, b) in enumerate(dirs):
        copy = pltpu.make_async_remote_copy(
            src_ref=x_ref.at[src_rows[a], src_cols[b]],
            dst_ref=buf.at[dst_rows[a], dst_cols[b]],
            send_sem=send_sem.at[k],
            recv_sem=recv_sem.at[k],
            device_id=((i + a) % nlat, (j + b) % nlon),
            device_id_type=mesh,
        )
        copies.append((a, copy))
        pl.when(has[a])(copy.start)
    sends = []
    for t in range(nlon):
        copy = pltpu.make_async_remote_copy(
            src_ref=p_ref.at[pl.ds(t, 1)],
            dst_ref=inbox.at[pl.ds(j, 1)],
            send_sem=p_send.at[t],
            recv_sem=p_recv.at[j],
            device_id=(i, t),
            device_id_type=mesh,
        )
        sends.append(copy)
        pl.when(t != j)(copy.start)
    for a, copy in copies:
        pl.when(has[a])(copy.wait_send)
        pl.when(has[-a])(copy.wait_recv)
    for t in range(nlon):
        arrival = pltpu.make_async_remote_copy(
            src_ref=p_ref.at[pl.ds(t, 1)],
            dst_ref=inbox.at[pl.ds(t, 1)],
            send_sem=p_send.at[t],
            recv_sem=p_recv.at[t],
            device_id=(i, t),
            device_id_type=mesh,
        )
        pl.when(t != j)(sends[t].wait_send)
        pl.when(t != j)(arrival.wait_recv)


def band_into(k_ref, t_ref):
    levels = t_ref.shape[2] // k_ref.shape[3]
    cin, cout = k_ref.shape[3], k_ref.shape[4]
    t_ref[...] = jnp.zeros(t_ref.shape, t_ref.dtype)
    for a in range(3):
        for b in range(3):
            for p in range(levels):
                for q in range(levels):
                    tap = p - q + 1
                    if 0 <= tap < 3:
                        t_ref[a, b, p * cin : (p + 1) * cin, q * cout : (q + 1) * cout] = k_ref[
                            a, b, tap
                        ]


def halo_kernel(
    width, nlat, nlon, x_ref, p_ref, kin_ref, kmid_ref, kout_ref,
    o_ref, q_ref, tin_ref, tmid_ref, tout_ref, buf, inbox, *sems
):
    rows, cols = x_ref.shape[0], x_ref.shape[1]
    edge = (buf.shape[1] - cols) // 2
    j = lax.axis_index("lon")
    buf[...] = jnp.zeros(buf.shape, buf.dtype)
    buf[width : width + rows, edge : edge + cols, :] = x_ref[...]
    inbox[pl.ds(j, 1)] = p_ref[pl.ds(j, 1)]
    count = greet(nlat, nlon)
    band_into(kin_ref, tin_ref)
    band_into(kmid_ref, tmid_ref)
    band_into(kout_ref, tout_ref)
    trade(width, nlat, nlon, count, x_ref, p_ref, buf, inbox, *sems)
    o_ref[...] = buf[...]
    q_ref[...] = inbox[...]


def back_kernel(
    width, nlat, nlon, got_ref, high_ref, low_ref, slope_ref,
    grad_ref, o_ref, q_ref, buf, inbox, innov_ref, x_src, *sems
):
    rows, cols = x_src.shape[0], x_src.shape[1]
    edge = (buf.shape[1] - cols) // 2
    j = lax.axis_index("lon")
    buf[...] = jnp.zeros(buf.shape, buf.dtype)
    count = greet(nlat, nlon)
    observe_kernel(got_ref, high_ref, low_ref, innov_ref, grad_ref)
    grads = (grad_ref[...] * slope_ref[...]).astype(x_src.dtype).reshape(x_src.shape)
    x_src[...] = grads
    trade(width, nlat, nlon, count, x_src, innov_ref, buf, inbox, *sems)
    buf[width : width + rows, edge : edge + cols, :] = x_src[...]
    inbox[pl.ds(j, 1)] = innov_ref[pl.ds(j, 1)]
    o_ref[...] = buf[...]
    q_ref[...] = inbox[...]


def sem_scratch(nlon):
    return [
        pltpu.SemaphoreType.DMA((8,)),
        pltpu.SemaphoreType.DMA((8,)),
        pltpu.SemaphoreType.DMA((nlon,)),
        pltpu.SemaphoreType.DMA((nlon,)),
    ]


def exchange(block, width, payload, kernels):
    rows, cols, feats = block.shape
    edge = 16
    nlat = lax.axis_size("lat")
    nlon = lax.axis_size("lon")
    full = (rows + 2 * width, cols + 2 * edge, feats)
    vmem = pl.BlockSpec(memory_space=pltpu.VMEM)
    taps = [
        jax.ShapeDtypeStruct((3, 3, LEV * k.shape[3], LEV * k.shape[4]), k.dtype) for k in kernels
    ]
    out, got, *mats = pl.pallas_call(
        functools.partial(halo_kernel, width, nlat, nlon),
        out_shape=(
            jax.ShapeDtypeStruct(full, block.dtype),
            jax.ShapeDtypeStruct(payload.shape, payload.dtype),
            *taps,
        ),
        in_specs=[vmem] * 5,
        out_specs=(vmem,) * 5,
        scratch_shapes=[
            pltpu.VMEM(full, block.dtype),
            pltpu.VMEM(payload.shape, payload.dtype),
        ]
        + sem_scratch(nlon),
        compiler_params=pltpu.CompilerParams(collective_id=0, has_side_effects=True),
    )(block, payload, *kernels)
    return out[:, edge - width : edge + cols + width], got, mats


def observe_and_exchange(output, got, slope, width):
    rows, cols, feats = output.shape
    ncell = rows * cols
    edge = 16
    nlat = lax.axis_size("lat")
    nlon = lax.axis_size("lon")
    owners, nslot = got.shape[0], got.shape[2]
    o_hi, o_lo = split_bf16(output.reshape(ncell, feats).T)
    full = (rows + 2 * width, cols + 2 * edge, feats)
    vmem = pl.BlockSpec(memory_space=pltpu.VMEM)
    innov_shape = (owners, 1, nslot)
    grad, out, innovation = pl.pallas_call(
        functools.partial(back_kernel, width, nlat, nlon),
        out_shape=(
            jax.ShapeDtypeStruct((ncell, feats), jnp.float32),
            jax.ShapeDtypeStruct(full, jnp.bfloat16),
            jax.ShapeDtypeStruct(innov_shape, jnp.float32),
        ),
        in_specs=[vmem] * 4,
        out_specs=(vmem, vmem, vmem),
        scratch_shapes=[
            pltpu.VMEM(full, jnp.bfloat16),
            pltpu.VMEM(innov_shape, jnp.float32),
            pltpu.VMEM(innov_shape, jnp.float32),
            pltpu.VMEM((rows, cols, feats), jnp.bfloat16),
        ]
        + sem_scratch(nlon),
        compiler_params=pltpu.CompilerParams(collective_id=1, has_side_effects=True),
    )(got, o_hi, o_lo, slope.reshape(ncell, feats))
    grads = out[:, edge - width : edge + cols + width]
    return grad.reshape(rows, cols, feats), grads, innovation


def inside(field, tile_rows, halo):
    rows = field.shape[0]
    first = lax.axis_index("lat") * tile_rows - halo
    where = first + lax.broadcasted_iota(jnp.int32, (rows, 1, 1), 0)
    keep = (where >= 0) & (where < lax.axis_size("lat") * tile_rows)
    return jnp.where(keep, field, jnp.zeros_like(field))


def trim(field, width):
    return field[width : field.shape[0] - width, width : field.shape[1] - width]


def shards(
    state,
    kernel_in,
    kernel_mid,
    kernel_out,
    lift,
    obs_cells,
    obs_chan,
    obs_weights,
    obs_value,
    obs_count,
):
    rows, cols = (state.shape[0], state.shape[1])
    crows = rows // 2
    lift_full = block_diagonal(lift, LEV)
    packed = pack(obs_cells, obs_chan, obs_weights, obs_value, obs_count)
    padded, got, mats = exchange(state, 7, packed, (kernel_in, kernel_mid, kernel_out))
    mat_in, mat_mid, mat_out = [m.reshape(9, m.shape[2], m.shape[3]) for m in mats]
    pre_first = conv_valid(padded, mat_in, rows + 12, cols + 12)
    act_first = jax.nn.gelu(pre_first, approximate=True).astype(jnp.bfloat16)
    pooled = (block_sum(act_first.astype(jnp.float32)) * 0.25).astype(jnp.bfloat16)
    pooled = inside(pooled, crows, 3)
    pre_mid = conv_valid(pooled, mat_mid, crows + 4, cols // 2 + 4)
    act_mid = jax.nn.gelu(trim(pre_mid, 1), approximate=True).astype(jnp.bfloat16)
    lifted = jnp.einsum("ijg,gf->ijf", act_mid, lift_full, preferred_element_type=jnp.float32)
    merged = (trim(act_first, 5).astype(jnp.float32) + trim(widen(lifted), 1)).astype(jnp.bfloat16)
    merged = inside(merged, rows, 1)
    pre_last = conv_valid(merged, mat_out, rows, cols)
    slope_first = gelu_slope(trim(pre_first, 5))
    slope_mid = gelu_slope(pre_mid)
    output = state.astype(jnp.float32) + jax.nn.gelu(pre_last, approximate=True)
    grad_out, grads, innovation = observe_and_exchange(output, got, gelu_slope(pre_last), 5)
    innovation = innovation.reshape(obs_value.shape)
    grad_merged = adjoint_valid(grads, mat_out, rows + 8, cols + 8)
    grad_coarse = block_sum(grad_merged).astype(jnp.bfloat16)
    back_mid = jnp.einsum("ijf,gf->ijg", grad_coarse, lift_full, preferred_element_type=jnp.float32)
    grad_mid = inside((back_mid * slope_mid).astype(jnp.bfloat16), crows, 2)
    grad_pooled = adjoint_valid(grad_mid, mat_mid, crows + 2, cols // 2 + 2)
    grad_first = (
        (trim(grad_merged, 3) + trim(widen(grad_pooled), 1) * 0.25) * slope_first
    ).astype(jnp.bfloat16)
    grad_first = inside(grad_first, rows, 1)
    gradient = grad_out + adjoint_valid(grad_first, mat_in, rows, cols)
    return (gradient, innovation)


def solution(mesh):
    placed = (
        P("lat", "lon", None),
        P(),
        P(),
        P(),
        P(),
        P("lat", "lon", None, None),
        P("lat", "lon", None),
        P("lat", "lon", None, None),
        P("lat", "lon", None),
        P("lat", "lon"),
    )
    return jax.shard_map(
        shards,
        mesh=mesh,
        in_specs=placed,
        out_specs=(P("lat", "lon", None), P("lat", "lon", None)),
        check_vma=False,
    )
```

```python
import jax
import jax.numpy as jnp
from jax import lax
import functools

from jax.experimental import pallas as pl
from jax.experimental.pallas import tpu as pltpu
from jax.sharding import PartitionSpec as P

C = 32
C2 = 64
LEV = 4


def with_halo(block, sides, width, periodic):
    for axis, dim in sides:
        count = lax.axis_size(axis)
        forward = [(i, i + 1) for i in range(count - 1)]
        if periodic:
            forward.append((count - 1, 0))
        backward = [(target, source) for source, target in forward]
        low = lax.ppermute(
            lax.slice_in_dim(block, block.shape[dim] - width, None, axis=dim), axis, forward
        )
        high = lax.ppermute(lax.slice_in_dim(block, 0, width, axis=dim), axis, backward)
        block = jnp.concatenate([low, block, high], axis=dim)
    return block


def banded(kernel, levels):
    zero = jnp.zeros(kernel.shape[:2] + kernel.shape[3:], kernel.dtype)
    rows = []
    for p in range(levels):
        blocks = [kernel[:, :, p - q + 1] if 0 <= p - q + 1 < 3 else zero for q in range(levels)]
        rows.append(jnp.concatenate(blocks, axis=-1))
    full = jnp.concatenate(rows, axis=-2)
    return full.reshape(9, full.shape[2], full.shape[3])


def block_diagonal(matrix, levels):
    zero = jnp.zeros_like(matrix)
    rows = [
        jnp.concatenate([matrix if p == q else zero for q in range(levels)], axis=1)
        for p in range(levels)
    ]
    return jnp.concatenate(rows, axis=0)


def gelu_slope(value):
    inner = 0.7978845608 * (value + 0.044715 * value**3)
    tval = jnp.tanh(inner)
    return 0.5 * (1.0 + tval) + 0.5 * value * (1.0 - tval * tval) * 0.7978845608 * (
        1.0 + 0.134145 * value * value
    )


def extend(field):
    wide = with_halo(field, (("lon", 1),), 1, True)
    return with_halo(wide, (("lat", 0),), 1, False)


def conv_valid(padded, matrices, rows, cols):
    taps = matrices.reshape(3, 3, matrices.shape[1], matrices.shape[2])
    out = lax.conv_general_dilated(
        padded[None],
        taps,
        (1, 1),
        "VALID",
        dimension_numbers=("NHWC", "HWIO", "NHWC"),
        preferred_element_type=jnp.float32,
    )
    return out[0]


def adjoint_valid(padded, matrices, rows, cols):
    taps = matrices.reshape(3, 3, matrices.shape[1], matrices.shape[2])
    taps = jnp.swapaxes(taps[::-1, ::-1], 2, 3)
    out = lax.conv_general_dilated(
        padded[None],
        taps,
        (1, 1),
        "VALID",
        dimension_numbers=("NHWC", "HWIO", "NHWC"),
        preferred_element_type=jnp.float32,
    )
    return out[0]


def convolve(field, matrices):
    return conv_valid(extend(field), matrices, field.shape[0], field.shape[1])


def convolve_adjoint(grads, matrices):
    return adjoint_valid(extend(grads), matrices, grads.shape[0], grads.shape[1])


def widen(coarse):
    rows, cols, feats = coarse.shape
    return jnp.broadcast_to(coarse[:, None, :, None, :], (rows, 2, cols, 2, feats)).reshape(
        rows * 2, cols * 2, feats
    )


def block_sum(fine):
    rows, cols, feats = fine.shape
    return fine.reshape(rows // 2, 2, cols // 2, 2, feats).sum(axis=(1, 3))


def split_bf16(value):
    high = lax.reduce_precision(value, exponent_bits=8, mantissa_bits=7)
    return high.astype(jnp.bfloat16), (value - high).astype(jnp.bfloat16)


def observe_kernel(got_ref, high_ref, low_ref, innov_ref, grad_ref):
    fields, nslot = got_ref.shape[1], got_ref.shape[2]
    feats, ncell = high_ref.shape
    cell_ids = lax.broadcasted_iota(jnp.int32, (ncell, nslot), 0).astype(jnp.float32)
    feat_ids = lax.broadcasted_iota(jnp.int32, (feats, nslot), 0).astype(jnp.float32)
    high = high_ref[...]
    low = low_ref[...]
    both = jnp.concatenate([high, low], axis=0)
    grad_ref[...] = jnp.zeros(grad_ref.shape, jnp.float32)
    trans = (((1,), (1,)), ((), ()))

    def body(owner, carry):
        block = got_ref[owner]
        table = jnp.zeros((ncell, nslot), jnp.float32)
        for j in range(4):
            table = table + jnp.where(
                cell_ids == block[j : j + 1, :], block[5 + j : 6 + j, :], 0.0
            )
        t_hi = table.astype(jnp.bfloat16)
        t_lo = (table - t_hi.astype(jnp.float32)).astype(jnp.bfloat16)
        two = jnp.dot(both, t_hi, preferred_element_type=jnp.float32)
        picked = two[:feats] + two[feats:] + jnp.dot(high, t_lo, preferred_element_type=jnp.float32)
        pick = feat_ids == block[4:5, :]
        innov = jnp.sum(jnp.where(pick, picked, 0.0), axis=0, keepdims=True) - block[9:10, :]
        innov_ref[owner] = innov
        spread = jnp.where(pick, innov, 0.0)
        s_hi = spread.astype(jnp.bfloat16)
        s_lo = (spread - s_hi.astype(jnp.float32)).astype(jnp.bfloat16)
        sums = lax.dot_general(
            t_hi, jnp.concatenate([s_hi, s_lo], axis=0), trans, preferred_element_type=jnp.float32
        )
        grad_ref[...] += (
            sums[:, :feats]
            + sums[:, feats:]
            + lax.dot_general(t_lo, s_hi, trans, preferred_element_type=jnp.float32)
        )
        return carry

    lax.fori_loop(0, got_ref.shape[0], body, 0)


def pack(obs_cells, obs_chan, obs_weights, obs_value, obs_count):
    slots = lax.broadcasted_iota(jnp.int32, obs_chan.shape, 2)
    live = (slots < obs_count[:, :, None]).astype(jnp.float32)
    weights = obs_weights * live[..., None]
    values = obs_value * live
    packed = jnp.concatenate(
        [
            jnp.swapaxes(obs_cells, 2, 3).astype(jnp.float32),
            obs_chan[:, :, None, :].astype(jnp.float32),
            jnp.swapaxes(weights, 2, 3),
            values[:, :, None, :],
        ],
        axis=2,
    )
    return packed.reshape(packed.shape[1:])


def observe(output, got):
    rows, cols, feats = output.shape
    ncell = rows * cols
    owners, nslot = got.shape[0], got.shape[2]
    o_hi, o_lo = split_bf16(output.reshape(ncell, feats).T)
    innov, grad = pl.pallas_call(
        observe_kernel,
        out_shape=(
            jax.ShapeDtypeStruct((owners, 1, nslot), jnp.float32),
            jax.ShapeDtypeStruct((ncell, feats), jnp.float32),
        ),
    )(got, o_hi, o_lo)
    return grad.reshape(rows, cols, feats), innov


def greet(nlat, nlon):
    i = lax.axis_index("lat")
    j = lax.axis_index("lon")
    has = {-1: i > 0, 0: i >= 0, 1: i < nlat - 1}
    mesh = pl.DeviceIdType.MESH
    barrier = pltpu.get_barrier_semaphore()
    for a in (-1, 1):
        for b in (-1, 0, 1):

            @pl.when(has[a])
            def _():
                pl.semaphore_signal(
                    barrier, inc=1, device_id=((i + a) % nlat, (j + b) % nlon), device_id_type=mesh
                )

    for t in range(nlon):

        @pl.when(t != j)
        def _():
            pl.semaphore_signal(barrier, inc=1, device_id=(i, t), device_id_type=mesh)

    return (nlon - 1) + 3 * has[-1].astype(jnp.int32) + 3 * has[1].astype(jnp.int32)


def trade(width, nlat, nlon, count, x_ref, p_ref, buf, inbox, send_sem, recv_sem, p_send, p_recv):
    rows, cols = x_ref.shape[0], x_ref.shape[1]
    edge = (buf.shape[1] - cols) // 2
    i = lax.axis_index("lat")
    j = lax.axis_index("lon")
    has = {-1: i > 0, 0: i >= 0, 1: i < nlat - 1}
    mesh = pl.DeviceIdType.MESH
    dirs = [(a, b) for a in (-1, 0, 1) for b in (-1, 0, 1) if (a, b) != (0, 0)]
    pl.semaphore_wait(pltpu.get_barrier_semaphore(), count)
    src_rows = {1: pl.ds(rows - width, width), -1: pl.ds(0, width), 0: pl.ds(0, rows)}
    dst_rows = {1: pl.ds(0, width), -1: pl.ds(width + rows, width), 0: pl.ds(width, rows)}
    src_cols = {1: pl.ds(cols - edge, edge), -1: pl.ds(0, edge), 0: pl.ds(0, cols)}
    dst_cols = {1: pl.ds(0, edge), -1: pl.ds(edge + cols, edge), 0: pl.ds(edge, cols)}
    copies = []
    for k, (a, b) in enumerate(dirs):
        copy = pltpu.make_async_remote_copy(
            src_ref=x_ref.at[src_rows[a], src_cols[b]],
            dst_ref=buf.at[dst_rows[a], dst_cols[b]],
            send_sem=send_sem.at[k],
            recv_sem=recv_sem.at[k],
            device_id=((i + a) % nlat, (j + b) % nlon),
            device_id_type=mesh,
        )
        copies.append((a, copy))
        pl.when(has[a])(copy.start)
    sends = []
    for t in range(nlon):
        copy = pltpu.make_async_remote_copy(
            src_ref=p_ref.at[pl.ds(t, 1)],
            dst_ref=inbox.at[pl.ds(j, 1)],
            send_sem=p_send.at[t],
            recv_sem=p_recv.at[j],
            device_id=(i, t),
            device_id_type=mesh,
        )
        sends.append(copy)
        pl.when(t != j)(copy.start)
    for a, copy in copies:
        pl.when(has[a])(copy.wait_send)
        pl.when(has[-a])(copy.wait_recv)
    for t in range(nlon):
        arrival = pltpu.make_async_remote_copy(
            src_ref=p_ref.at[pl.ds(t, 1)],
            dst_ref=inbox.at[pl.ds(t, 1)],
            send_sem=p_send.at[t],
            recv_sem=p_recv.at[t],
            device_id=(i, t),
            device_id_type=mesh,
        )
        pl.when(t != j)(sends[t].wait_send)
        pl.when(t != j)(arrival.wait_recv)


def halo_kernel(width, nlat, nlon, x_ref, p_ref, o_ref, q_ref, buf, inbox, *sems):
    rows, cols = x_ref.shape[0], x_ref.shape[1]
    edge = (buf.shape[1] - cols) // 2
    j = lax.axis_index("lon")
    buf[...] = jnp.zeros(buf.shape, buf.dtype)
    buf[width : width + rows, edge : edge + cols, :] = x_ref[...]
    inbox[pl.ds(j, 1)] = p_ref[pl.ds(j, 1)]
    count = greet(nlat, nlon)
    trade(width, nlat, nlon, count, x_ref, p_ref, buf, inbox, *sems)
    o_ref[...] = buf[...]
    q_ref[...] = inbox[...]


def back_kernel(
    width, nlat, nlon, got_ref, high_ref, low_ref, slope_ref,
    grad_ref, o_ref, q_ref, buf, inbox, innov_ref, x_src, *sems
):
    rows, cols = x_src.shape[0], x_src.shape[1]
    edge = (buf.shape[1] - cols) // 2
    j = lax.axis_index("lon")
    buf[...] = jnp.zeros(buf.shape, buf.dtype)
    count = greet(nlat, nlon)
    observe_kernel(got_ref, high_ref, low_ref, innov_ref, grad_ref)
    grads = (grad_ref[...] * gelu_slope(slope_ref[...])).astype(x_src.dtype).reshape(x_src.shape)
    x_src[...] = grads
    trade(width, nlat, nlon, count, x_src, innov_ref, buf, inbox, *sems)
    buf[width : width + rows, edge : edge + cols, :] = x_src[...]
    inbox[pl.ds(j, 1)] = innov_ref[pl.ds(j, 1)]
    o_ref[...] = buf[...]
    q_ref[...] = inbox[...]


def sem_scratch(nlon):
    return [
        pltpu.SemaphoreType.DMA((8,)),
        pltpu.SemaphoreType.DMA((8,)),
        pltpu.SemaphoreType.DMA((nlon,)),
        pltpu.SemaphoreType.DMA((nlon,)),
    ]


def exchange(block, width, payload):
    rows, cols, feats = block.shape
    edge = 16
    nlat = lax.axis_size("lat")
    nlon = lax.axis_size("lon")
    full = (rows + 2 * width, cols + 2 * edge, feats)
    vmem = pl.BlockSpec(memory_space=pltpu.VMEM)
    out, got = pl.pallas_call(
        functools.partial(halo_kernel, width, nlat, nlon),
        out_shape=(
            jax.ShapeDtypeStruct(full, block.dtype),
            jax.ShapeDtypeStruct(payload.shape, payload.dtype),
        ),
        in_specs=[vmem, vmem],
        out_specs=(vmem, vmem),
        scratch_shapes=[
            pltpu.VMEM(full, block.dtype),
            pltpu.VMEM(payload.shape, payload.dtype),
        ]
        + sem_scratch(nlon),
        compiler_params=pltpu.CompilerParams(collective_id=0, has_side_effects=True),
    )(block, payload)
    return out[:, edge - width : edge + cols + width], got


def observe_and_exchange(output, got, slope, width):
    rows, cols, feats = output.shape
    ncell = rows * cols
    edge = 16
    nlat = lax.axis_size("lat")
    nlon = lax.axis_size("lon")
    owners, nslot = got.shape[0], got.shape[2]
    o_hi, o_lo = split_bf16(output.reshape(ncell, feats).T)
    full = (rows + 2 * width, cols + 2 * edge, feats)
    vmem = pl.BlockSpec(memory_space=pltpu.VMEM)
    innov_shape = (owners, 1, nslot)
    grad, out, innovation = pl.pallas_call(
        functools.partial(back_kernel, width, nlat, nlon),
        out_shape=(
            jax.ShapeDtypeStruct((ncell, feats), jnp.float32),
            jax.ShapeDtypeStruct(full, jnp.bfloat16),
            jax.ShapeDtypeStruct(innov_shape, jnp.float32),
        ),
        in_specs=[vmem] * 4,
        out_specs=(vmem, vmem, vmem),
        scratch_shapes=[
            pltpu.VMEM(full, jnp.bfloat16),
            pltpu.VMEM(innov_shape, jnp.float32),
            pltpu.VMEM(innov_shape, jnp.float32),
            pltpu.VMEM((rows, cols, feats), jnp.bfloat16),
        ]
        + sem_scratch(nlon),
        compiler_params=pltpu.CompilerParams(collective_id=1, has_side_effects=True),
    )(got, o_hi, o_lo, slope.reshape(ncell, feats))
    grads = out[:, edge - width : edge + cols + width]
    return grad.reshape(rows, cols, feats), grads, innovation


def inside(field, tile_rows, halo):
    rows = field.shape[0]
    first = lax.axis_index("lat") * tile_rows - halo
    where = first + lax.broadcasted_iota(jnp.int32, (rows, 1, 1), 0)
    keep = (where >= 0) & (where < lax.axis_size("lat") * tile_rows)
    return jnp.where(keep, field, jnp.zeros_like(field))


def trim(field, width):
    return field[width : field.shape[0] - width, width : field.shape[1] - width]


def shards(
    state,
    kernel_in,
    kernel_mid,
    kernel_out,
    lift,
    obs_cells,
    obs_chan,
    obs_weights,
    obs_value,
    obs_count,
):
    rows, cols = (state.shape[0], state.shape[1])
    crows = rows // 2
    mat_in = banded(kernel_in, LEV)
    mat_mid = banded(kernel_mid, LEV)
    mat_out = banded(kernel_out, LEV)
    lift_full = block_diagonal(lift, LEV)
    packed = pack(obs_cells, obs_chan, obs_weights, obs_value, obs_count)
    padded, got = exchange(state, 7, packed)
    pre_first = conv_valid(padded, mat_in, rows + 12, cols + 12)
    act_first = jax.nn.gelu(pre_first, approximate=True).astype(jnp.bfloat16)
    pooled = (block_sum(act_first.astype(jnp.float32)) * 0.25).astype(jnp.bfloat16)
    pooled = inside(pooled, crows, 3)
    pre_mid = conv_valid(pooled, mat_mid, crows + 4, cols // 2 + 4)
    act_mid = jax.nn.gelu(trim(pre_mid, 1), approximate=True).astype(jnp.bfloat16)
    lifted = jnp.einsum("ijg,gf->ijf", act_mid, lift_full, preferred_element_type=jnp.float32)
    merged = (trim(act_first, 5).astype(jnp.float32) + trim(widen(lifted), 1)).astype(jnp.bfloat16)
    merged = inside(merged, rows, 1)
    pre_last = conv_valid(merged, mat_out, rows, cols)
    slope_first = gelu_slope(trim(pre_first, 5))
    slope_mid = gelu_slope(pre_mid)
    output = state.astype(jnp.float32) + jax.nn.gelu(pre_last, approximate=True)
    grad_out, grads, innovation = observe_and_exchange(output, got, pre_last, 5)
    innovation = innovation.reshape(obs_value.shape)
    grad_merged = adjoint_valid(grads, mat_out, rows + 8, cols + 8)
    grad_coarse = block_sum(grad_merged).astype(jnp.bfloat16)
    back_mid = jnp.einsum("ijf,gf->ijg", grad_coarse, lift_full, preferred_element_type=jnp.float32)
    grad_mid = inside((back_mid * slope_mid).astype(jnp.bfloat16), crows, 2)
    grad_pooled = adjoint_valid(grad_mid, mat_mid, crows + 2, cols // 2 + 2)
    grad_first = (
        (trim(grad_merged, 3) + trim(widen(grad_pooled), 1) * 0.25) * slope_first
    ).astype(jnp.bfloat16)
    grad_first = inside(grad_first, rows, 1)
    gradient = grad_out + adjoint_valid(grad_first, mat_in, rows, cols)
    return (gradient, innovation)


def solution(mesh):
    placed = (
        P("lat", "lon", None),
        P(),
        P(),
        P(),
        P(),
        P("lat", "lon", None, None),
        P("lat", "lon", None),
        P("lat", "lon", None, None),
        P("lat", "lon", None),
        P("lat", "lon"),
    )
    return jax.shard_map(
        shards,
        mesh=mesh,
        in_specs=placed,
        out_specs=(P("lat", "lon", None), P("lat", "lon", None)),
        check_vma=False,
    )
```

```python
import jax
import jax.numpy as jnp
from jax import lax
import functools

from jax.experimental import pallas as pl
from jax.experimental.pallas import tpu as pltpu
from jax.sharding import PartitionSpec as P

C = 32
C2 = 64
LEV = 4


def with_halo(block, sides, width, periodic):
    for axis, dim in sides:
        count = lax.axis_size(axis)
        forward = [(i, i + 1) for i in range(count - 1)]
        if periodic:
            forward.append((count - 1, 0))
        backward = [(target, source) for source, target in forward]
        low = lax.ppermute(
            lax.slice_in_dim(block, block.shape[dim] - width, None, axis=dim), axis, forward
        )
        high = lax.ppermute(lax.slice_in_dim(block, 0, width, axis=dim), axis, backward)
        block = jnp.concatenate([low, block, high], axis=dim)
    return block


def banded(kernel, levels):
    zero = jnp.zeros(kernel.shape[:2] + kernel.shape[3:], kernel.dtype)
    rows = []
    for p in range(levels):
        blocks = [kernel[:, :, p - q + 1] if 0 <= p - q + 1 < 3 else zero for q in range(levels)]
        rows.append(jnp.concatenate(blocks, axis=-1))
    full = jnp.concatenate(rows, axis=-2)
    return full.reshape(9, full.shape[2], full.shape[3])


def block_diagonal(matrix, levels):
    zero = jnp.zeros_like(matrix)
    rows = [
        jnp.concatenate([matrix if p == q else zero for q in range(levels)], axis=1)
        for p in range(levels)
    ]
    return jnp.concatenate(rows, axis=0)


def gelu_slope(value):
    inner = 0.7978845608 * (value + 0.044715 * value**3)
    tval = jnp.tanh(inner)
    return 0.5 * (1.0 + tval) + 0.5 * value * (1.0 - tval * tval) * 0.7978845608 * (
        1.0 + 0.134145 * value * value
    )


def extend(field):
    wide = with_halo(field, (("lon", 1),), 1, True)
    return with_halo(wide, (("lat", 0),), 1, False)


def conv_valid(padded, matrices, rows, cols):
    taps = matrices.reshape(3, 3, matrices.shape[1], matrices.shape[2])
    out = lax.conv_general_dilated(
        padded[None],
        taps,
        (1, 1),
        "VALID",
        dimension_numbers=("NHWC", "HWIO", "NHWC"),
        preferred_element_type=jnp.float32,
    )
    return out[0]


def adjoint_valid(padded, matrices, rows, cols):
    taps = matrices.reshape(3, 3, matrices.shape[1], matrices.shape[2])
    taps = jnp.swapaxes(taps[::-1, ::-1], 2, 3)
    out = lax.conv_general_dilated(
        padded[None],
        taps,
        (1, 1),
        "VALID",
        dimension_numbers=("NHWC", "HWIO", "NHWC"),
        preferred_element_type=jnp.float32,
    )
    return out[0]


def convolve(field, matrices):
    return conv_valid(extend(field), matrices, field.shape[0], field.shape[1])


def convolve_adjoint(grads, matrices):
    return adjoint_valid(extend(grads), matrices, grads.shape[0], grads.shape[1])


def widen(coarse):
    rows, cols, feats = coarse.shape
    return jnp.broadcast_to(coarse[:, None, :, None, :], (rows, 2, cols, 2, feats)).reshape(
        rows * 2, cols * 2, feats
    )


def block_sum(fine):
    rows, cols, feats = fine.shape
    return fine.reshape(rows // 2, 2, cols // 2, 2, feats).sum(axis=(1, 3))


def split_bf16(value):
    high = lax.reduce_precision(value, exponent_bits=8, mantissa_bits=7)
    return high.astype(jnp.bfloat16), (value - high).astype(jnp.bfloat16)


def observe_kernel(got_ref, high_ref, innov_ref, grad_ref):
    fields, nslot = got_ref.shape[1], got_ref.shape[2]
    ncell, feats = high_ref.shape
    cell_ids = lax.broadcasted_iota(jnp.int32, (ncell, nslot), 0).astype(jnp.float32)
    feat_ids = lax.broadcasted_iota(jnp.int32, (feats, nslot), 0).astype(jnp.float32)
    value = high_ref[...].T
    high = value.astype(jnp.bfloat16)
    low = (value - high.astype(jnp.float32)).astype(jnp.bfloat16)
    both = jnp.concatenate([high, low], axis=0)
    grad_ref[...] = jnp.zeros(grad_ref.shape, jnp.float32)
    trans = (((1,), (1,)), ((), ()))

    def body(owner, carry):
        block = got_ref[owner]
        table = jnp.zeros((ncell, nslot), jnp.float32)
        for j in range(4):
            table = table + jnp.where(
                cell_ids == block[j : j + 1, :], block[5 + j : 6 + j, :], 0.0
            )
        t_hi = table.astype(jnp.bfloat16)
        t_lo = (table - t_hi.astype(jnp.float32)).astype(jnp.bfloat16)
        two = jnp.dot(both, t_hi, preferred_element_type=jnp.float32)
        picked = two[:feats] + two[feats:] + jnp.dot(high, t_lo, preferred_element_type=jnp.float32)
        pick = feat_ids == block[4:5, :]
        innov = jnp.sum(jnp.where(pick, picked, 0.0), axis=0, keepdims=True) - block[9:10, :]
        innov_ref[owner] = innov
        spread = jnp.where(pick, innov, 0.0)
        s_hi = spread.astype(jnp.bfloat16)
        s_lo = (spread - s_hi.astype(jnp.float32)).astype(jnp.bfloat16)
        sums = lax.dot_general(
            t_hi, jnp.concatenate([s_hi, s_lo], axis=0), trans, preferred_element_type=jnp.float32
        )
        grad_ref[...] += (
            sums[:, :feats]
            + sums[:, feats:]
            + lax.dot_general(t_lo, s_hi, trans, preferred_element_type=jnp.float32)
        )
        return carry

    lax.fori_loop(0, got_ref.shape[0], body, 0)


def pack(obs_cells, obs_chan, obs_weights, obs_value, obs_count):
    slots = lax.broadcasted_iota(jnp.int32, obs_chan.shape, 2)
    live = (slots < obs_count[:, :, None]).astype(jnp.float32)
    weights = obs_weights * live[..., None]
    values = obs_value * live
    packed = jnp.concatenate(
        [
            jnp.swapaxes(obs_cells, 2, 3).astype(jnp.float32),
            obs_chan[:, :, None, :].astype(jnp.float32),
            jnp.swapaxes(weights, 2, 3),
            values[:, :, None, :],
        ],
        axis=2,
    )
    return packed.reshape(packed.shape[1:])


def observe(output, got):
    rows, cols, feats = output.shape
    ncell = rows * cols
    owners, nslot = got.shape[0], got.shape[2]
    o_hi, o_lo = split_bf16(output.reshape(ncell, feats).T)
    innov, grad = pl.pallas_call(
        observe_kernel,
        out_shape=(
            jax.ShapeDtypeStruct((owners, 1, nslot), jnp.float32),
            jax.ShapeDtypeStruct((ncell, feats), jnp.float32),
        ),
    )(got, o_hi, o_lo)
    return grad.reshape(rows, cols, feats), innov


def greet(nlat, nlon):
    i = lax.axis_index("lat")
    j = lax.axis_index("lon")
    has = {-1: i > 0, 0: i >= 0, 1: i < nlat - 1}
    mesh = pl.DeviceIdType.MESH
    barrier = pltpu.get_barrier_semaphore()
    for a in (-1, 1):
        for b in (-1, 0, 1):

            @pl.when(has[a])
            def _():
                pl.semaphore_signal(
                    barrier, inc=1, device_id=((i + a) % nlat, (j + b) % nlon), device_id_type=mesh
                )

    for t in range(nlon):

        @pl.when(t != j)
        def _():
            pl.semaphore_signal(barrier, inc=1, device_id=(i, t), device_id_type=mesh)

    return (nlon - 1) + 3 * has[-1].astype(jnp.int32) + 3 * has[1].astype(jnp.int32)


def trade(width, nlat, nlon, count, x_ref, p_ref, buf, inbox, send_sem, recv_sem, p_send, p_recv):
    rows, cols = x_ref.shape[0], x_ref.shape[1]
    edge = (buf.shape[1] - cols) // 2
    i = lax.axis_index("lat")
    j = lax.axis_index("lon")
    has = {-1: i > 0, 0: i >= 0, 1: i < nlat - 1}
    mesh = pl.DeviceIdType.MESH
    dirs = [(a, b) for a in (-1, 0, 1) for b in (-1, 0, 1) if (a, b) != (0, 0)]
    pl.semaphore_wait(pltpu.get_barrier_semaphore(), count)
    src_rows = {1: pl.ds(rows - width, width), -1: pl.ds(0, width), 0: pl.ds(0, rows)}
    dst_rows = {1: pl.ds(0, width), -1: pl.ds(width + rows, width), 0: pl.ds(width, rows)}
    src_cols = {1: pl.ds(cols - edge, edge), -1: pl.ds(0, edge), 0: pl.ds(0, cols)}
    dst_cols = {1: pl.ds(0, edge), -1: pl.ds(edge + cols, edge), 0: pl.ds(edge, cols)}
    copies = []
    for k, (a, b) in enumerate(dirs):
        copy = pltpu.make_async_remote_copy(
            src_ref=x_ref.at[src_rows[a], src_cols[b]],
            dst_ref=buf.at[dst_rows[a], dst_cols[b]],
            send_sem=send_sem.at[k],
            recv_sem=recv_sem.at[k],
            device_id=((i + a) % nlat, (j + b) % nlon),
            device_id_type=mesh,
        )
        copies.append((a, copy))
        pl.when(has[a])(copy.start)
    sends = []
    for t in range(nlon):
        copy = pltpu.make_async_remote_copy(
            src_ref=p_ref.at[pl.ds(t, 1)],
            dst_ref=inbox.at[pl.ds(j, 1)],
            send_sem=p_send.at[t],
            recv_sem=p_recv.at[j],
            device_id=(i, t),
            device_id_type=mesh,
        )
        sends.append(copy)
        pl.when(t != j)(copy.start)
    for a, copy in copies:
        pl.when(has[a])(copy.wait_send)
        pl.when(has[-a])(copy.wait_recv)
    for t in range(nlon):
        arrival = pltpu.make_async_remote_copy(
            src_ref=p_ref.at[pl.ds(t, 1)],
            dst_ref=inbox.at[pl.ds(t, 1)],
            send_sem=p_send.at[t],
            recv_sem=p_recv.at[t],
            device_id=(i, t),
            device_id_type=mesh,
        )
        pl.when(t != j)(sends[t].wait_send)
        pl.when(t != j)(arrival.wait_recv)


def halo_kernel(width, nlat, nlon, x_ref, p_ref, o_ref, q_ref, buf, inbox, *sems):
    rows, cols = x_ref.shape[0], x_ref.shape[1]
    edge = (buf.shape[1] - cols) // 2
    j = lax.axis_index("lon")
    buf[...] = jnp.zeros(buf.shape, buf.dtype)
    buf[width : width + rows, edge : edge + cols, :] = x_ref[...]
    inbox[pl.ds(j, 1)] = p_ref[pl.ds(j, 1)]
    count = greet(nlat, nlon)
    trade(width, nlat, nlon, count, x_ref, p_ref, buf, inbox, *sems)
    o_ref[...] = buf[...]
    q_ref[...] = inbox[...]


def back_kernel(
    width, nlat, nlon, got_ref, high_ref, slope_ref,
    grad_ref, o_ref, q_ref, buf, inbox, innov_ref, x_src, *sems
):
    rows, cols = x_src.shape[0], x_src.shape[1]
    edge = (buf.shape[1] - cols) // 2
    j = lax.axis_index("lon")
    buf[...] = jnp.zeros(buf.shape, buf.dtype)
    count = greet(nlat, nlon)
    observe_kernel(got_ref, high_ref, innov_ref, grad_ref)
    grads = (grad_ref[...] * gelu_slope(slope_ref[...])).astype(x_src.dtype).reshape(x_src.shape)
    x_src[...] = grads
    trade(width, nlat, nlon, count, x_src, innov_ref, buf, inbox, *sems)
    buf[width : width + rows, edge : edge + cols, :] = x_src[...]
    inbox[pl.ds(j, 1)] = innov_ref[pl.ds(j, 1)]
    o_ref[...] = buf[...]
    q_ref[...] = inbox[...]


def sem_scratch(nlon):
    return [
        pltpu.SemaphoreType.DMA((8,)),
        pltpu.SemaphoreType.DMA((8,)),
        pltpu.SemaphoreType.DMA((nlon,)),
        pltpu.SemaphoreType.DMA((nlon,)),
    ]


def exchange(block, width, payload):
    rows, cols, feats = block.shape
    edge = 16
    nlat = lax.axis_size("lat")
    nlon = lax.axis_size("lon")
    full = (rows + 2 * width, cols + 2 * edge, feats)
    vmem = pl.BlockSpec(memory_space=pltpu.VMEM)
    out, got = pl.pallas_call(
        functools.partial(halo_kernel, width, nlat, nlon),
        out_shape=(
            jax.ShapeDtypeStruct(full, block.dtype),
            jax.ShapeDtypeStruct(payload.shape, payload.dtype),
        ),
        in_specs=[vmem, vmem],
        out_specs=(vmem, vmem),
        scratch_shapes=[
            pltpu.VMEM(full, block.dtype),
            pltpu.VMEM(payload.shape, payload.dtype),
        ]
        + sem_scratch(nlon),
        compiler_params=pltpu.CompilerParams(collective_id=0, has_side_effects=True),
    )(block, payload)
    return out[:, edge - width : edge + cols + width], got


def observe_and_exchange(output, got, slope, width):
    rows, cols, feats = output.shape
    ncell = rows * cols
    edge = 16
    nlat = lax.axis_size("lat")
    nlon = lax.axis_size("lon")
    owners, nslot = got.shape[0], got.shape[2]
    full = (rows + 2 * width, cols + 2 * edge, feats)
    vmem = pl.BlockSpec(memory_space=pltpu.VMEM)
    innov_shape = (owners, 1, nslot)
    grad, out, innovation = pl.pallas_call(
        functools.partial(back_kernel, width, nlat, nlon),
        out_shape=(
            jax.ShapeDtypeStruct((ncell, feats), jnp.float32),
            jax.ShapeDtypeStruct(full, jnp.bfloat16),
            jax.ShapeDtypeStruct(innov_shape, jnp.float32),
        ),
        in_specs=[vmem] * 3,
        out_specs=(vmem, vmem, vmem),
        scratch_shapes=[
            pltpu.VMEM(full, jnp.bfloat16),
            pltpu.VMEM(innov_shape, jnp.float32),
            pltpu.VMEM(innov_shape, jnp.float32),
            pltpu.VMEM((rows, cols, feats), jnp.bfloat16),
        ]
        + sem_scratch(nlon),
        compiler_params=pltpu.CompilerParams(collective_id=1, has_side_effects=True),
    )(got, output.reshape(ncell, feats), slope.reshape(ncell, feats))
    grads = out[:, edge - width : edge + cols + width]
    return grad.reshape(rows, cols, feats), grads, innovation


def inside(field, tile_rows, halo):
    rows = field.shape[0]
    first = lax.axis_index("lat") * tile_rows - halo
    where = first + lax.broadcasted_iota(jnp.int32, (rows, 1, 1), 0)
    keep = (where >= 0) & (where < lax.axis_size("lat") * tile_rows)
    return jnp.where(keep, field, jnp.zeros_like(field))


def trim(field, width):
    return field[width : field.shape[0] - width, width : field.shape[1] - width]


def shards(
    state,
    kernel_in,
    kernel_mid,
    kernel_out,
    lift,
    obs_cells,
    obs_chan,
    obs_weights,
    obs_value,
    obs_count,
):
    rows, cols = (state.shape[0], state.shape[1])
    crows = rows // 2
    mat_in = banded(kernel_in, LEV)
    mat_mid = banded(kernel_mid, LEV)
    mat_out = banded(kernel_out, LEV)
    lift_full = block_diagonal(lift, LEV)
    packed = pack(obs_cells, obs_chan, obs_weights, obs_value, obs_count)
    padded, got = exchange(state, 7, packed)
    pre_first = conv_valid(padded, mat_in, rows + 12, cols + 12)
    act_first = jax.nn.gelu(pre_first, approximate=True).astype(jnp.bfloat16)
    pooled = (block_sum(act_first.astype(jnp.float32)) * 0.25).astype(jnp.bfloat16)
    pooled = inside(pooled, crows, 3)
    pre_mid = conv_valid(pooled, mat_mid, crows + 4, cols // 2 + 4)
    act_mid = jax.nn.gelu(trim(pre_mid, 1), approximate=True).astype(jnp.bfloat16)
    lifted = jnp.einsum("ijg,gf->ijf", act_mid, lift_full, preferred_element_type=jnp.float32)
    merged = (trim(act_first, 5).astype(jnp.float32) + trim(widen(lifted), 1)).astype(jnp.bfloat16)
    merged = inside(merged, rows, 1)
    pre_last = conv_valid(merged, mat_out, rows, cols)
    slope_first = gelu_slope(trim(pre_first, 5))
    slope_mid = gelu_slope(pre_mid)
    output = state.astype(jnp.float32) + jax.nn.gelu(pre_last, approximate=True)
    grad_out, grads, innovation = observe_and_exchange(output, got, pre_last, 5)
    innovation = innovation.reshape(obs_value.shape)
    grad_merged = adjoint_valid(grads, mat_out, rows + 8, cols + 8)
    grad_coarse = block_sum(grad_merged).astype(jnp.bfloat16)
    back_mid = jnp.einsum("ijf,gf->ijg", grad_coarse, lift_full, preferred_element_type=jnp.float32)
    grad_mid = inside((back_mid * slope_mid).astype(jnp.bfloat16), crows, 2)
    grad_pooled = adjoint_valid(grad_mid, mat_mid, crows + 2, cols // 2 + 2)
    grad_first = (
        (trim(grad_merged, 3) + trim(widen(grad_pooled), 1) * 0.25) * slope_first
    ).astype(jnp.bfloat16)
    grad_first = inside(grad_first, rows, 1)
    gradient = grad_out + adjoint_valid(grad_first, mat_in, rows, cols)
    return (gradient, innovation)


def solution(mesh):
    placed = (
        P("lat", "lon", None),
        P(),
        P(),
        P(),
        P(),
        P("lat", "lon", None, None),
        P("lat", "lon", None),
        P("lat", "lon", None, None),
        P("lat", "lon", None),
        P("lat", "lon"),
    )
    return jax.shard_map(
        shards,
        mesh=mesh,
        in_specs=placed,
        out_specs=(P("lat", "lon", None), P("lat", "lon", None)),
        check_vma=False,
    )
```

```python
import jax
import jax.numpy as jnp
from jax import lax
import functools

from jax.experimental import pallas as pl
from jax.experimental.pallas import tpu as pltpu
from jax.sharding import PartitionSpec as P

C = 32
C2 = 64
LEV = 4


def with_halo(block, sides, width, periodic):
    for axis, dim in sides:
        count = lax.axis_size(axis)
        forward = [(i, i + 1) for i in range(count - 1)]
        if periodic:
            forward.append((count - 1, 0))
        backward = [(target, source) for source, target in forward]
        low = lax.ppermute(
            lax.slice_in_dim(block, block.shape[dim] - width, None, axis=dim), axis, forward
        )
        high = lax.ppermute(lax.slice_in_dim(block, 0, width, axis=dim), axis, backward)
        block = jnp.concatenate([low, block, high], axis=dim)
    return block


def banded(kernel, levels):
    zero = jnp.zeros(kernel.shape[:2] + kernel.shape[3:], kernel.dtype)
    rows = []
    for p in range(levels):
        blocks = [kernel[:, :, p - q + 1] if 0 <= p - q + 1 < 3 else zero for q in range(levels)]
        rows.append(jnp.concatenate(blocks, axis=-1))
    full = jnp.concatenate(rows, axis=-2)
    return full.reshape(9, full.shape[2], full.shape[3])


def block_diagonal(matrix, levels):
    zero = jnp.zeros_like(matrix)
    rows = [
        jnp.concatenate([matrix if p == q else zero for q in range(levels)], axis=1)
        for p in range(levels)
    ]
    return jnp.concatenate(rows, axis=0)


def gelu_slope(value):
    inner = 0.7978845608 * (value + 0.044715 * value**3)
    tval = jnp.tanh(inner)
    return 0.5 * (1.0 + tval) + 0.5 * value * (1.0 - tval * tval) * 0.7978845608 * (
        1.0 + 0.134145 * value * value
    )


def extend(field):
    wide = with_halo(field, (("lon", 1),), 1, True)
    return with_halo(wide, (("lat", 0),), 1, False)


def conv_valid(padded, matrices, rows, cols):
    taps = matrices.reshape(3, 3, matrices.shape[1], matrices.shape[2])
    out = lax.conv_general_dilated(
        padded[None],
        taps,
        (1, 1),
        "VALID",
        dimension_numbers=("NHWC", "HWIO", "NHWC"),
        preferred_element_type=jnp.float32,
    )
    return out[0]


def adjoint_valid(padded, matrices, rows, cols):
    taps = matrices.reshape(3, 3, matrices.shape[1], matrices.shape[2])
    taps = jnp.swapaxes(taps[::-1, ::-1], 2, 3)
    out = lax.conv_general_dilated(
        padded[None],
        taps,
        (1, 1),
        "VALID",
        dimension_numbers=("NHWC", "HWIO", "NHWC"),
        preferred_element_type=jnp.float32,
    )
    return out[0]


def convolve(field, matrices):
    return conv_valid(extend(field), matrices, field.shape[0], field.shape[1])


def convolve_adjoint(grads, matrices):
    return adjoint_valid(extend(grads), matrices, grads.shape[0], grads.shape[1])


def widen(coarse):
    rows, cols, feats = coarse.shape
    return jnp.broadcast_to(coarse[:, None, :, None, :], (rows, 2, cols, 2, feats)).reshape(
        rows * 2, cols * 2, feats
    )


def block_sum(fine):
    rows, cols, feats = fine.shape
    return fine.reshape(rows // 2, 2, cols // 2, 2, feats).sum(axis=(1, 3))


def split_bf16(value):
    high = lax.reduce_precision(value, exponent_bits=8, mantissa_bits=7)
    return high.astype(jnp.bfloat16), (value - high).astype(jnp.bfloat16)


def observe_kernel(got_ref, high_ref, innov_ref, grad_ref):
    fields, nslot = got_ref.shape[1], got_ref.shape[2]
    ncell, feats = high_ref.shape
    cell_ids = lax.broadcasted_iota(jnp.int32, (ncell, nslot), 0).astype(jnp.float32)
    feat_ids = lax.broadcasted_iota(jnp.int32, (feats, nslot), 0).astype(jnp.float32)
    value = high_ref[...].T
    high = value.astype(jnp.bfloat16)
    low = (value - high.astype(jnp.float32)).astype(jnp.bfloat16)
    both = jnp.concatenate([high, low], axis=0)
    grad_ref[...] = jnp.zeros(grad_ref.shape, jnp.float32)
    trans = (((1,), (1,)), ((), ()))

    def body(owner, carry):
        block = got_ref[owner]
        table = jnp.zeros((ncell, nslot), jnp.float32)
        for j in range(4):
            table = table + jnp.where(
                cell_ids == block[j : j + 1, :], block[5 + j : 6 + j, :], 0.0
            )
        t_hi = table.astype(jnp.bfloat16)
        t_lo = (table - t_hi.astype(jnp.float32)).astype(jnp.bfloat16)
        two = jnp.dot(both, t_hi, preferred_element_type=jnp.float32)
        picked = two[:feats] + two[feats:] + jnp.dot(high, t_lo, preferred_element_type=jnp.float32)
        pick = feat_ids == block[4:5, :]
        innov = jnp.sum(jnp.where(pick, picked, 0.0), axis=0, keepdims=True) - block[9:10, :]
        innov_ref[owner] = innov
        spread = jnp.where(pick, innov, 0.0)
        s_hi = spread.astype(jnp.bfloat16)
        s_lo = (spread - s_hi.astype(jnp.float32)).astype(jnp.bfloat16)
        sums = lax.dot_general(
            t_hi, jnp.concatenate([s_hi, s_lo], axis=0), trans, preferred_element_type=jnp.float32
        )
        grad_ref[...] += (
            sums[:, :feats]
            + sums[:, feats:]
            + lax.dot_general(t_lo, s_hi, trans, preferred_element_type=jnp.float32)
        )
        return carry

    lax.fori_loop(0, got_ref.shape[0], body, 0, unroll=4)


def pack(obs_cells, obs_chan, obs_weights, obs_value, obs_count):
    slots = lax.broadcasted_iota(jnp.int32, obs_chan.shape, 2)
    live = (slots < obs_count[:, :, None]).astype(jnp.float32)
    weights = obs_weights * live[..., None]
    values = obs_value * live
    packed = jnp.concatenate(
        [
            jnp.swapaxes(obs_cells, 2, 3).astype(jnp.float32),
            obs_chan[:, :, None, :].astype(jnp.float32),
            jnp.swapaxes(weights, 2, 3),
            values[:, :, None, :],
        ],
        axis=2,
    )
    return packed.reshape(packed.shape[1:])


def observe(output, got):
    rows, cols, feats = output.shape
    ncell = rows * cols
    owners, nslot = got.shape[0], got.shape[2]
    o_hi, o_lo = split_bf16(output.reshape(ncell, feats).T)
    innov, grad = pl.pallas_call(
        observe_kernel,
        out_shape=(
            jax.ShapeDtypeStruct((owners, 1, nslot), jnp.float32),
            jax.ShapeDtypeStruct((ncell, feats), jnp.float32),
        ),
    )(got, o_hi, o_lo)
    return grad.reshape(rows, cols, feats), innov


def greet(nlat, nlon):
    i = lax.axis_index("lat")
    j = lax.axis_index("lon")
    has = {-1: i > 0, 0: i >= 0, 1: i < nlat - 1}
    mesh = pl.DeviceIdType.MESH
    barrier = pltpu.get_barrier_semaphore()
    for a in (-1, 1):
        for b in (-1, 0, 1):

            @pl.when(has[a])
            def _():
                pl.semaphore_signal(
                    barrier, inc=1, device_id=((i + a) % nlat, (j + b) % nlon), device_id_type=mesh
                )

    for t in range(nlon):

        @pl.when(t != j)
        def _():
            pl.semaphore_signal(barrier, inc=1, device_id=(i, t), device_id_type=mesh)

    return (nlon - 1) + 3 * has[-1].astype(jnp.int32) + 3 * has[1].astype(jnp.int32)


def trade(width, nlat, nlon, count, x_ref, p_ref, buf, inbox, send_sem, recv_sem, p_send, p_recv):
    rows, cols = x_ref.shape[0], x_ref.shape[1]
    edge = (buf.shape[1] - cols) // 2
    i = lax.axis_index("lat")
    j = lax.axis_index("lon")
    has = {-1: i > 0, 0: i >= 0, 1: i < nlat - 1}
    mesh = pl.DeviceIdType.MESH
    dirs = [(a, b) for a in (-1, 0, 1) for b in (-1, 0, 1) if (a, b) != (0, 0)]
    pl.semaphore_wait(pltpu.get_barrier_semaphore(), count)
    src_rows = {1: pl.ds(rows - width, width), -1: pl.ds(0, width), 0: pl.ds(0, rows)}
    dst_rows = {1: pl.ds(0, width), -1: pl.ds(width + rows, width), 0: pl.ds(width, rows)}
    src_cols = {1: pl.ds(cols - edge, edge), -1: pl.ds(0, edge), 0: pl.ds(0, cols)}
    dst_cols = {1: pl.ds(0, edge), -1: pl.ds(edge + cols, edge), 0: pl.ds(edge, cols)}
    copies = []
    for k, (a, b) in enumerate(dirs):
        copy = pltpu.make_async_remote_copy(
            src_ref=x_ref.at[src_rows[a], src_cols[b]],
            dst_ref=buf.at[dst_rows[a], dst_cols[b]],
            send_sem=send_sem.at[k],
            recv_sem=recv_sem.at[k],
            device_id=((i + a) % nlat, (j + b) % nlon),
            device_id_type=mesh,
        )
        copies.append((a, copy))
        pl.when(has[a])(copy.start)
    sends = []
    for t in range(nlon):
        copy = pltpu.make_async_remote_copy(
            src_ref=p_ref.at[pl.ds(t, 1)],
            dst_ref=inbox.at[pl.ds(j, 1)],
            send_sem=p_send.at[t],
            recv_sem=p_recv.at[j],
            device_id=(i, t),
            device_id_type=mesh,
        )
        sends.append(copy)
        pl.when(t != j)(copy.start)
    for a, copy in copies:
        pl.when(has[a])(copy.wait_send)
        pl.when(has[-a])(copy.wait_recv)
    for t in range(nlon):
        arrival = pltpu.make_async_remote_copy(
            src_ref=p_ref.at[pl.ds(t, 1)],
            dst_ref=inbox.at[pl.ds(t, 1)],
            send_sem=p_send.at[t],
            recv_sem=p_recv.at[t],
            device_id=(i, t),
            device_id_type=mesh,
        )
        pl.when(t != j)(sends[t].wait_send)
        pl.when(t != j)(arrival.wait_recv)


def halo_kernel(width, nlat, nlon, x_ref, p_ref, o_ref, q_ref, buf, inbox, *sems):
    rows, cols = x_ref.shape[0], x_ref.shape[1]
    edge = (buf.shape[1] - cols) // 2
    j = lax.axis_index("lon")
    buf[...] = jnp.zeros(buf.shape, buf.dtype)
    buf[width : width + rows, edge : edge + cols, :] = x_ref[...]
    inbox[pl.ds(j, 1)] = p_ref[pl.ds(j, 1)]
    count = greet(nlat, nlon)
    trade(width, nlat, nlon, count, x_ref, p_ref, buf, inbox, *sems)
    o_ref[...] = buf[...]
    q_ref[...] = inbox[...]


def back_kernel(
    width, nlat, nlon, got_ref, high_ref, slope_ref,
    grad_ref, o_ref, q_ref, buf, inbox, innov_ref, x_src, *sems
):
    rows, cols = x_src.shape[0], x_src.shape[1]
    edge = (buf.shape[1] - cols) // 2
    j = lax.axis_index("lon")
    buf[...] = jnp.zeros(buf.shape, buf.dtype)
    count = greet(nlat, nlon)
    observe_kernel(got_ref, high_ref, innov_ref, grad_ref)
    grads = (grad_ref[...] * gelu_slope(slope_ref[...])).astype(x_src.dtype).reshape(x_src.shape)
    x_src[...] = grads
    trade(width, nlat, nlon, count, x_src, innov_ref, buf, inbox, *sems)
    buf[width : width + rows, edge : edge + cols, :] = x_src[...]
    inbox[pl.ds(j, 1)] = innov_ref[pl.ds(j, 1)]
    o_ref[...] = buf[...]
    q_ref[...] = inbox[...]


def sem_scratch(nlon):
    return [
        pltpu.SemaphoreType.DMA((8,)),
        pltpu.SemaphoreType.DMA((8,)),
        pltpu.SemaphoreType.DMA((nlon,)),
        pltpu.SemaphoreType.DMA((nlon,)),
    ]


def exchange(block, width, payload):
    rows, cols, feats = block.shape
    edge = 16
    nlat = lax.axis_size("lat")
    nlon = lax.axis_size("lon")
    full = (rows + 2 * width, cols + 2 * edge, feats)
    vmem = pl.BlockSpec(memory_space=pltpu.VMEM)
    out, got = pl.pallas_call(
        functools.partial(halo_kernel, width, nlat, nlon),
        out_shape=(
            jax.ShapeDtypeStruct(full, block.dtype),
            jax.ShapeDtypeStruct(payload.shape, payload.dtype),
        ),
        in_specs=[vmem, vmem],
        out_specs=(vmem, vmem),
        scratch_shapes=[
            pltpu.VMEM(full, block.dtype),
            pltpu.VMEM(payload.shape, payload.dtype),
        ]
        + sem_scratch(nlon),
        compiler_params=pltpu.CompilerParams(collective_id=0, has_side_effects=True),
    )(block, payload)
    return out[:, edge - width : edge + cols + width], got


def observe_and_exchange(output, got, slope, width):
    rows, cols, feats = output.shape
    ncell = rows * cols
    edge = 16
    nlat = lax.axis_size("lat")
    nlon = lax.axis_size("lon")
    owners, nslot = got.shape[0], got.shape[2]
    full = (rows + 2 * width, cols + 2 * edge, feats)
    vmem = pl.BlockSpec(memory_space=pltpu.VMEM)
    innov_shape = (owners, 1, nslot)
    grad, out, innovation = pl.pallas_call(
        functools.partial(back_kernel, width, nlat, nlon),
        out_shape=(
            jax.ShapeDtypeStruct((ncell, feats), jnp.float32),
            jax.ShapeDtypeStruct(full, jnp.bfloat16),
            jax.ShapeDtypeStruct(innov_shape, jnp.float32),
        ),
        in_specs=[vmem] * 3,
        out_specs=(vmem, vmem, vmem),
        scratch_shapes=[
            pltpu.VMEM(full, jnp.bfloat16),
            pltpu.VMEM(innov_shape, jnp.float32),
            pltpu.VMEM(innov_shape, jnp.float32),
            pltpu.VMEM((rows, cols, feats), jnp.bfloat16),
        ]
        + sem_scratch(nlon),
        compiler_params=pltpu.CompilerParams(collective_id=1, has_side_effects=True),
    )(got, output.reshape(ncell, feats), slope.reshape(ncell, feats))
    grads = out[:, edge - width : edge + cols + width]
    return grad.reshape(rows, cols, feats), grads, innovation


def inside(field, tile_rows, halo):
    rows = field.shape[0]
    first = lax.axis_index("lat") * tile_rows - halo
    where = first + lax.broadcasted_iota(jnp.int32, (rows, 1, 1), 0)
    keep = (where >= 0) & (where < lax.axis_size("lat") * tile_rows)
    return jnp.where(keep, field, jnp.zeros_like(field))


def trim(field, width):
    return field[width : field.shape[0] - width, width : field.shape[1] - width]


def shards(
    state,
    kernel_in,
    kernel_mid,
    kernel_out,
    lift,
    obs_cells,
    obs_chan,
    obs_weights,
    obs_value,
    obs_count,
):
    rows, cols = (state.shape[0], state.shape[1])
    crows = rows // 2
    mat_in = banded(kernel_in, LEV)
    mat_mid = banded(kernel_mid, LEV)
    mat_out = banded(kernel_out, LEV)
    lift_full = block_diagonal(lift, LEV)
    packed = pack(obs_cells, obs_chan, obs_weights, obs_value, obs_count)
    padded, got = exchange(state, 7, packed)
    pre_first = conv_valid(padded, mat_in, rows + 12, cols + 12)
    act_first = jax.nn.gelu(pre_first, approximate=True).astype(jnp.bfloat16)
    pooled = (block_sum(act_first.astype(jnp.float32)) * 0.25).astype(jnp.bfloat16)
    pooled = inside(pooled, crows, 3)
    pre_mid = conv_valid(pooled, mat_mid, crows + 4, cols // 2 + 4)
    act_mid = jax.nn.gelu(trim(pre_mid, 1), approximate=True).astype(jnp.bfloat16)
    lifted = jnp.einsum("ijg,gf->ijf", act_mid, lift_full, preferred_element_type=jnp.float32)
    merged = (trim(act_first, 5).astype(jnp.float32) + trim(widen(lifted), 1)).astype(jnp.bfloat16)
    merged = inside(merged, rows, 1)
    pre_last = conv_valid(merged, mat_out, rows, cols)
    slope_first = gelu_slope(trim(pre_first, 5))
    slope_mid = gelu_slope(pre_mid)
    output = state.astype(jnp.float32) + jax.nn.gelu(pre_last, approximate=True)
    grad_out, grads, innovation = observe_and_exchange(output, got, pre_last, 5)
    innovation = innovation.reshape(obs_value.shape)
    grad_merged = adjoint_valid(grads, mat_out, rows + 8, cols + 8)
    grad_coarse = block_sum(grad_merged).astype(jnp.bfloat16)
    back_mid = jnp.einsum("ijf,gf->ijg", grad_coarse, lift_full, preferred_element_type=jnp.float32)
    grad_mid = inside((back_mid * slope_mid).astype(jnp.bfloat16), crows, 2)
    grad_pooled = adjoint_valid(grad_mid, mat_mid, crows + 2, cols // 2 + 2)
    grad_first = (
        (trim(grad_merged, 3) + trim(widen(grad_pooled), 1) * 0.25) * slope_first
    ).astype(jnp.bfloat16)
    grad_first = inside(grad_first, rows, 1)
    gradient = grad_out + adjoint_valid(grad_first, mat_in, rows, cols)
    return (gradient, innovation)


def solution(mesh):
    placed = (
        P("lat", "lon", None),
        P(),
        P(),
        P(),
        P(),
        P("lat", "lon", None, None),
        P("lat", "lon", None),
        P("lat", "lon", None, None),
        P("lat", "lon", None),
        P("lat", "lon"),
    )
    return jax.shard_map(
        shards,
        mesh=mesh,
        in_specs=placed,
        out_specs=(P("lat", "lon", None), P("lat", "lon", None)),
        check_vma=False,
    )
```

```python
import jax
import jax.numpy as jnp
from jax import lax
import functools

from jax.experimental import pallas as pl
from jax.experimental.pallas import tpu as pltpu
from jax.sharding import PartitionSpec as P

C = 32
C2 = 64
LEV = 4


def with_halo(block, sides, width, periodic):
    for axis, dim in sides:
        count = lax.axis_size(axis)
        forward = [(i, i + 1) for i in range(count - 1)]
        if periodic:
            forward.append((count - 1, 0))
        backward = [(target, source) for source, target in forward]
        low = lax.ppermute(
            lax.slice_in_dim(block, block.shape[dim] - width, None, axis=dim), axis, forward
        )
        high = lax.ppermute(lax.slice_in_dim(block, 0, width, axis=dim), axis, backward)
        block = jnp.concatenate([low, block, high], axis=dim)
    return block


def banded(kernel, levels):
    zero = jnp.zeros(kernel.shape[:2] + kernel.shape[3:], kernel.dtype)
    rows = []
    for p in range(levels):
        blocks = [kernel[:, :, p - q + 1] if 0 <= p - q + 1 < 3 else zero for q in range(levels)]
        rows.append(jnp.concatenate(blocks, axis=-1))
    full = jnp.concatenate(rows, axis=-2)
    return full.reshape(9, full.shape[2], full.shape[3])


def block_diagonal(matrix, levels):
    zero = jnp.zeros_like(matrix)
    rows = [
        jnp.concatenate([matrix if p == q else zero for q in range(levels)], axis=1)
        for p in range(levels)
    ]
    return jnp.concatenate(rows, axis=0)


def gelu_slope(value):
    inner = 0.7978845608 * (value + 0.044715 * value**3)
    tval = jnp.tanh(inner)
    return 0.5 * (1.0 + tval) + 0.5 * value * (1.0 - tval * tval) * 0.7978845608 * (
        1.0 + 0.134145 * value * value
    )


def extend(field):
    wide = with_halo(field, (("lon", 1),), 1, True)
    return with_halo(wide, (("lat", 0),), 1, False)


def conv_valid(padded, matrices, rows, cols):
    taps = matrices.reshape(3, 3, matrices.shape[1], matrices.shape[2])
    out = lax.conv_general_dilated(
        padded[None],
        taps,
        (1, 1),
        "VALID",
        dimension_numbers=("NHWC", "HWIO", "NHWC"),
        preferred_element_type=jnp.float32,
    )
    return out[0]


def adjoint_valid(padded, matrices, rows, cols):
    taps = matrices.reshape(3, 3, matrices.shape[1], matrices.shape[2])
    taps = jnp.swapaxes(taps[::-1, ::-1], 2, 3)
    out = lax.conv_general_dilated(
        padded[None],
        taps,
        (1, 1),
        "VALID",
        dimension_numbers=("NHWC", "HWIO", "NHWC"),
        preferred_element_type=jnp.float32,
    )
    return out[0]


def convolve(field, matrices):
    return conv_valid(extend(field), matrices, field.shape[0], field.shape[1])


def convolve_adjoint(grads, matrices):
    return adjoint_valid(extend(grads), matrices, grads.shape[0], grads.shape[1])


def widen(coarse):
    rows, cols, feats = coarse.shape
    return jnp.broadcast_to(coarse[:, None, :, None, :], (rows, 2, cols, 2, feats)).reshape(
        rows * 2, cols * 2, feats
    )


def block_sum(fine):
    rows, cols, feats = fine.shape
    return fine.reshape(rows // 2, 2, cols // 2, 2, feats).sum(axis=(1, 3))


def split_bf16(value):
    high = lax.reduce_precision(value, exponent_bits=8, mantissa_bits=7)
    return high.astype(jnp.bfloat16), (value - high).astype(jnp.bfloat16)


def observe_kernel(got_ref, high_ref, innov_ref, grad_ref):
    fields, nslot = got_ref.shape[1], got_ref.shape[2]
    ncell, feats = high_ref.shape
    cell_ids = lax.broadcasted_iota(jnp.int32, (ncell, nslot), 0).astype(jnp.float32)
    feat_ids = lax.broadcasted_iota(jnp.int32, (feats, nslot), 0).astype(jnp.float32)
    value = high_ref[...].T
    high = value.astype(jnp.bfloat16)
    low = (value - high.astype(jnp.float32)).astype(jnp.bfloat16)
    both = jnp.concatenate([high, low], axis=0)
    grad_ref[...] = jnp.zeros(grad_ref.shape, jnp.float32)
    trans = (((1,), (1,)), ((), ()))

    def body(owner, carry):
        block = got_ref[owner]
        table = jnp.zeros((ncell, nslot), jnp.float32)
        for j in range(4):
            table = table + jnp.where(
                cell_ids == block[j : j + 1, :], block[5 + j : 6 + j, :], 0.0
            )
        t_hi = table.astype(jnp.bfloat16)
        t_lo = (table - t_hi.astype(jnp.float32)).astype(jnp.bfloat16)
        two = jnp.dot(both, t_hi, preferred_element_type=jnp.float32)
        picked = two[:feats] + two[feats:] + jnp.dot(high, t_lo, preferred_element_type=jnp.float32)
        pick = feat_ids == block[4:5, :]
        innov = jnp.sum(jnp.where(pick, picked, 0.0), axis=0, keepdims=True) - block[9:10, :]
        innov_ref[owner] = innov
        spread = jnp.where(pick, innov, 0.0)
        s_hi = spread.astype(jnp.bfloat16)
        s_lo = (spread - s_hi.astype(jnp.float32)).astype(jnp.bfloat16)
        sums = lax.dot_general(
            t_hi, jnp.concatenate([s_hi, s_lo], axis=0), trans, preferred_element_type=jnp.float32
        )
        grad_ref[...] += (
            sums[:, :feats]
            + sums[:, feats:]
            + lax.dot_general(t_lo, s_hi, trans, preferred_element_type=jnp.float32)
        )
        return carry

    lax.fori_loop(0, got_ref.shape[0], body, 0, unroll=16)


def pack(obs_cells, obs_chan, obs_weights, obs_value, obs_count):
    slots = lax.broadcasted_iota(jnp.int32, obs_chan.shape, 2)
    live = (slots < obs_count[:, :, None]).astype(jnp.float32)
    weights = obs_weights * live[..., None]
    values = obs_value * live
    packed = jnp.concatenate(
        [
            jnp.swapaxes(obs_cells, 2, 3).astype(jnp.float32),
            obs_chan[:, :, None, :].astype(jnp.float32),
            jnp.swapaxes(weights, 2, 3),
            values[:, :, None, :],
        ],
        axis=2,
    )
    return packed.reshape(packed.shape[1:])


def observe(output, got):
    rows, cols, feats = output.shape
    ncell = rows * cols
    owners, nslot = got.shape[0], got.shape[2]
    o_hi, o_lo = split_bf16(output.reshape(ncell, feats).T)
    innov, grad = pl.pallas_call(
        observe_kernel,
        out_shape=(
            jax.ShapeDtypeStruct((owners, 1, nslot), jnp.float32),
            jax.ShapeDtypeStruct((ncell, feats), jnp.float32),
        ),
    )(got, o_hi, o_lo)
    return grad.reshape(rows, cols, feats), innov


def greet(nlat, nlon):
    i = lax.axis_index("lat")
    j = lax.axis_index("lon")
    has = {-1: i > 0, 0: i >= 0, 1: i < nlat - 1}
    mesh = pl.DeviceIdType.MESH
    barrier = pltpu.get_barrier_semaphore()
    for a in (-1, 1):
        for b in (-1, 0, 1):

            @pl.when(has[a])
            def _():
                pl.semaphore_signal(
                    barrier, inc=1, device_id=((i + a) % nlat, (j + b) % nlon), device_id_type=mesh
                )

    for t in range(nlon):

        @pl.when(t != j)
        def _():
            pl.semaphore_signal(barrier, inc=1, device_id=(i, t), device_id_type=mesh)

    return (nlon - 1) + 3 * has[-1].astype(jnp.int32) + 3 * has[1].astype(jnp.int32)


def trade(width, nlat, nlon, count, x_ref, p_ref, buf, inbox, send_sem, recv_sem, p_send, p_recv):
    rows, cols = x_ref.shape[0], x_ref.shape[1]
    edge = (buf.shape[1] - cols) // 2
    i = lax.axis_index("lat")
    j = lax.axis_index("lon")
    has = {-1: i > 0, 0: i >= 0, 1: i < nlat - 1}
    mesh = pl.DeviceIdType.MESH
    dirs = [(a, b) for a in (-1, 0, 1) for b in (-1, 0, 1) if (a, b) != (0, 0)]
    pl.semaphore_wait(pltpu.get_barrier_semaphore(), count)
    src_rows = {1: pl.ds(rows - width, width), -1: pl.ds(0, width), 0: pl.ds(0, rows)}
    dst_rows = {1: pl.ds(0, width), -1: pl.ds(width + rows, width), 0: pl.ds(width, rows)}
    src_cols = {1: pl.ds(cols - edge, edge), -1: pl.ds(0, edge), 0: pl.ds(0, cols)}
    dst_cols = {1: pl.ds(0, edge), -1: pl.ds(edge + cols, edge), 0: pl.ds(edge, cols)}
    copies = []
    for k, (a, b) in enumerate(dirs):
        copy = pltpu.make_async_remote_copy(
            src_ref=x_ref.at[src_rows[a], src_cols[b]],
            dst_ref=buf.at[dst_rows[a], dst_cols[b]],
            send_sem=send_sem.at[k],
            recv_sem=recv_sem.at[k],
            device_id=((i + a) % nlat, (j + b) % nlon),
            device_id_type=mesh,
        )
        copies.append((a, copy))
        pl.when(has[a])(copy.start)
    sends = []
    for t in range(nlon):
        copy = pltpu.make_async_remote_copy(
            src_ref=p_ref.at[pl.ds(t, 1)],
            dst_ref=inbox.at[pl.ds(j, 1)],
            send_sem=p_send.at[t],
            recv_sem=p_recv.at[j],
            device_id=(i, t),
            device_id_type=mesh,
        )
        sends.append(copy)
        pl.when(t != j)(copy.start)
    for a, copy in copies:
        pl.when(has[a])(copy.wait_send)
        pl.when(has[-a])(copy.wait_recv)
    for t in range(nlon):
        arrival = pltpu.make_async_remote_copy(
            src_ref=p_ref.at[pl.ds(t, 1)],
            dst_ref=inbox.at[pl.ds(t, 1)],
            send_sem=p_send.at[t],
            recv_sem=p_recv.at[t],
            device_id=(i, t),
            device_id_type=mesh,
        )
        pl.when(t != j)(sends[t].wait_send)
        pl.when(t != j)(arrival.wait_recv)


def halo_kernel(width, nlat, nlon, x_ref, p_ref, o_ref, q_ref, buf, inbox, *sems):
    rows, cols = x_ref.shape[0], x_ref.shape[1]
    edge = (buf.shape[1] - cols) // 2
    j = lax.axis_index("lon")
    buf[...] = jnp.zeros(buf.shape, buf.dtype)
    buf[width : width + rows, edge : edge + cols, :] = x_ref[...]
    inbox[pl.ds(j, 1)] = p_ref[pl.ds(j, 1)]
    count = greet(nlat, nlon)
    trade(width, nlat, nlon, count, x_ref, p_ref, buf, inbox, *sems)
    o_ref[...] = buf[...]
    q_ref[...] = inbox[...]


def back_kernel(
    width, nlat, nlon, got_ref, high_ref, slope_ref,
    grad_ref, o_ref, q_ref, buf, inbox, innov_ref, x_src, *sems
):
    rows, cols = x_src.shape[0], x_src.shape[1]
    edge = (buf.shape[1] - cols) // 2
    j = lax.axis_index("lon")
    buf[...] = jnp.zeros(buf.shape, buf.dtype)
    count = greet(nlat, nlon)
    observe_kernel(got_ref, high_ref, innov_ref, grad_ref)
    grads = (grad_ref[...] * gelu_slope(slope_ref[...])).astype(x_src.dtype).reshape(x_src.shape)
    x_src[...] = grads
    trade(width, nlat, nlon, count, x_src, innov_ref, buf, inbox, *sems)
    buf[width : width + rows, edge : edge + cols, :] = x_src[...]
    inbox[pl.ds(j, 1)] = innov_ref[pl.ds(j, 1)]
    o_ref[...] = buf[...]
    q_ref[...] = inbox[...]


def sem_scratch(nlon):
    return [
        pltpu.SemaphoreType.DMA((8,)),
        pltpu.SemaphoreType.DMA((8,)),
        pltpu.SemaphoreType.DMA((nlon,)),
        pltpu.SemaphoreType.DMA((nlon,)),
    ]


def exchange(block, width, payload):
    rows, cols, feats = block.shape
    edge = 16
    nlat = lax.axis_size("lat")
    nlon = lax.axis_size("lon")
    full = (rows + 2 * width, cols + 2 * edge, feats)
    vmem = pl.BlockSpec(memory_space=pltpu.VMEM)
    out, got = pl.pallas_call(
        functools.partial(halo_kernel, width, nlat, nlon),
        out_shape=(
            jax.ShapeDtypeStruct(full, block.dtype),
            jax.ShapeDtypeStruct(payload.shape, payload.dtype),
        ),
        in_specs=[vmem, vmem],
        out_specs=(vmem, vmem),
        scratch_shapes=[
            pltpu.VMEM(full, block.dtype),
            pltpu.VMEM(payload.shape, payload.dtype),
        ]
        + sem_scratch(nlon),
        compiler_params=pltpu.CompilerParams(collective_id=0, has_side_effects=True),
    )(block, payload)
    return out[:, edge - width : edge + cols + width], got


def observe_and_exchange(output, got, slope, width):
    rows, cols, feats = output.shape
    ncell = rows * cols
    edge = 16
    nlat = lax.axis_size("lat")
    nlon = lax.axis_size("lon")
    owners, nslot = got.shape[0], got.shape[2]
    full = (rows + 2 * width, cols + 2 * edge, feats)
    vmem = pl.BlockSpec(memory_space=pltpu.VMEM)
    innov_shape = (owners, 1, nslot)
    grad, out, innovation = pl.pallas_call(
        functools.partial(back_kernel, width, nlat, nlon),
        out_shape=(
            jax.ShapeDtypeStruct((ncell, feats), jnp.float32),
            jax.ShapeDtypeStruct(full, jnp.bfloat16),
            jax.ShapeDtypeStruct(innov_shape, jnp.float32),
        ),
        in_specs=[vmem] * 3,
        out_specs=(vmem, vmem, vmem),
        scratch_shapes=[
            pltpu.VMEM(full, jnp.bfloat16),
            pltpu.VMEM(innov_shape, jnp.float32),
            pltpu.VMEM(innov_shape, jnp.float32),
            pltpu.VMEM((rows, cols, feats), jnp.bfloat16),
        ]
        + sem_scratch(nlon),
        compiler_params=pltpu.CompilerParams(collective_id=1, has_side_effects=True),
    )(got, output.reshape(ncell, feats), slope.reshape(ncell, feats))
    grads = out[:, edge - width : edge + cols + width]
    return grad.reshape(rows, cols, feats), grads, innovation


def inside(field, tile_rows, halo):
    rows = field.shape[0]
    first = lax.axis_index("lat") * tile_rows - halo
    where = first + lax.broadcasted_iota(jnp.int32, (rows, 1, 1), 0)
    keep = (where >= 0) & (where < lax.axis_size("lat") * tile_rows)
    return jnp.where(keep, field, jnp.zeros_like(field))


def trim(field, width):
    return field[width : field.shape[0] - width, width : field.shape[1] - width]


def shards(
    state,
    kernel_in,
    kernel_mid,
    kernel_out,
    lift,
    obs_cells,
    obs_chan,
    obs_weights,
    obs_value,
    obs_count,
):
    rows, cols = (state.shape[0], state.shape[1])
    crows = rows // 2
    mat_in = banded(kernel_in, LEV)
    mat_mid = banded(kernel_mid, LEV)
    mat_out = banded(kernel_out, LEV)
    lift_full = block_diagonal(lift, LEV)
    packed = pack(obs_cells, obs_chan, obs_weights, obs_value, obs_count)
    padded, got = exchange(state, 7, packed)
    pre_first = conv_valid(padded, mat_in, rows + 12, cols + 12)
    act_first = jax.nn.gelu(pre_first, approximate=True).astype(jnp.bfloat16)
    pooled = (block_sum(act_first.astype(jnp.float32)) * 0.25).astype(jnp.bfloat16)
    pooled = inside(pooled, crows, 3)
    pre_mid = conv_valid(pooled, mat_mid, crows + 4, cols // 2 + 4)
    act_mid = jax.nn.gelu(trim(pre_mid, 1), approximate=True).astype(jnp.bfloat16)
    lifted = jnp.einsum("ijg,gf->ijf", act_mid, lift_full, preferred_element_type=jnp.float32)
    merged = (trim(act_first, 5).astype(jnp.float32) + trim(widen(lifted), 1)).astype(jnp.bfloat16)
    merged = inside(merged, rows, 1)
    pre_last = conv_valid(merged, mat_out, rows, cols)
    slope_first = gelu_slope(trim(pre_first, 5))
    slope_mid = gelu_slope(pre_mid)
    output = state.astype(jnp.float32) + jax.nn.gelu(pre_last, approximate=True)
    grad_out, grads, innovation = observe_and_exchange(output, got, pre_last, 5)
    innovation = innovation.reshape(obs_value.shape)
    grad_merged = adjoint_valid(grads, mat_out, rows + 8, cols + 8)
    grad_coarse = block_sum(grad_merged).astype(jnp.bfloat16)
    back_mid = jnp.einsum("ijf,gf->ijg", grad_coarse, lift_full, preferred_element_type=jnp.float32)
    grad_mid = inside((back_mid * slope_mid).astype(jnp.bfloat16), crows, 2)
    grad_pooled = adjoint_valid(grad_mid, mat_mid, crows + 2, cols // 2 + 2)
    grad_first = (
        (trim(grad_merged, 3) + trim(widen(grad_pooled), 1) * 0.25) * slope_first
    ).astype(jnp.bfloat16)
    grad_first = inside(grad_first, rows, 1)
    gradient = grad_out + adjoint_valid(grad_first, mat_in, rows, cols)
    return (gradient, innovation)


def solution(mesh):
    placed = (
        P("lat", "lon", None),
        P(),
        P(),
        P(),
        P(),
        P("lat", "lon", None, None),
        P("lat", "lon", None),
        P("lat", "lon", None, None),
        P("lat", "lon", None),
        P("lat", "lon"),
    )
    return jax.shard_map(
        shards,
        mesh=mesh,
        in_specs=placed,
        out_specs=(P("lat", "lon", None), P("lat", "lon", None)),
        check_vma=False,
    )
```

```python
import jax
import jax.numpy as jnp
from jax import lax
import functools

from jax.experimental import pallas as pl
from jax.experimental.pallas import tpu as pltpu
from jax.sharding import PartitionSpec as P

C = 32
C2 = 64
LEV = 4


def with_halo(block, sides, width, periodic):
    for axis, dim in sides:
        count = lax.axis_size(axis)
        forward = [(i, i + 1) for i in range(count - 1)]
        if periodic:
            forward.append((count - 1, 0))
        backward = [(target, source) for source, target in forward]
        low = lax.ppermute(
            lax.slice_in_dim(block, block.shape[dim] - width, None, axis=dim), axis, forward
        )
        high = lax.ppermute(lax.slice_in_dim(block, 0, width, axis=dim), axis, backward)
        block = jnp.concatenate([low, block, high], axis=dim)
    return block


def banded(kernel, levels):
    zero = jnp.zeros(kernel.shape[:2] + kernel.shape[3:], kernel.dtype)
    rows = []
    for p in range(levels):
        blocks = [kernel[:, :, p - q + 1] if 0 <= p - q + 1 < 3 else zero for q in range(levels)]
        rows.append(jnp.concatenate(blocks, axis=-1))
    full = jnp.concatenate(rows, axis=-2)
    return full.reshape(9, full.shape[2], full.shape[3])


def block_diagonal(matrix, levels):
    zero = jnp.zeros_like(matrix)
    rows = [
        jnp.concatenate([matrix if p == q else zero for q in range(levels)], axis=1)
        for p in range(levels)
    ]
    return jnp.concatenate(rows, axis=0)


def gelu_slope(value):
    inner = 0.7978845608 * (value + 0.044715 * value**3)
    tval = jnp.tanh(inner)
    return 0.5 * (1.0 + tval) + 0.5 * value * (1.0 - tval * tval) * 0.7978845608 * (
        1.0 + 0.134145 * value * value
    )


def extend(field):
    wide = with_halo(field, (("lon", 1),), 1, True)
    return with_halo(wide, (("lat", 0),), 1, False)


def conv_valid(padded, matrices, rows, cols):
    taps = matrices.reshape(3, 3, matrices.shape[1], matrices.shape[2])
    out = lax.conv_general_dilated(
        padded[None],
        taps,
        (1, 1),
        "VALID",
        dimension_numbers=("NHWC", "HWIO", "NHWC"),
        preferred_element_type=jnp.float32,
    )
    return out[0]


def adjoint_valid(padded, matrices, rows, cols):
    taps = matrices.reshape(3, 3, matrices.shape[1], matrices.shape[2])
    taps = jnp.swapaxes(taps[::-1, ::-1], 2, 3)
    out = lax.conv_general_dilated(
        padded[None],
        taps,
        (1, 1),
        "VALID",
        dimension_numbers=("NHWC", "HWIO", "NHWC"),
        preferred_element_type=jnp.float32,
    )
    return out[0]


def convolve(field, matrices):
    return conv_valid(extend(field), matrices, field.shape[0], field.shape[1])


def convolve_adjoint(grads, matrices):
    return adjoint_valid(extend(grads), matrices, grads.shape[0], grads.shape[1])


def widen(coarse):
    rows, cols, feats = coarse.shape
    return jnp.broadcast_to(coarse[:, None, :, None, :], (rows, 2, cols, 2, feats)).reshape(
        rows * 2, cols * 2, feats
    )


def block_sum(fine):
    rows, cols, feats = fine.shape
    return fine.reshape(rows // 2, 2, cols // 2, 2, feats).sum(axis=(1, 3))


def split_bf16(value):
    high = lax.reduce_precision(value, exponent_bits=8, mantissa_bits=7)
    return high.astype(jnp.bfloat16), (value - high).astype(jnp.bfloat16)


def observe_kernel(got_ref, high_ref, innov_ref, grad_ref):
    fields, nslot = got_ref.shape[1], got_ref.shape[2]
    ncell, feats = high_ref.shape
    cell_ids = lax.broadcasted_iota(jnp.int32, (ncell, nslot), 0).astype(jnp.float32)
    feat_ids = lax.broadcasted_iota(jnp.int32, (feats, nslot), 0).astype(jnp.float32)
    value = high_ref[...].T
    high = value.astype(jnp.bfloat16)
    low = (value - high.astype(jnp.float32)).astype(jnp.bfloat16)
    both = jnp.concatenate([high, low], axis=0)
    grad_ref[...] = jnp.zeros(grad_ref.shape, jnp.float32)
    trans = (((1,), (1,)), ((), ()))

    def body(owner, carry):
        block = got_ref[owner]
        table = jnp.zeros((ncell, nslot), jnp.float32)
        for j in range(4):
            table = table + jnp.where(
                cell_ids == block[j : j + 1, :], block[5 + j : 6 + j, :], 0.0
            )
        t_hi = table.astype(jnp.bfloat16)
        t_lo = (table - t_hi.astype(jnp.float32)).astype(jnp.bfloat16)
        two = jnp.dot(both, t_hi, preferred_element_type=jnp.float32)
        picked = two[:feats] + two[feats:] + jnp.dot(high, t_lo, preferred_element_type=jnp.float32)
        pick = feat_ids == block[4:5, :]
        innov = jnp.sum(jnp.where(pick, picked, 0.0), axis=0, keepdims=True) - block[9:10, :]
        innov_ref[owner] = innov
        spread = jnp.where(pick, innov, 0.0)
        s_hi = spread.astype(jnp.bfloat16)
        s_lo = (spread - s_hi.astype(jnp.float32)).astype(jnp.bfloat16)
        sums = lax.dot_general(
            t_hi, jnp.concatenate([s_hi, s_lo], axis=0), trans, preferred_element_type=jnp.float32
        )
        grad_ref[...] += (
            sums[:, :feats]
            + sums[:, feats:]
            + lax.dot_general(t_lo, s_hi, trans, preferred_element_type=jnp.float32)
        )
        return carry

    lax.fori_loop(0, got_ref.shape[0], body, 0, unroll=16)


def pack(obs_cells, obs_chan, obs_weights, obs_value, obs_count):
    slots = lax.broadcasted_iota(jnp.int32, obs_chan.shape, 2)
    live = (slots < obs_count[:, :, None]).astype(jnp.float32)
    weights = obs_weights * live[..., None]
    values = obs_value * live
    packed = jnp.concatenate(
        [
            jnp.swapaxes(obs_cells, 2, 3).astype(jnp.float32),
            obs_chan[:, :, None, :].astype(jnp.float32),
            jnp.swapaxes(weights, 2, 3),
            values[:, :, None, :],
        ],
        axis=2,
    )
    return packed.reshape(packed.shape[1:])


def observe(output, got):
    rows, cols, feats = output.shape
    ncell = rows * cols
    owners, nslot = got.shape[0], got.shape[2]
    o_hi, o_lo = split_bf16(output.reshape(ncell, feats).T)
    innov, grad = pl.pallas_call(
        observe_kernel,
        out_shape=(
            jax.ShapeDtypeStruct((owners, 1, nslot), jnp.float32),
            jax.ShapeDtypeStruct((ncell, feats), jnp.float32),
        ),
    )(got, o_hi, o_lo)
    return grad.reshape(rows, cols, feats), innov


def greet(nlat, nlon):
    i = lax.axis_index("lat")
    j = lax.axis_index("lon")
    has = {-1: i > 0, 0: i >= 0, 1: i < nlat - 1}
    mesh = pl.DeviceIdType.MESH
    barrier = pltpu.get_barrier_semaphore()
    for a in (-1, 1):
        for b in (-1, 0, 1):

            @pl.when(has[a])
            def _():
                pl.semaphore_signal(
                    barrier, inc=1, device_id=((i + a) % nlat, (j + b) % nlon), device_id_type=mesh
                )

    for t in range(nlon):

        @pl.when(t != j)
        def _():
            pl.semaphore_signal(barrier, inc=1, device_id=(i, t), device_id_type=mesh)

    return (nlon - 1) + 3 * has[-1].astype(jnp.int32) + 3 * has[1].astype(jnp.int32)


def trade(width, nlat, nlon, count, x_ref, p_ref, buf, inbox, send_sem, recv_sem, p_send, p_recv):
    rows, cols = x_ref.shape[0], x_ref.shape[1]
    edge = (buf.shape[1] - cols) // 2
    i = lax.axis_index("lat")
    j = lax.axis_index("lon")
    has = {-1: i > 0, 0: i >= 0, 1: i < nlat - 1}
    mesh = pl.DeviceIdType.MESH
    dirs = [(a, b) for a in (-1, 0, 1) for b in (-1, 0, 1) if (a, b) != (0, 0)]
    pl.semaphore_wait(pltpu.get_barrier_semaphore(), count)
    src_rows = {1: pl.ds(rows - width, width), -1: pl.ds(0, width), 0: pl.ds(0, rows)}
    dst_rows = {1: pl.ds(0, width), -1: pl.ds(width + rows, width), 0: pl.ds(width, rows)}
    src_cols = {1: pl.ds(cols - edge, edge), -1: pl.ds(0, edge), 0: pl.ds(0, cols)}
    dst_cols = {1: pl.ds(0, edge), -1: pl.ds(edge + cols, edge), 0: pl.ds(edge, cols)}
    copies = []
    for k, (a, b) in enumerate(dirs):
        copy = pltpu.make_async_remote_copy(
            src_ref=x_ref.at[src_rows[a], src_cols[b]],
            dst_ref=buf.at[dst_rows[a], dst_cols[b]],
            send_sem=send_sem.at[k],
            recv_sem=recv_sem.at[k],
            device_id=((i + a) % nlat, (j + b) % nlon),
            device_id_type=mesh,
        )
        copies.append((a, copy))
        pl.when(has[a])(copy.start)
    sends = []
    for t in range(nlon):
        copy = pltpu.make_async_remote_copy(
            src_ref=p_ref.at[pl.ds(t, 1)],
            dst_ref=inbox.at[pl.ds(j, 1)],
            send_sem=p_send.at[t],
            recv_sem=p_recv.at[j],
            device_id=(i, t),
            device_id_type=mesh,
        )
        sends.append(copy)
        pl.when(t != j)(copy.start)
    for a, copy in copies:
        pl.when(has[a])(copy.wait_send)
        pl.when(has[-a])(copy.wait_recv)
    for t in range(nlon):
        arrival = pltpu.make_async_remote_copy(
            src_ref=p_ref.at[pl.ds(t, 1)],
            dst_ref=inbox.at[pl.ds(t, 1)],
            send_sem=p_send.at[t],
            recv_sem=p_recv.at[t],
            device_id=(i, t),
            device_id_type=mesh,
        )
        pl.when(t != j)(sends[t].wait_send)
        pl.when(t != j)(arrival.wait_recv)


def halo_kernel(width, nlat, nlon, x_ref, p_ref, o_ref, q_ref, buf, inbox, *sems):
    rows, cols = x_ref.shape[0], x_ref.shape[1]
    edge = (buf.shape[1] - cols) // 2
    j = lax.axis_index("lon")
    buf[...] = jnp.zeros(buf.shape, buf.dtype)
    buf[width : width + rows, edge : edge + cols, :] = x_ref[...]
    inbox[pl.ds(j, 1)] = p_ref[pl.ds(j, 1)]
    count = greet(nlat, nlon)
    trade(width, nlat, nlon, count, x_ref, p_ref, buf, inbox, *sems)
    o_ref[...] = buf[:, edge - width : edge + cols + width, :]
    q_ref[...] = inbox[...]


def back_kernel(
    width, nlat, nlon, got_ref, high_ref, slope_ref,
    grad_ref, o_ref, q_ref, buf, inbox, innov_ref, x_src, *sems
):
    rows, cols = x_src.shape[0], x_src.shape[1]
    edge = (buf.shape[1] - cols) // 2
    j = lax.axis_index("lon")
    buf[...] = jnp.zeros(buf.shape, buf.dtype)
    count = greet(nlat, nlon)
    observe_kernel(got_ref, high_ref, innov_ref, grad_ref)
    grads = (grad_ref[...] * gelu_slope(slope_ref[...])).astype(x_src.dtype).reshape(x_src.shape)
    x_src[...] = grads
    trade(width, nlat, nlon, count, x_src, innov_ref, buf, inbox, *sems)
    buf[width : width + rows, edge : edge + cols, :] = x_src[...]
    inbox[pl.ds(j, 1)] = innov_ref[pl.ds(j, 1)]
    o_ref[...] = buf[:, edge - width : edge + cols + width, :]
    q_ref[...] = inbox[...]


def sem_scratch(nlon):
    return [
        pltpu.SemaphoreType.DMA((8,)),
        pltpu.SemaphoreType.DMA((8,)),
        pltpu.SemaphoreType.DMA((nlon,)),
        pltpu.SemaphoreType.DMA((nlon,)),
    ]


def exchange(block, width, payload):
    rows, cols, feats = block.shape
    edge = 16
    nlat = lax.axis_size("lat")
    nlon = lax.axis_size("lon")
    full = (rows + 2 * width, cols + 2 * edge, feats)
    vmem = pl.BlockSpec(memory_space=pltpu.VMEM)
    out, got = pl.pallas_call(
        functools.partial(halo_kernel, width, nlat, nlon),
        out_shape=(
            jax.ShapeDtypeStruct((rows + 2 * width, cols + 2 * width, feats), block.dtype),
            jax.ShapeDtypeStruct(payload.shape, payload.dtype),
        ),
        in_specs=[vmem, vmem],
        out_specs=(vmem, vmem),
        scratch_shapes=[
            pltpu.VMEM(full, block.dtype),
            pltpu.VMEM(payload.shape, payload.dtype),
        ]
        + sem_scratch(nlon),
        compiler_params=pltpu.CompilerParams(collective_id=0, has_side_effects=True),
    )(block, payload)
    return out, got


def observe_and_exchange(output, got, slope, width):
    rows, cols, feats = output.shape
    ncell = rows * cols
    edge = 16
    nlat = lax.axis_size("lat")
    nlon = lax.axis_size("lon")
    owners, nslot = got.shape[0], got.shape[2]
    full = (rows + 2 * width, cols + 2 * edge, feats)
    vmem = pl.BlockSpec(memory_space=pltpu.VMEM)
    innov_shape = (owners, 1, nslot)
    grad, out, innovation = pl.pallas_call(
        functools.partial(back_kernel, width, nlat, nlon),
        out_shape=(
            jax.ShapeDtypeStruct((ncell, feats), jnp.float32),
            jax.ShapeDtypeStruct((rows + 2 * width, cols + 2 * width, feats), jnp.bfloat16),
            jax.ShapeDtypeStruct(innov_shape, jnp.float32),
        ),
        in_specs=[vmem] * 3,
        out_specs=(vmem, vmem, vmem),
        scratch_shapes=[
            pltpu.VMEM(full, jnp.bfloat16),
            pltpu.VMEM(innov_shape, jnp.float32),
            pltpu.VMEM(innov_shape, jnp.float32),
            pltpu.VMEM((rows, cols, feats), jnp.bfloat16),
        ]
        + sem_scratch(nlon),
        compiler_params=pltpu.CompilerParams(collective_id=1, has_side_effects=True),
    )(got, output.reshape(ncell, feats), slope.reshape(ncell, feats))
    grads = out
    return grad.reshape(rows, cols, feats), grads, innovation


def inside(field, tile_rows, halo):
    rows = field.shape[0]
    first = lax.axis_index("lat") * tile_rows - halo
    where = first + lax.broadcasted_iota(jnp.int32, (rows, 1, 1), 0)
    keep = (where >= 0) & (where < lax.axis_size("lat") * tile_rows)
    return jnp.where(keep, field, jnp.zeros_like(field))


def trim(field, width):
    return field[width : field.shape[0] - width, width : field.shape[1] - width]


def shards(
    state,
    kernel_in,
    kernel_mid,
    kernel_out,
    lift,
    obs_cells,
    obs_chan,
    obs_weights,
    obs_value,
    obs_count,
):
    rows, cols = (state.shape[0], state.shape[1])
    crows = rows // 2
    mat_in = banded(kernel_in, LEV)
    mat_mid = banded(kernel_mid, LEV)
    mat_out = banded(kernel_out, LEV)
    lift_full = block_diagonal(lift, LEV)
    packed = pack(obs_cells, obs_chan, obs_weights, obs_value, obs_count)
    padded, got = exchange(state, 7, packed)
    pre_first = conv_valid(padded, mat_in, rows + 12, cols + 12)
    act_first = jax.nn.gelu(pre_first, approximate=True).astype(jnp.bfloat16)
    pooled = (block_sum(act_first.astype(jnp.float32)) * 0.25).astype(jnp.bfloat16)
    pooled = inside(pooled, crows, 3)
    pre_mid = conv_valid(pooled, mat_mid, crows + 4, cols // 2 + 4)
    act_mid = jax.nn.gelu(trim(pre_mid, 1), approximate=True).astype(jnp.bfloat16)
    lifted = jnp.einsum("ijg,gf->ijf", act_mid, lift_full, preferred_element_type=jnp.float32)
    merged = (trim(act_first, 5).astype(jnp.float32) + trim(widen(lifted), 1)).astype(jnp.bfloat16)
    merged = inside(merged, rows, 1)
    pre_last = conv_valid(merged, mat_out, rows, cols)
    slope_first = gelu_slope(trim(pre_first, 5))
    slope_mid = gelu_slope(pre_mid)
    output = state.astype(jnp.float32) + jax.nn.gelu(pre_last, approximate=True)
    grad_out, grads, innovation = observe_and_exchange(output, got, pre_last, 5)
    innovation = innovation.reshape(obs_value.shape)
    grad_merged = adjoint_valid(grads, mat_out, rows + 8, cols + 8)
    grad_coarse = block_sum(grad_merged).astype(jnp.bfloat16)
    back_mid = jnp.einsum("ijf,gf->ijg", grad_coarse, lift_full, preferred_element_type=jnp.float32)
    grad_mid = inside((back_mid * slope_mid).astype(jnp.bfloat16), crows, 2)
    grad_pooled = adjoint_valid(grad_mid, mat_mid, crows + 2, cols // 2 + 2)
    grad_first = (
        (trim(grad_merged, 3) + trim(widen(grad_pooled), 1) * 0.25) * slope_first
    ).astype(jnp.bfloat16)
    grad_first = inside(grad_first, rows, 1)
    gradient = grad_out + adjoint_valid(grad_first, mat_in, rows, cols)
    return (gradient, innovation)


def solution(mesh):
    placed = (
        P("lat", "lon", None),
        P(),
        P(),
        P(),
        P(),
        P("lat", "lon", None, None),
        P("lat", "lon", None),
        P("lat", "lon", None, None),
        P("lat", "lon", None),
        P("lat", "lon"),
    )
    return jax.shard_map(
        shards,
        mesh=mesh,
        in_specs=placed,
        out_specs=(P("lat", "lon", None), P("lat", "lon", None)),
        check_vma=False,
    )
```

```python
import jax
import jax.numpy as jnp
from jax import lax
import functools

from jax.experimental import pallas as pl
from jax.experimental.pallas import tpu as pltpu
from jax.sharding import PartitionSpec as P

C = 32
C2 = 64
LEV = 4


def with_halo(block, sides, width, periodic):
    for axis, dim in sides:
        count = lax.axis_size(axis)
        forward = [(i, i + 1) for i in range(count - 1)]
        if periodic:
            forward.append((count - 1, 0))
        backward = [(target, source) for source, target in forward]
        low = lax.ppermute(
            lax.slice_in_dim(block, block.shape[dim] - width, None, axis=dim), axis, forward
        )
        high = lax.ppermute(lax.slice_in_dim(block, 0, width, axis=dim), axis, backward)
        block = jnp.concatenate([low, block, high], axis=dim)
    return block


def banded(kernel, levels):
    lin = jnp.arange(levels, dtype=jnp.int32)
    taps = jnp.arange(3, dtype=jnp.int32)
    select = (lin[:, None, None] - lin[None, :, None] + 1 == taps[None, None, :]).astype(
        kernel.dtype
    )
    full = jnp.einsum("pqt,abtcg->abpcqg", select, kernel, preferred_element_type=jnp.float32)
    cin = kernel.shape[3]
    cout = kernel.shape[4]
    return full.reshape(9, levels * cin, levels * cout).astype(kernel.dtype)


def block_diagonal(matrix, levels):
    zero = jnp.zeros_like(matrix)
    rows = [
        jnp.concatenate([matrix if p == q else zero for q in range(levels)], axis=1)
        for p in range(levels)
    ]
    return jnp.concatenate(rows, axis=0)


def gelu_slope(value):
    inner = 0.7978845608 * (value + 0.044715 * value**3)
    tval = jnp.tanh(inner)
    return 0.5 * (1.0 + tval) + 0.5 * value * (1.0 - tval * tval) * 0.7978845608 * (
        1.0 + 0.134145 * value * value
    )


def extend(field):
    wide = with_halo(field, (("lon", 1),), 1, True)
    return with_halo(wide, (("lat", 0),), 1, False)


def conv_valid(padded, matrices, rows, cols):
    taps = matrices.reshape(3, 3, matrices.shape[1], matrices.shape[2])
    out = lax.conv_general_dilated(
        padded[None],
        taps,
        (1, 1),
        "VALID",
        dimension_numbers=("NHWC", "HWIO", "NHWC"),
        preferred_element_type=jnp.float32,
    )
    return out[0]


def adjoint_valid(padded, matrices, rows, cols):
    taps = matrices.reshape(3, 3, matrices.shape[1], matrices.shape[2])
    taps = jnp.swapaxes(taps[::-1, ::-1], 2, 3)
    out = lax.conv_general_dilated(
        padded[None],
        taps,
        (1, 1),
        "VALID",
        dimension_numbers=("NHWC", "HWIO", "NHWC"),
        preferred_element_type=jnp.float32,
    )
    return out[0]


def convolve(field, matrices):
    return conv_valid(extend(field), matrices, field.shape[0], field.shape[1])


def convolve_adjoint(grads, matrices):
    return adjoint_valid(extend(grads), matrices, grads.shape[0], grads.shape[1])


def widen(coarse):
    rows, cols, feats = coarse.shape
    return jnp.broadcast_to(coarse[:, None, :, None, :], (rows, 2, cols, 2, feats)).reshape(
        rows * 2, cols * 2, feats
    )


def block_sum(fine):
    rows, cols, feats = fine.shape
    return fine.reshape(rows // 2, 2, cols // 2, 2, feats).sum(axis=(1, 3))


def split_bf16(value):
    high = lax.reduce_precision(value, exponent_bits=8, mantissa_bits=7)
    return high.astype(jnp.bfloat16), (value - high).astype(jnp.bfloat16)


def observe_kernel(got_ref, high_ref, innov_ref, grad_ref):
    fields, nslot = got_ref.shape[1], got_ref.shape[2]
    ncell, feats = high_ref.shape
    cell_ids = lax.broadcasted_iota(jnp.int32, (ncell, nslot), 0).astype(jnp.float32)
    feat_ids = lax.broadcasted_iota(jnp.int32, (feats, nslot), 0).astype(jnp.float32)
    value = high_ref[...].T
    high = value.astype(jnp.bfloat16)
    low = (value - high.astype(jnp.float32)).astype(jnp.bfloat16)
    both = jnp.concatenate([high, low], axis=0)
    grad_ref[...] = jnp.zeros(grad_ref.shape, jnp.float32)
    trans = (((1,), (1,)), ((), ()))

    def body(owner, carry):
        block = got_ref[owner]
        table = jnp.zeros((ncell, nslot), jnp.float32)
        for j in range(4):
            table = table + jnp.where(
                cell_ids == block[j : j + 1, :], block[5 + j : 6 + j, :], 0.0
            )
        t_hi = table.astype(jnp.bfloat16)
        t_lo = (table - t_hi.astype(jnp.float32)).astype(jnp.bfloat16)
        two = jnp.dot(both, t_hi, preferred_element_type=jnp.float32)
        picked = two[:feats] + two[feats:] + jnp.dot(high, t_lo, preferred_element_type=jnp.float32)
        pick = feat_ids == block[4:5, :]
        innov = jnp.sum(jnp.where(pick, picked, 0.0), axis=0, keepdims=True) - block[9:10, :]
        innov_ref[owner] = innov
        spread = jnp.where(pick, innov, 0.0)
        s_hi = spread.astype(jnp.bfloat16)
        s_lo = (spread - s_hi.astype(jnp.float32)).astype(jnp.bfloat16)
        sums = lax.dot_general(
            t_hi, jnp.concatenate([s_hi, s_lo], axis=0), trans, preferred_element_type=jnp.float32
        )
        grad_ref[...] += (
            sums[:, :feats]
            + sums[:, feats:]
            + lax.dot_general(t_lo, s_hi, trans, preferred_element_type=jnp.float32)
        )
        return carry

    lax.fori_loop(0, got_ref.shape[0], body, 0, unroll=16)


def pack(obs_cells, obs_chan, obs_weights, obs_value, obs_count):
    slots = lax.broadcasted_iota(jnp.int32, obs_chan.shape, 2)
    live = (slots < obs_count[:, :, None]).astype(jnp.float32)
    weights = obs_weights * live[..., None]
    values = obs_value * live
    packed = jnp.concatenate(
        [
            jnp.swapaxes(obs_cells, 2, 3).astype(jnp.float32),
            obs_chan[:, :, None, :].astype(jnp.float32),
            jnp.swapaxes(weights, 2, 3),
            values[:, :, None, :],
        ],
        axis=2,
    )
    return packed.reshape(packed.shape[1:])


def observe(output, got):
    rows, cols, feats = output.shape
    ncell = rows * cols
    owners, nslot = got.shape[0], got.shape[2]
    o_hi, o_lo = split_bf16(output.reshape(ncell, feats).T)
    innov, grad = pl.pallas_call(
        observe_kernel,
        out_shape=(
            jax.ShapeDtypeStruct((owners, 1, nslot), jnp.float32),
            jax.ShapeDtypeStruct((ncell, feats), jnp.float32),
        ),
    )(got, o_hi, o_lo)
    return grad.reshape(rows, cols, feats), innov


def greet(nlat, nlon):
    i = lax.axis_index("lat")
    j = lax.axis_index("lon")
    has = {-1: i > 0, 0: i >= 0, 1: i < nlat - 1}
    mesh = pl.DeviceIdType.MESH
    barrier = pltpu.get_barrier_semaphore()
    for a in (-1, 1):
        for b in (-1, 0, 1):

            @pl.when(has[a])
            def _():
                pl.semaphore_signal(
                    barrier, inc=1, device_id=((i + a) % nlat, (j + b) % nlon), device_id_type=mesh
                )

    for t in range(nlon):

        @pl.when(t != j)
        def _():
            pl.semaphore_signal(barrier, inc=1, device_id=(i, t), device_id_type=mesh)

    return (nlon - 1) + 3 * has[-1].astype(jnp.int32) + 3 * has[1].astype(jnp.int32)


def trade(width, nlat, nlon, count, x_ref, p_ref, buf, inbox, send_sem, recv_sem, p_send, p_recv):
    rows, cols = x_ref.shape[0], x_ref.shape[1]
    edge = (buf.shape[1] - cols) // 2
    i = lax.axis_index("lat")
    j = lax.axis_index("lon")
    has = {-1: i > 0, 0: i >= 0, 1: i < nlat - 1}
    mesh = pl.DeviceIdType.MESH
    dirs = [(a, b) for a in (-1, 0, 1) for b in (-1, 0, 1) if (a, b) != (0, 0)]
    pl.semaphore_wait(pltpu.get_barrier_semaphore(), count)
    src_rows = {1: pl.ds(rows - width, width), -1: pl.ds(0, width), 0: pl.ds(0, rows)}
    dst_rows = {1: pl.ds(0, width), -1: pl.ds(width + rows, width), 0: pl.ds(width, rows)}
    src_cols = {1: pl.ds(cols - edge, edge), -1: pl.ds(0, edge), 0: pl.ds(0, cols)}
    dst_cols = {1: pl.ds(0, edge), -1: pl.ds(edge + cols, edge), 0: pl.ds(edge, cols)}
    copies = []
    for k, (a, b) in enumerate(dirs):
        copy = pltpu.make_async_remote_copy(
            src_ref=x_ref.at[src_rows[a], src_cols[b]],
            dst_ref=buf.at[dst_rows[a], dst_cols[b]],
            send_sem=send_sem.at[k],
            recv_sem=recv_sem.at[k],
            device_id=((i + a) % nlat, (j + b) % nlon),
            device_id_type=mesh,
        )
        copies.append((a, copy))
        pl.when(has[a])(copy.start)
    sends = []
    for t in range(nlon):
        copy = pltpu.make_async_remote_copy(
            src_ref=p_ref.at[pl.ds(t, 1)],
            dst_ref=inbox.at[pl.ds(j, 1)],
            send_sem=p_send.at[t],
            recv_sem=p_recv.at[j],
            device_id=(i, t),
            device_id_type=mesh,
        )
        sends.append(copy)
        pl.when(t != j)(copy.start)
    for a, copy in copies:
        pl.when(has[a])(copy.wait_send)
        pl.when(has[-a])(copy.wait_recv)
    for t in range(nlon):
        arrival = pltpu.make_async_remote_copy(
            src_ref=p_ref.at[pl.ds(t, 1)],
            dst_ref=inbox.at[pl.ds(t, 1)],
            send_sem=p_send.at[t],
            recv_sem=p_recv.at[t],
            device_id=(i, t),
            device_id_type=mesh,
        )
        pl.when(t != j)(sends[t].wait_send)
        pl.when(t != j)(arrival.wait_recv)


def halo_kernel(width, nlat, nlon, x_ref, p_ref, o_ref, q_ref, buf, inbox, *sems):
    rows, cols = x_ref.shape[0], x_ref.shape[1]
    edge = (buf.shape[1] - cols) // 2
    j = lax.axis_index("lon")
    buf[...] = jnp.zeros(buf.shape, buf.dtype)
    buf[width : width + rows, edge : edge + cols, :] = x_ref[...]
    inbox[pl.ds(j, 1)] = p_ref[pl.ds(j, 1)]
    count = greet(nlat, nlon)
    trade(width, nlat, nlon, count, x_ref, p_ref, buf, inbox, *sems)
    o_ref[...] = buf[:, edge - width : edge + cols + width, :]
    q_ref[...] = inbox[...]


def back_kernel(
    width, nlat, nlon, got_ref, high_ref, slope_ref,
    grad_ref, o_ref, q_ref, buf, inbox, innov_ref, x_src, *sems
):
    rows, cols = x_src.shape[0], x_src.shape[1]
    edge = (buf.shape[1] - cols) // 2
    j = lax.axis_index("lon")
    buf[...] = jnp.zeros(buf.shape, buf.dtype)
    count = greet(nlat, nlon)
    observe_kernel(got_ref, high_ref, innov_ref, grad_ref)
    grads = (grad_ref[...] * gelu_slope(slope_ref[...])).astype(x_src.dtype).reshape(x_src.shape)
    x_src[...] = grads
    trade(width, nlat, nlon, count, x_src, innov_ref, buf, inbox, *sems)
    buf[width : width + rows, edge : edge + cols, :] = x_src[...]
    inbox[pl.ds(j, 1)] = innov_ref[pl.ds(j, 1)]
    o_ref[...] = buf[:, edge - width : edge + cols + width, :]
    q_ref[...] = inbox[...]


def sem_scratch(nlon):
    return [
        pltpu.SemaphoreType.DMA((8,)),
        pltpu.SemaphoreType.DMA((8,)),
        pltpu.SemaphoreType.DMA((nlon,)),
        pltpu.SemaphoreType.DMA((nlon,)),
    ]


def exchange(block, width, payload):
    rows, cols, feats = block.shape
    edge = 16
    nlat = lax.axis_size("lat")
    nlon = lax.axis_size("lon")
    full = (rows + 2 * width, cols + 2 * edge, feats)
    vmem = pl.BlockSpec(memory_space=pltpu.VMEM)
    out, got = pl.pallas_call(
        functools.partial(halo_kernel, width, nlat, nlon),
        out_shape=(
            jax.ShapeDtypeStruct((rows + 2 * width, cols + 2 * width, feats), block.dtype),
            jax.ShapeDtypeStruct(payload.shape, payload.dtype),
        ),
        in_specs=[vmem, vmem],
        out_specs=(vmem, vmem),
        scratch_shapes=[
            pltpu.VMEM(full, block.dtype),
            pltpu.VMEM(payload.shape, payload.dtype),
        ]
        + sem_scratch(nlon),
        compiler_params=pltpu.CompilerParams(collective_id=0, has_side_effects=True),
    )(block, payload)
    return out, got


def observe_and_exchange(output, got, slope, width):
    rows, cols, feats = output.shape
    ncell = rows * cols
    edge = 16
    nlat = lax.axis_size("lat")
    nlon = lax.axis_size("lon")
    owners, nslot = got.shape[0], got.shape[2]
    full = (rows + 2 * width, cols + 2 * edge, feats)
    vmem = pl.BlockSpec(memory_space=pltpu.VMEM)
    innov_shape = (owners, 1, nslot)
    grad, out, innovation = pl.pallas_call(
        functools.partial(back_kernel, width, nlat, nlon),
        out_shape=(
            jax.ShapeDtypeStruct((ncell, feats), jnp.float32),
            jax.ShapeDtypeStruct((rows + 2 * width, cols + 2 * width, feats), jnp.bfloat16),
            jax.ShapeDtypeStruct(innov_shape, jnp.float32),
        ),
        in_specs=[vmem] * 3,
        out_specs=(vmem, vmem, vmem),
        scratch_shapes=[
            pltpu.VMEM(full, jnp.bfloat16),
            pltpu.VMEM(innov_shape, jnp.float32),
            pltpu.VMEM(innov_shape, jnp.float32),
            pltpu.VMEM((rows, cols, feats), jnp.bfloat16),
        ]
        + sem_scratch(nlon),
        compiler_params=pltpu.CompilerParams(collective_id=1, has_side_effects=True),
    )(got, output.reshape(ncell, feats), slope.reshape(ncell, feats))
    grads = out
    return grad.reshape(rows, cols, feats), grads, innovation


def inside(field, tile_rows, halo):
    rows = field.shape[0]
    first = lax.axis_index("lat") * tile_rows - halo
    where = first + lax.broadcasted_iota(jnp.int32, (rows, 1, 1), 0)
    keep = (where >= 0) & (where < lax.axis_size("lat") * tile_rows)
    return jnp.where(keep, field, jnp.zeros_like(field))


def trim(field, width):
    return field[width : field.shape[0] - width, width : field.shape[1] - width]


def shards(
    state,
    kernel_in,
    kernel_mid,
    kernel_out,
    lift,
    obs_cells,
    obs_chan,
    obs_weights,
    obs_value,
    obs_count,
):
    rows, cols = (state.shape[0], state.shape[1])
    crows = rows // 2
    mat_in = banded(kernel_in, LEV)
    mat_mid = banded(kernel_mid, LEV)
    mat_out = banded(kernel_out, LEV)
    lift_full = block_diagonal(lift, LEV)
    packed = pack(obs_cells, obs_chan, obs_weights, obs_value, obs_count)
    padded, got = exchange(state, 7, packed)
    pre_first = conv_valid(padded, mat_in, rows + 12, cols + 12)
    act_first = jax.nn.gelu(pre_first, approximate=True).astype(jnp.bfloat16)
    pooled = (block_sum(act_first.astype(jnp.float32)) * 0.25).astype(jnp.bfloat16)
    pooled = inside(pooled, crows, 3)
    pre_mid = conv_valid(pooled, mat_mid, crows + 4, cols // 2 + 4)
    act_mid = jax.nn.gelu(trim(pre_mid, 1), approximate=True).astype(jnp.bfloat16)
    lifted = jnp.einsum("ijg,gf->ijf", act_mid, lift_full, preferred_element_type=jnp.float32)
    merged = (trim(act_first, 5).astype(jnp.float32) + trim(widen(lifted), 1)).astype(jnp.bfloat16)
    merged = inside(merged, rows, 1)
    pre_last = conv_valid(merged, mat_out, rows, cols)
    slope_first = gelu_slope(trim(pre_first, 5))
    slope_mid = gelu_slope(pre_mid)
    output = state.astype(jnp.float32) + jax.nn.gelu(pre_last, approximate=True)
    grad_out, grads, innovation = observe_and_exchange(output, got, pre_last, 5)
    innovation = innovation.reshape(obs_value.shape)
    grad_merged = adjoint_valid(grads, mat_out, rows + 8, cols + 8)
    grad_coarse = block_sum(grad_merged).astype(jnp.bfloat16)
    back_mid = jnp.einsum("ijf,gf->ijg", grad_coarse, lift_full, preferred_element_type=jnp.float32)
    grad_mid = inside((back_mid * slope_mid).astype(jnp.bfloat16), crows, 2)
    grad_pooled = adjoint_valid(grad_mid, mat_mid, crows + 2, cols // 2 + 2)
    grad_first = (
        (trim(grad_merged, 3) + trim(widen(grad_pooled), 1) * 0.25) * slope_first
    ).astype(jnp.bfloat16)
    grad_first = inside(grad_first, rows, 1)
    gradient = grad_out + adjoint_valid(grad_first, mat_in, rows, cols)
    return (gradient, innovation)


def solution(mesh):
    placed = (
        P("lat", "lon", None),
        P(),
        P(),
        P(),
        P(),
        P("lat", "lon", None, None),
        P("lat", "lon", None),
        P("lat", "lon", None, None),
        P("lat", "lon", None),
        P("lat", "lon"),
    )
    return jax.shard_map(
        shards,
        mesh=mesh,
        in_specs=placed,
        out_specs=(P("lat", "lon", None), P("lat", "lon", None)),
        check_vma=False,
    )
```

```python
import jax
import jax.numpy as jnp
from jax import lax
import functools

from jax.experimental import pallas as pl
from jax.experimental.pallas import tpu as pltpu
from jax.sharding import PartitionSpec as P

C = 32
C2 = 64
LEV = 4


def with_halo(block, sides, width, periodic):
    for axis, dim in sides:
        count = lax.axis_size(axis)
        forward = [(i, i + 1) for i in range(count - 1)]
        if periodic:
            forward.append((count - 1, 0))
        backward = [(target, source) for source, target in forward]
        low = lax.ppermute(
            lax.slice_in_dim(block, block.shape[dim] - width, None, axis=dim), axis, forward
        )
        high = lax.ppermute(lax.slice_in_dim(block, 0, width, axis=dim), axis, backward)
        block = jnp.concatenate([low, block, high], axis=dim)
    return block


def banded(kernel, levels):
    zero = jnp.zeros(kernel.shape[:2] + kernel.shape[3:], kernel.dtype)
    rows = []
    for p in range(levels):
        blocks = [kernel[:, :, p - q + 1] if 0 <= p - q + 1 < 3 else zero for q in range(levels)]
        rows.append(jnp.concatenate(blocks, axis=-1))
    full = jnp.concatenate(rows, axis=-2)
    return full.reshape(9, full.shape[2], full.shape[3])


def block_diagonal(matrix, levels):
    zero = jnp.zeros_like(matrix)
    rows = [
        jnp.concatenate([matrix if p == q else zero for q in range(levels)], axis=1)
        for p in range(levels)
    ]
    return jnp.concatenate(rows, axis=0)


def gelu_slope(value):
    inner = 0.7978845608 * (value + 0.044715 * value**3)
    tval = jnp.tanh(inner)
    return 0.5 * (1.0 + tval) + 0.5 * value * (1.0 - tval * tval) * 0.7978845608 * (
        1.0 + 0.134145 * value * value
    )


def extend(field):
    wide = with_halo(field, (("lon", 1),), 1, True)
    return with_halo(wide, (("lat", 0),), 1, False)


def conv_valid(padded, matrices, rows, cols):
    taps = matrices.reshape(3, 3, matrices.shape[1], matrices.shape[2])
    out = lax.conv_general_dilated(
        padded[None],
        taps,
        (1, 1),
        "VALID",
        dimension_numbers=("NHWC", "HWIO", "NHWC"),
        preferred_element_type=jnp.float32,
    )
    return out[0]


def adjoint_valid(padded, matrices, rows, cols):
    taps = matrices.reshape(3, 3, matrices.shape[1], matrices.shape[2])
    taps = jnp.swapaxes(taps[::-1, ::-1], 2, 3)
    out = lax.conv_general_dilated(
        padded[None],
        taps,
        (1, 1),
        "VALID",
        dimension_numbers=("NHWC", "HWIO", "NHWC"),
        preferred_element_type=jnp.float32,
    )
    return out[0]


def convolve(field, matrices):
    return conv_valid(extend(field), matrices, field.shape[0], field.shape[1])


def convolve_adjoint(grads, matrices):
    return adjoint_valid(extend(grads), matrices, grads.shape[0], grads.shape[1])


def widen(coarse):
    rows, cols, feats = coarse.shape
    return jnp.broadcast_to(coarse[:, None, :, None, :], (rows, 2, cols, 2, feats)).reshape(
        rows * 2, cols * 2, feats
    )


def block_sum(fine):
    rows, cols, feats = fine.shape
    return fine.reshape(rows // 2, 2, cols // 2, 2, feats).sum(axis=(1, 3))


def split_bf16(value):
    high = lax.reduce_precision(value, exponent_bits=8, mantissa_bits=7)
    return high.astype(jnp.bfloat16), (value - high).astype(jnp.bfloat16)


def observe_kernel(got_ref, high_ref, innov_ref, grad_ref):
    fields, nslot = got_ref.shape[1], got_ref.shape[2]
    ncell, feats = high_ref.shape
    cell_ids = lax.broadcasted_iota(jnp.int32, (ncell, nslot), 0).astype(jnp.float32)
    feat_ids = lax.broadcasted_iota(jnp.int32, (feats, nslot), 0).astype(jnp.float32)
    value = high_ref[...].T
    high = value.astype(jnp.bfloat16)
    low = (value - high.astype(jnp.float32)).astype(jnp.bfloat16)
    both = jnp.concatenate([high, low], axis=0)
    grad_ref[...] = jnp.zeros(grad_ref.shape, jnp.float32)
    trans = (((1,), (1,)), ((), ()))

    def body(owner, carry):
        block = got_ref[owner]
        table = jnp.zeros((ncell, nslot), jnp.float32)
        for j in range(4):
            table = table + jnp.where(
                cell_ids == block[j : j + 1, :], block[5 + j : 6 + j, :], 0.0
            )
        t_hi = table.astype(jnp.bfloat16)
        t_lo = (table - t_hi.astype(jnp.float32)).astype(jnp.bfloat16)
        two = jnp.dot(both, t_hi, preferred_element_type=jnp.float32)
        picked = two[:feats] + two[feats:] + jnp.dot(high, t_lo, preferred_element_type=jnp.float32)
        pick = feat_ids == block[4:5, :]
        innov = jnp.sum(jnp.where(pick, picked, 0.0), axis=0, keepdims=True) - block[9:10, :]
        innov_ref[owner] = innov
        spread = jnp.where(pick, innov, 0.0)
        s_hi = spread.astype(jnp.bfloat16)
        s_lo = (spread - s_hi.astype(jnp.float32)).astype(jnp.bfloat16)
        sums = lax.dot_general(
            t_hi, jnp.concatenate([s_hi, s_lo], axis=0), trans, preferred_element_type=jnp.float32
        )
        grad_ref[...] += (
            sums[:, :feats]
            + sums[:, feats:]
            + lax.dot_general(t_lo, s_hi, trans, preferred_element_type=jnp.float32)
        )
        return carry

    lax.fori_loop(0, got_ref.shape[0], body, 0, unroll=16)


def pack(obs_cells, obs_chan, obs_weights, obs_value, obs_count):
    slots = lax.broadcasted_iota(jnp.int32, obs_chan.shape, 2)
    live = (slots < obs_count[:, :, None]).astype(jnp.float32)
    weights = obs_weights * live[..., None]
    values = obs_value * live
    packed = jnp.concatenate(
        [
            jnp.swapaxes(obs_cells, 2, 3).astype(jnp.float32),
            obs_chan[:, :, None, :].astype(jnp.float32),
            jnp.swapaxes(weights, 2, 3),
            values[:, :, None, :],
        ],
        axis=2,
    )
    return packed.reshape(packed.shape[1:])


def observe(output, got):
    rows, cols, feats = output.shape
    ncell = rows * cols
    owners, nslot = got.shape[0], got.shape[2]
    o_hi, o_lo = split_bf16(output.reshape(ncell, feats).T)
    innov, grad = pl.pallas_call(
        observe_kernel,
        out_shape=(
            jax.ShapeDtypeStruct((owners, 1, nslot), jnp.float32),
            jax.ShapeDtypeStruct((ncell, feats), jnp.float32),
        ),
    )(got, o_hi, o_lo)
    return grad.reshape(rows, cols, feats), innov


def greet(nlat, nlon):
    i = lax.axis_index("lat")
    j = lax.axis_index("lon")
    has = {-1: i > 0, 0: i >= 0, 1: i < nlat - 1}
    mesh = pl.DeviceIdType.MESH
    barrier = pltpu.get_barrier_semaphore()
    for a in (-1, 1):
        for b in (-1, 0, 1):

            @pl.when(has[a])
            def _():
                pl.semaphore_signal(
                    barrier, inc=1, device_id=((i + a) % nlat, (j + b) % nlon), device_id_type=mesh
                )

    for t in range(nlon):

        @pl.when(t != j)
        def _():
            pl.semaphore_signal(barrier, inc=1, device_id=(i, t), device_id_type=mesh)

    return (nlon - 1) + 3 * has[-1].astype(jnp.int32) + 3 * has[1].astype(jnp.int32)


def trade(width, nlat, nlon, count, x_ref, p_ref, buf, inbox, send_sem, recv_sem, p_send, p_recv):
    rows, cols = x_ref.shape[0], x_ref.shape[1]
    edge = (buf.shape[1] - cols) // 2
    i = lax.axis_index("lat")
    j = lax.axis_index("lon")
    has = {-1: i > 0, 0: i >= 0, 1: i < nlat - 1}
    mesh = pl.DeviceIdType.MESH
    dirs = [(a, b) for a in (-1, 0, 1) for b in (-1, 0, 1) if (a, b) != (0, 0)]
    pl.semaphore_wait(pltpu.get_barrier_semaphore(), count)
    src_rows = {1: pl.ds(rows - width, width), -1: pl.ds(0, width), 0: pl.ds(0, rows)}
    dst_rows = {1: pl.ds(0, width), -1: pl.ds(width + rows, width), 0: pl.ds(width, rows)}
    src_cols = {1: pl.ds(cols - edge, edge), -1: pl.ds(0, edge), 0: pl.ds(0, cols)}
    dst_cols = {1: pl.ds(0, edge), -1: pl.ds(edge + cols, edge), 0: pl.ds(edge, cols)}
    sends = []
    for t in range(nlon):
        copy = pltpu.make_async_remote_copy(
            src_ref=p_ref.at[pl.ds(t, 1)],
            dst_ref=inbox.at[pl.ds(j, 1)],
            send_sem=p_send.at[t],
            recv_sem=p_recv.at[j],
            device_id=(i, t),
            device_id_type=mesh,
        )
        sends.append(copy)
        pl.when(t != j)(copy.start)
    copies = []
    for k, (a, b) in enumerate(dirs):
        copy = pltpu.make_async_remote_copy(
            src_ref=x_ref.at[src_rows[a], src_cols[b]],
            dst_ref=buf.at[dst_rows[a], dst_cols[b]],
            send_sem=send_sem.at[k],
            recv_sem=recv_sem.at[k],
            device_id=((i + a) % nlat, (j + b) % nlon),
            device_id_type=mesh,
        )
        copies.append((a, copy))
        pl.when(has[a])(copy.start)
    for a, copy in copies:
        pl.when(has[a])(copy.wait_send)
        pl.when(has[-a])(copy.wait_recv)
    for t in range(nlon):
        arrival = pltpu.make_async_remote_copy(
            src_ref=p_ref.at[pl.ds(t, 1)],
            dst_ref=inbox.at[pl.ds(t, 1)],
            send_sem=p_send.at[t],
            recv_sem=p_recv.at[t],
            device_id=(i, t),
            device_id_type=mesh,
        )
        pl.when(t != j)(sends[t].wait_send)
        pl.when(t != j)(arrival.wait_recv)


def halo_kernel(width, nlat, nlon, x_ref, p_ref, o_ref, q_ref, buf, inbox, *sems):
    rows, cols = x_ref.shape[0], x_ref.shape[1]
    edge = (buf.shape[1] - cols) // 2
    j = lax.axis_index("lon")
    buf[...] = jnp.zeros(buf.shape, buf.dtype)
    buf[width : width + rows, edge : edge + cols, :] = x_ref[...]
    inbox[pl.ds(j, 1)] = p_ref[pl.ds(j, 1)]
    count = greet(nlat, nlon)
    trade(width, nlat, nlon, count, x_ref, p_ref, buf, inbox, *sems)
    o_ref[...] = buf[:, edge - width : edge + cols + width, :]
    q_ref[...] = inbox[...]


def back_kernel(
    width, nlat, nlon, got_ref, high_ref, slope_ref,
    grad_ref, o_ref, q_ref, buf, inbox, innov_ref, x_src, *sems
):
    rows, cols = x_src.shape[0], x_src.shape[1]
    edge = (buf.shape[1] - cols) // 2
    j = lax.axis_index("lon")
    buf[...] = jnp.zeros(buf.shape, buf.dtype)
    count = greet(nlat, nlon)
    observe_kernel(got_ref, high_ref, innov_ref, grad_ref)
    grads = (grad_ref[...] * gelu_slope(slope_ref[...])).astype(x_src.dtype).reshape(x_src.shape)
    x_src[...] = grads
    trade(width, nlat, nlon, count, x_src, innov_ref, buf, inbox, *sems)
    buf[width : width + rows, edge : edge + cols, :] = x_src[...]
    inbox[pl.ds(j, 1)] = innov_ref[pl.ds(j, 1)]
    o_ref[...] = buf[:, edge - width : edge + cols + width, :]
    q_ref[...] = inbox[...]


def sem_scratch(nlon):
    return [
        pltpu.SemaphoreType.DMA((8,)),
        pltpu.SemaphoreType.DMA((8,)),
        pltpu.SemaphoreType.DMA((nlon,)),
        pltpu.SemaphoreType.DMA((nlon,)),
    ]


def exchange(block, width, payload):
    rows, cols, feats = block.shape
    edge = 16
    nlat = lax.axis_size("lat")
    nlon = lax.axis_size("lon")
    full = (rows + 2 * width, cols + 2 * edge, feats)
    vmem = pl.BlockSpec(memory_space=pltpu.VMEM)
    out, got = pl.pallas_call(
        functools.partial(halo_kernel, width, nlat, nlon),
        out_shape=(
            jax.ShapeDtypeStruct((rows + 2 * width, cols + 2 * width, feats), block.dtype),
            jax.ShapeDtypeStruct(payload.shape, payload.dtype),
        ),
        in_specs=[vmem, vmem],
        out_specs=(vmem, vmem),
        scratch_shapes=[
            pltpu.VMEM(full, block.dtype),
            pltpu.VMEM(payload.shape, payload.dtype),
        ]
        + sem_scratch(nlon),
        compiler_params=pltpu.CompilerParams(collective_id=0, has_side_effects=True),
    )(block, payload)
    return out, got


def observe_and_exchange(output, got, slope, width):
    rows, cols, feats = output.shape
    ncell = rows * cols
    edge = 16
    nlat = lax.axis_size("lat")
    nlon = lax.axis_size("lon")
    owners, nslot = got.shape[0], got.shape[2]
    full = (rows + 2 * width, cols + 2 * edge, feats)
    vmem = pl.BlockSpec(memory_space=pltpu.VMEM)
    innov_shape = (owners, 1, nslot)
    grad, out, innovation = pl.pallas_call(
        functools.partial(back_kernel, width, nlat, nlon),
        out_shape=(
            jax.ShapeDtypeStruct((ncell, feats), jnp.float32),
            jax.ShapeDtypeStruct((rows + 2 * width, cols + 2 * width, feats), jnp.bfloat16),
            jax.ShapeDtypeStruct(innov_shape, jnp.float32),
        ),
        in_specs=[vmem] * 3,
        out_specs=(vmem, vmem, vmem),
        scratch_shapes=[
            pltpu.VMEM(full, jnp.bfloat16),
            pltpu.VMEM(innov_shape, jnp.float32),
            pltpu.VMEM(innov_shape, jnp.float32),
            pltpu.VMEM((rows, cols, feats), jnp.bfloat16),
        ]
        + sem_scratch(nlon),
        compiler_params=pltpu.CompilerParams(collective_id=1, has_side_effects=True),
    )(got, output.reshape(ncell, feats), slope.reshape(ncell, feats))
    grads = out
    return grad.reshape(rows, cols, feats), grads, innovation


def inside(field, tile_rows, halo):
    rows = field.shape[0]
    first = lax.axis_index("lat") * tile_rows - halo
    where = first + lax.broadcasted_iota(jnp.int32, (rows, 1, 1), 0)
    keep = (where >= 0) & (where < lax.axis_size("lat") * tile_rows)
    return jnp.where(keep, field, jnp.zeros_like(field))


def trim(field, width):
    return field[width : field.shape[0] - width, width : field.shape[1] - width]


def shards(
    state,
    kernel_in,
    kernel_mid,
    kernel_out,
    lift,
    obs_cells,
    obs_chan,
    obs_weights,
    obs_value,
    obs_count,
):
    rows, cols = (state.shape[0], state.shape[1])
    crows = rows // 2
    mat_in = banded(kernel_in, LEV)
    mat_mid = banded(kernel_mid, LEV)
    mat_out = banded(kernel_out, LEV)
    lift_full = block_diagonal(lift, LEV)
    packed = pack(obs_cells, obs_chan, obs_weights, obs_value, obs_count)
    padded, got = exchange(state, 7, packed)
    pre_first = conv_valid(padded, mat_in, rows + 12, cols + 12)
    act_first = jax.nn.gelu(pre_first, approximate=True).astype(jnp.bfloat16)
    pooled = (block_sum(act_first.astype(jnp.float32)) * 0.25).astype(jnp.bfloat16)
    pooled = inside(pooled, crows, 3)
    pre_mid = conv_valid(pooled, mat_mid, crows + 4, cols // 2 + 4)
    act_mid = jax.nn.gelu(trim(pre_mid, 1), approximate=True).astype(jnp.bfloat16)
    lifted = jnp.einsum("ijg,gf->ijf", act_mid, lift_full, preferred_element_type=jnp.float32)
    merged = (trim(act_first, 5).astype(jnp.float32) + trim(widen(lifted), 1)).astype(jnp.bfloat16)
    merged = inside(merged, rows, 1)
    pre_last = conv_valid(merged, mat_out, rows, cols)
    slope_first = gelu_slope(trim(pre_first, 5))
    slope_mid = gelu_slope(pre_mid)
    output = state.astype(jnp.float32) + jax.nn.gelu(pre_last, approximate=True)
    grad_out, grads, innovation = observe_and_exchange(output, got, pre_last, 5)
    innovation = innovation.reshape(obs_value.shape)
    grad_merged = adjoint_valid(grads, mat_out, rows + 8, cols + 8)
    grad_coarse = block_sum(grad_merged).astype(jnp.bfloat16)
    back_mid = jnp.einsum("ijf,gf->ijg", grad_coarse, lift_full, preferred_element_type=jnp.float32)
    grad_mid = inside((back_mid * slope_mid).astype(jnp.bfloat16), crows, 2)
    grad_pooled = adjoint_valid(grad_mid, mat_mid, crows + 2, cols // 2 + 2)
    grad_first = (
        (trim(grad_merged, 3) + trim(widen(grad_pooled), 1) * 0.25) * slope_first
    ).astype(jnp.bfloat16)
    grad_first = inside(grad_first, rows, 1)
    gradient = grad_out + adjoint_valid(grad_first, mat_in, rows, cols)
    return (gradient, innovation)


def solution(mesh):
    placed = (
        P("lat", "lon", None),
        P(),
        P(),
        P(),
        P(),
        P("lat", "lon", None, None),
        P("lat", "lon", None),
        P("lat", "lon", None, None),
        P("lat", "lon", None),
        P("lat", "lon"),
    )
    return jax.shard_map(
        shards,
        mesh=mesh,
        in_specs=placed,
        out_specs=(P("lat", "lon", None), P("lat", "lon", None)),
        check_vma=False,
    )
```

```python
import jax
import jax.numpy as jnp
from jax import lax
import functools

from jax.experimental import pallas as pl
from jax.experimental.pallas import tpu as pltpu
from jax.sharding import PartitionSpec as P

C = 32
C2 = 64
LEV = 4


def with_halo(block, sides, width, periodic):
    for axis, dim in sides:
        count = lax.axis_size(axis)
        forward = [(i, i + 1) for i in range(count - 1)]
        if periodic:
            forward.append((count - 1, 0))
        backward = [(target, source) for source, target in forward]
        low = lax.ppermute(
            lax.slice_in_dim(block, block.shape[dim] - width, None, axis=dim), axis, forward
        )
        high = lax.ppermute(lax.slice_in_dim(block, 0, width, axis=dim), axis, backward)
        block = jnp.concatenate([low, block, high], axis=dim)
    return block


def banded(kernel, levels):
    zero = jnp.zeros(kernel.shape[:2] + kernel.shape[3:], kernel.dtype)
    rows = []
    for p in range(levels):
        blocks = [kernel[:, :, p - q + 1] if 0 <= p - q + 1 < 3 else zero for q in range(levels)]
        rows.append(jnp.concatenate(blocks, axis=-1))
    full = jnp.concatenate(rows, axis=-2)
    return full.reshape(9, full.shape[2], full.shape[3])


def block_diagonal(matrix, levels):
    zero = jnp.zeros_like(matrix)
    rows = [
        jnp.concatenate([matrix if p == q else zero for q in range(levels)], axis=1)
        for p in range(levels)
    ]
    return jnp.concatenate(rows, axis=0)


def gelu_slope(value):
    inner = 0.7978845608 * (value + 0.044715 * value**3)
    tval = jnp.tanh(inner)
    return 0.5 * (1.0 + tval) + 0.5 * value * (1.0 - tval * tval) * 0.7978845608 * (
        1.0 + 0.134145 * value * value
    )


def extend(field):
    wide = with_halo(field, (("lon", 1),), 1, True)
    return with_halo(wide, (("lat", 0),), 1, False)


def conv_valid(padded, matrices, rows, cols):
    taps = matrices.reshape(3, 3, matrices.shape[1], matrices.shape[2])
    out = lax.conv_general_dilated(
        padded[None],
        taps,
        (1, 1),
        "VALID",
        dimension_numbers=("NHWC", "HWIO", "NHWC"),
        preferred_element_type=jnp.float32,
    )
    return out[0]


def adjoint_valid(padded, matrices, rows, cols):
    taps = matrices.reshape(3, 3, matrices.shape[1], matrices.shape[2])
    taps = jnp.swapaxes(taps[::-1, ::-1], 2, 3)
    out = lax.conv_general_dilated(
        padded[None],
        taps,
        (1, 1),
        "VALID",
        dimension_numbers=("NHWC", "HWIO", "NHWC"),
        preferred_element_type=jnp.float32,
    )
    return out[0]


def convolve(field, matrices):
    return conv_valid(extend(field), matrices, field.shape[0], field.shape[1])


def convolve_adjoint(grads, matrices):
    return adjoint_valid(extend(grads), matrices, grads.shape[0], grads.shape[1])


def widen(coarse):
    rows, cols, feats = coarse.shape
    return jnp.broadcast_to(coarse[:, None, :, None, :], (rows, 2, cols, 2, feats)).reshape(
        rows * 2, cols * 2, feats
    )


def block_sum(fine):
    rows, cols, feats = fine.shape
    return fine.reshape(rows // 2, 2, cols // 2, 2, feats).sum(axis=(1, 3))


def split_bf16(value):
    high = lax.reduce_precision(value, exponent_bits=8, mantissa_bits=7)
    return high.astype(jnp.bfloat16), (value - high).astype(jnp.bfloat16)


def observe_kernel(got_ref, high_ref, innov_ref, grad_ref):
    fields, nslot = got_ref.shape[1], got_ref.shape[2]
    ncell, feats = high_ref.shape
    cell_ids = lax.broadcasted_iota(jnp.int32, (ncell, nslot), 0).astype(jnp.float32)
    feat_ids = lax.broadcasted_iota(jnp.int32, (feats, nslot), 0).astype(jnp.float32)
    value = high_ref[...].T
    high = value.astype(jnp.bfloat16)
    low = (value - high.astype(jnp.float32)).astype(jnp.bfloat16)
    both = jnp.concatenate([high, low], axis=0)
    grad_ref[...] = jnp.zeros(grad_ref.shape, jnp.float32)
    trans = (((1,), (1,)), ((), ()))

    def body(owner, carry):
        block = got_ref[owner]
        table = jnp.zeros((ncell, nslot), jnp.float32)
        for j in range(4):
            table = table + jnp.where(
                cell_ids == block[j : j + 1, :], block[5 + j : 6 + j, :], 0.0
            )
        t_hi = table.astype(jnp.bfloat16)
        t_lo = (table - t_hi.astype(jnp.float32)).astype(jnp.bfloat16)
        two = jnp.dot(both, t_hi, preferred_element_type=jnp.float32)
        picked = two[:feats] + two[feats:] + jnp.dot(high, t_lo, preferred_element_type=jnp.float32)
        pick = feat_ids == block[4:5, :]
        innov = jnp.sum(jnp.where(pick, picked, 0.0), axis=0, keepdims=True) - block[9:10, :]
        innov_ref[owner] = innov
        spread = jnp.where(pick, innov, 0.0)
        s_hi = spread.astype(jnp.bfloat16)
        s_lo = (spread - s_hi.astype(jnp.float32)).astype(jnp.bfloat16)
        sums = lax.dot_general(
            t_hi, jnp.concatenate([s_hi, s_lo], axis=0), trans, preferred_element_type=jnp.float32
        )
        grad_ref[...] += (
            sums[:, :feats]
            + sums[:, feats:]
            + lax.dot_general(t_lo, s_hi, trans, preferred_element_type=jnp.float32)
        )
        return carry

    lax.fori_loop(0, got_ref.shape[0], body, 0, unroll=16)


def pack(obs_cells, obs_chan, obs_weights, obs_value, obs_count):
    slots = lax.broadcasted_iota(jnp.int32, obs_chan.shape, 2)
    live = (slots < obs_count[:, :, None]).astype(jnp.float32)
    weights = obs_weights * live[..., None]
    values = obs_value * live
    packed = jnp.concatenate(
        [
            jnp.swapaxes(obs_cells, 2, 3).astype(jnp.float32),
            obs_chan[:, :, None, :].astype(jnp.float32),
            jnp.swapaxes(weights, 2, 3),
            values[:, :, None, :],
        ],
        axis=2,
    )
    return packed.reshape(packed.shape[1:])


def observe(output, got):
    rows, cols, feats = output.shape
    ncell = rows * cols
    owners, nslot = got.shape[0], got.shape[2]
    o_hi, o_lo = split_bf16(output.reshape(ncell, feats).T)
    innov, grad = pl.pallas_call(
        observe_kernel,
        out_shape=(
            jax.ShapeDtypeStruct((owners, 1, nslot), jnp.float32),
            jax.ShapeDtypeStruct((ncell, feats), jnp.float32),
        ),
    )(got, o_hi, o_lo)
    return grad.reshape(rows, cols, feats), innov


def greet(nlat, nlon):
    i = lax.axis_index("lat")
    j = lax.axis_index("lon")
    has = {-1: i > 0, 0: i >= 0, 1: i < nlat - 1}
    mesh = pl.DeviceIdType.MESH
    barrier = pltpu.get_barrier_semaphore()
    for a in (-1, 1):
        for b in (-1, 0, 1):

            @pl.when(has[a])
            def _():
                pl.semaphore_signal(
                    barrier, inc=1, device_id=((i + a) % nlat, (j + b) % nlon), device_id_type=mesh
                )

    for t in range(nlon):

        @pl.when(t != j)
        def _():
            pl.semaphore_signal(barrier, inc=1, device_id=(i, t), device_id_type=mesh)

    return (nlon - 1) + 3 * has[-1].astype(jnp.int32) + 3 * has[1].astype(jnp.int32)


def trade(width, nlat, nlon, count, x_ref, p_ref, buf, inbox, send_sem, recv_sem, p_send, p_recv):
    rows, cols = x_ref.shape[0], x_ref.shape[1]
    edge = (buf.shape[1] - cols) // 2
    i = lax.axis_index("lat")
    j = lax.axis_index("lon")
    has = {-1: i > 0, 0: i >= 0, 1: i < nlat - 1}
    mesh = pl.DeviceIdType.MESH
    dirs = [(a, b) for a in (-1, 1) for b in (-1, 1)] + [(-1, 0), (1, 0), (0, -1), (0, 1)]
    pl.semaphore_wait(pltpu.get_barrier_semaphore(), count)
    src_rows = {1: pl.ds(rows - width, width), -1: pl.ds(0, width), 0: pl.ds(0, rows)}
    dst_rows = {1: pl.ds(0, width), -1: pl.ds(width + rows, width), 0: pl.ds(width, rows)}
    src_cols = {1: pl.ds(cols - edge, edge), -1: pl.ds(0, edge), 0: pl.ds(0, cols)}
    dst_cols = {1: pl.ds(0, edge), -1: pl.ds(edge + cols, edge), 0: pl.ds(edge, cols)}
    sends = []
    for t in range(nlon):
        copy = pltpu.make_async_remote_copy(
            src_ref=p_ref.at[pl.ds(t, 1)],
            dst_ref=inbox.at[pl.ds(j, 1)],
            send_sem=p_send.at[t],
            recv_sem=p_recv.at[j],
            device_id=(i, t),
            device_id_type=mesh,
        )
        sends.append(copy)
        pl.when(t != j)(copy.start)
    copies = []
    for k, (a, b) in enumerate(dirs):
        copy = pltpu.make_async_remote_copy(
            src_ref=x_ref.at[src_rows[a], src_cols[b]],
            dst_ref=buf.at[dst_rows[a], dst_cols[b]],
            send_sem=send_sem.at[k],
            recv_sem=recv_sem.at[k],
            device_id=((i + a) % nlat, (j + b) % nlon),
            device_id_type=mesh,
        )
        copies.append((a, copy))
        pl.when(has[a])(copy.start)
    for a, copy in copies:
        pl.when(has[a])(copy.wait_send)
        pl.when(has[-a])(copy.wait_recv)
    for t in range(nlon):
        arrival = pltpu.make_async_remote_copy(
            src_ref=p_ref.at[pl.ds(t, 1)],
            dst_ref=inbox.at[pl.ds(t, 1)],
            send_sem=p_send.at[t],
            recv_sem=p_recv.at[t],
            device_id=(i, t),
            device_id_type=mesh,
        )
        pl.when(t != j)(sends[t].wait_send)
        pl.when(t != j)(arrival.wait_recv)


def halo_kernel(width, nlat, nlon, x_ref, p_ref, o_ref, q_ref, buf, inbox, *sems):
    rows, cols = x_ref.shape[0], x_ref.shape[1]
    edge = (buf.shape[1] - cols) // 2
    j = lax.axis_index("lon")
    buf[...] = jnp.zeros(buf.shape, buf.dtype)
    buf[width : width + rows, edge : edge + cols, :] = x_ref[...]
    inbox[pl.ds(j, 1)] = p_ref[pl.ds(j, 1)]
    count = greet(nlat, nlon)
    trade(width, nlat, nlon, count, x_ref, p_ref, buf, inbox, *sems)
    o_ref[...] = buf[:, edge - width : edge + cols + width, :]
    q_ref[...] = inbox[...]


def back_kernel(
    width, nlat, nlon, got_ref, high_ref, slope_ref,
    grad_ref, o_ref, q_ref, buf, inbox, innov_ref, x_src, *sems
):
    rows, cols = x_src.shape[0], x_src.shape[1]
    edge = (buf.shape[1] - cols) // 2
    j = lax.axis_index("lon")
    buf[...] = jnp.zeros(buf.shape, buf.dtype)
    count = greet(nlat, nlon)
    observe_kernel(got_ref, high_ref, innov_ref, grad_ref)
    grads = (grad_ref[...] * gelu_slope(slope_ref[...])).astype(x_src.dtype).reshape(x_src.shape)
    x_src[...] = grads
    trade(width, nlat, nlon, count, x_src, innov_ref, buf, inbox, *sems)
    buf[width : width + rows, edge : edge + cols, :] = x_src[...]
    inbox[pl.ds(j, 1)] = innov_ref[pl.ds(j, 1)]
    o_ref[...] = buf[:, edge - width : edge + cols + width, :]
    q_ref[...] = inbox[...]


def sem_scratch(nlon):
    return [
        pltpu.SemaphoreType.DMA((8,)),
        pltpu.SemaphoreType.DMA((8,)),
        pltpu.SemaphoreType.DMA((nlon,)),
        pltpu.SemaphoreType.DMA((nlon,)),
    ]


def exchange(block, width, payload):
    rows, cols, feats = block.shape
    edge = 16
    nlat = lax.axis_size("lat")
    nlon = lax.axis_size("lon")
    full = (rows + 2 * width, cols + 2 * edge, feats)
    vmem = pl.BlockSpec(memory_space=pltpu.VMEM)
    out, got = pl.pallas_call(
        functools.partial(halo_kernel, width, nlat, nlon),
        out_shape=(
            jax.ShapeDtypeStruct((rows + 2 * width, cols + 2 * width, feats), block.dtype),
            jax.ShapeDtypeStruct(payload.shape, payload.dtype),
        ),
        in_specs=[vmem, vmem],
        out_specs=(vmem, vmem),
        scratch_shapes=[
            pltpu.VMEM(full, block.dtype),
            pltpu.VMEM(payload.shape, payload.dtype),
        ]
        + sem_scratch(nlon),
        compiler_params=pltpu.CompilerParams(collective_id=0, has_side_effects=True),
    )(block, payload)
    return out, got


def observe_and_exchange(output, got, slope, width):
    rows, cols, feats = output.shape
    ncell = rows * cols
    edge = 16
    nlat = lax.axis_size("lat")
    nlon = lax.axis_size("lon")
    owners, nslot = got.shape[0], got.shape[2]
    full = (rows + 2 * width, cols + 2 * edge, feats)
    vmem = pl.BlockSpec(memory_space=pltpu.VMEM)
    innov_shape = (owners, 1, nslot)
    grad, out, innovation = pl.pallas_call(
        functools.partial(back_kernel, width, nlat, nlon),
        out_shape=(
            jax.ShapeDtypeStruct((ncell, feats), jnp.float32),
            jax.ShapeDtypeStruct((rows + 2 * width, cols + 2 * width, feats), jnp.bfloat16),
            jax.ShapeDtypeStruct(innov_shape, jnp.float32),
        ),
        in_specs=[vmem] * 3,
        out_specs=(vmem, vmem, vmem),
        scratch_shapes=[
            pltpu.VMEM(full, jnp.bfloat16),
            pltpu.VMEM(innov_shape, jnp.float32),
            pltpu.VMEM(innov_shape, jnp.float32),
            pltpu.VMEM((rows, cols, feats), jnp.bfloat16),
        ]
        + sem_scratch(nlon),
        compiler_params=pltpu.CompilerParams(collective_id=1, has_side_effects=True),
    )(got, output.reshape(ncell, feats), slope.reshape(ncell, feats))
    grads = out
    return grad.reshape(rows, cols, feats), grads, innovation


def inside(field, tile_rows, halo):
    rows = field.shape[0]
    first = lax.axis_index("lat") * tile_rows - halo
    where = first + lax.broadcasted_iota(jnp.int32, (rows, 1, 1), 0)
    keep = (where >= 0) & (where < lax.axis_size("lat") * tile_rows)
    return jnp.where(keep, field, jnp.zeros_like(field))


def trim(field, width):
    return field[width : field.shape[0] - width, width : field.shape[1] - width]


def shards(
    state,
    kernel_in,
    kernel_mid,
    kernel_out,
    lift,
    obs_cells,
    obs_chan,
    obs_weights,
    obs_value,
    obs_count,
):
    rows, cols = (state.shape[0], state.shape[1])
    crows = rows // 2
    mat_in = banded(kernel_in, LEV)
    mat_mid = banded(kernel_mid, LEV)
    mat_out = banded(kernel_out, LEV)
    lift_full = block_diagonal(lift, LEV)
    packed = pack(obs_cells, obs_chan, obs_weights, obs_value, obs_count)
    padded, got = exchange(state, 7, packed)
    pre_first = conv_valid(padded, mat_in, rows + 12, cols + 12)
    act_first = jax.nn.gelu(pre_first, approximate=True).astype(jnp.bfloat16)
    pooled = (block_sum(act_first.astype(jnp.float32)) * 0.25).astype(jnp.bfloat16)
    pooled = inside(pooled, crows, 3)
    pre_mid = conv_valid(pooled, mat_mid, crows + 4, cols // 2 + 4)
    act_mid = jax.nn.gelu(trim(pre_mid, 1), approximate=True).astype(jnp.bfloat16)
    lifted = jnp.einsum("ijg,gf->ijf", act_mid, lift_full, preferred_element_type=jnp.float32)
    merged = (trim(act_first, 5).astype(jnp.float32) + trim(widen(lifted), 1)).astype(jnp.bfloat16)
    merged = inside(merged, rows, 1)
    pre_last = conv_valid(merged, mat_out, rows, cols)
    slope_first = gelu_slope(trim(pre_first, 5))
    slope_mid = gelu_slope(pre_mid)
    output = state.astype(jnp.float32) + jax.nn.gelu(pre_last, approximate=True)
    grad_out, grads, innovation = observe_and_exchange(output, got, pre_last, 5)
    innovation = innovation.reshape(obs_value.shape)
    grad_merged = adjoint_valid(grads, mat_out, rows + 8, cols + 8)
    grad_coarse = block_sum(grad_merged).astype(jnp.bfloat16)
    back_mid = jnp.einsum("ijf,gf->ijg", grad_coarse, lift_full, preferred_element_type=jnp.float32)
    grad_mid = inside((back_mid * slope_mid).astype(jnp.bfloat16), crows, 2)
    grad_pooled = adjoint_valid(grad_mid, mat_mid, crows + 2, cols // 2 + 2)
    grad_first = (
        (trim(grad_merged, 3) + trim(widen(grad_pooled), 1) * 0.25) * slope_first
    ).astype(jnp.bfloat16)
    grad_first = inside(grad_first, rows, 1)
    gradient = grad_out + adjoint_valid(grad_first, mat_in, rows, cols)
    return (gradient, innovation)


def solution(mesh):
    placed = (
        P("lat", "lon", None),
        P(),
        P(),
        P(),
        P(),
        P("lat", "lon", None, None),
        P("lat", "lon", None),
        P("lat", "lon", None, None),
        P("lat", "lon", None),
        P("lat", "lon"),
    )
    return jax.shard_map(
        shards,
        mesh=mesh,
        in_specs=placed,
        out_specs=(P("lat", "lon", None), P("lat", "lon", None)),
        check_vma=False,
    )
```

```python
import jax
import jax.numpy as jnp
from jax import lax
import functools

from jax.experimental import pallas as pl
from jax.experimental.pallas import tpu as pltpu
from jax.sharding import PartitionSpec as P

C = 32
C2 = 64
LEV = 4


def with_halo(block, sides, width, periodic):
    for axis, dim in sides:
        count = lax.axis_size(axis)
        forward = [(i, i + 1) for i in range(count - 1)]
        if periodic:
            forward.append((count - 1, 0))
        backward = [(target, source) for source, target in forward]
        low = lax.ppermute(
            lax.slice_in_dim(block, block.shape[dim] - width, None, axis=dim), axis, forward
        )
        high = lax.ppermute(lax.slice_in_dim(block, 0, width, axis=dim), axis, backward)
        block = jnp.concatenate([low, block, high], axis=dim)
    return block


def banded(kernel, levels):
    zero = jnp.zeros(kernel.shape[:2] + kernel.shape[3:], kernel.dtype)
    rows = []
    for p in range(levels):
        blocks = [kernel[:, :, p - q + 1] if 0 <= p - q + 1 < 3 else zero for q in range(levels)]
        rows.append(jnp.concatenate(blocks, axis=-1))
    full = jnp.concatenate(rows, axis=-2)
    return full.reshape(9, full.shape[2], full.shape[3])


def block_diagonal(matrix, levels):
    zero = jnp.zeros_like(matrix)
    rows = [
        jnp.concatenate([matrix if p == q else zero for q in range(levels)], axis=1)
        for p in range(levels)
    ]
    return jnp.concatenate(rows, axis=0)


def gelu_slope(value):
    inner = 0.7978845608 * (value + 0.044715 * value**3)
    tval = jnp.tanh(inner)
    return 0.5 * (1.0 + tval) + 0.5 * value * (1.0 - tval * tval) * 0.7978845608 * (
        1.0 + 0.134145 * value * value
    )


def extend(field):
    wide = with_halo(field, (("lon", 1),), 1, True)
    return with_halo(wide, (("lat", 0),), 1, False)


def conv_valid(padded, matrices, rows, cols):
    taps = matrices.reshape(3, 3, matrices.shape[1], matrices.shape[2])
    out = lax.conv_general_dilated(
        padded[None],
        taps,
        (1, 1),
        "VALID",
        dimension_numbers=("NHWC", "HWIO", "NHWC"),
        preferred_element_type=jnp.float32,
    )
    return out[0]


def adjoint_valid(padded, matrices, rows, cols):
    taps = matrices.reshape(3, 3, matrices.shape[1], matrices.shape[2])
    taps = jnp.swapaxes(taps[::-1, ::-1], 2, 3)
    out = lax.conv_general_dilated(
        padded[None],
        taps,
        (1, 1),
        "VALID",
        dimension_numbers=("NHWC", "HWIO", "NHWC"),
        preferred_element_type=jnp.float32,
    )
    return out[0]


def convolve(field, matrices):
    return conv_valid(extend(field), matrices, field.shape[0], field.shape[1])


def convolve_adjoint(grads, matrices):
    return adjoint_valid(extend(grads), matrices, grads.shape[0], grads.shape[1])


def widen(coarse):
    rows, cols, feats = coarse.shape
    return jnp.broadcast_to(coarse[:, None, :, None, :], (rows, 2, cols, 2, feats)).reshape(
        rows * 2, cols * 2, feats
    )


def block_sum(fine):
    rows, cols, feats = fine.shape
    return fine.reshape(rows // 2, 2, cols // 2, 2, feats).sum(axis=(1, 3))


def split_bf16(value):
    high = lax.reduce_precision(value, exponent_bits=8, mantissa_bits=7)
    return high.astype(jnp.bfloat16), (value - high).astype(jnp.bfloat16)


def observe_kernel(got_ref, high_ref, innov_ref, grad_ref):
    fields, nslot = got_ref.shape[1], got_ref.shape[2]
    ncell, feats = high_ref.shape
    cell_ids = lax.broadcasted_iota(jnp.int32, (ncell, nslot), 0).astype(jnp.float32)
    feat_ids = lax.broadcasted_iota(jnp.int32, (feats, nslot), 0).astype(jnp.float32)
    value = high_ref[...].T
    high = value.astype(jnp.bfloat16)
    low = (value - high.astype(jnp.float32)).astype(jnp.bfloat16)
    both = jnp.concatenate([high, low], axis=0)
    grad_ref[...] = jnp.zeros(grad_ref.shape, jnp.float32)
    trans = (((1,), (1,)), ((), ()))

    def body(owner, carry):
        block = got_ref[owner]
        table = jnp.zeros((ncell, nslot), jnp.float32)
        for j in range(4):
            table = table + jnp.where(
                cell_ids == block[j : j + 1, :], block[5 + j : 6 + j, :], 0.0
            )
        t_hi = table.astype(jnp.bfloat16)
        t_lo = (table - t_hi.astype(jnp.float32)).astype(jnp.bfloat16)
        two = jnp.dot(both, t_hi, preferred_element_type=jnp.float32)
        picked = two[:feats] + two[feats:] + jnp.dot(high, t_lo, preferred_element_type=jnp.float32)
        pick = feat_ids == block[4:5, :]
        innov = jnp.sum(jnp.where(pick, picked, 0.0), axis=0, keepdims=True) - block[9:10, :]
        innov_ref[owner] = innov
        spread = jnp.where(pick, innov, 0.0)
        s_hi = spread.astype(jnp.bfloat16)
        s_lo = (spread - s_hi.astype(jnp.float32)).astype(jnp.bfloat16)
        sums = lax.dot_general(
            t_hi, jnp.concatenate([s_hi, s_lo], axis=0), trans, preferred_element_type=jnp.float32
        )
        grad_ref[...] += (
            sums[:, :feats]
            + sums[:, feats:]
            + lax.dot_general(t_lo, s_hi, trans, preferred_element_type=jnp.float32)
        )
        return carry

    lax.fori_loop(0, got_ref.shape[0], body, 0, unroll=16)


def pack(obs_cells, obs_chan, obs_weights, obs_value, obs_count):
    slots = lax.broadcasted_iota(jnp.int32, obs_chan.shape, 2)
    live = (slots < obs_count[:, :, None]).astype(jnp.float32)
    weights = obs_weights * live[..., None]
    values = obs_value * live
    packed = jnp.concatenate(
        [
            jnp.swapaxes(obs_cells, 2, 3).astype(jnp.float32),
            obs_chan[:, :, None, :].astype(jnp.float32),
            jnp.swapaxes(weights, 2, 3),
            values[:, :, None, :],
        ],
        axis=2,
    )
    return packed.reshape(packed.shape[1:])


def observe(output, got):
    rows, cols, feats = output.shape
    ncell = rows * cols
    owners, nslot = got.shape[0], got.shape[2]
    o_hi, o_lo = split_bf16(output.reshape(ncell, feats).T)
    innov, grad = pl.pallas_call(
        observe_kernel,
        out_shape=(
            jax.ShapeDtypeStruct((owners, 1, nslot), jnp.float32),
            jax.ShapeDtypeStruct((ncell, feats), jnp.float32),
        ),
    )(got, o_hi, o_lo)
    return grad.reshape(rows, cols, feats), innov


def greet(nlat, nlon):
    i = lax.axis_index("lat")
    j = lax.axis_index("lon")
    has = {-1: i > 0, 0: i >= 0, 1: i < nlat - 1}
    mesh = pl.DeviceIdType.MESH
    barrier = pltpu.get_barrier_semaphore()
    for a in (-1, 1):
        for b in (-1, 0, 1):

            @pl.when(has[a])
            def _():
                pl.semaphore_signal(
                    barrier, inc=1, device_id=((i + a) % nlat, (j + b) % nlon), device_id_type=mesh
                )

    for t in range(nlon):

        @pl.when(t != j)
        def _():
            pl.semaphore_signal(barrier, inc=1, device_id=(i, t), device_id_type=mesh)

    return (nlon - 1) + 3 * has[-1].astype(jnp.int32) + 3 * has[1].astype(jnp.int32)


def trade(width, nlat, nlon, count, x_ref, p_ref, buf, inbox, send_sem, recv_sem, p_send, p_recv):
    rows, cols = x_ref.shape[0], x_ref.shape[1]
    edge = (buf.shape[1] - cols) // 2
    i = lax.axis_index("lat")
    j = lax.axis_index("lon")
    has = {-1: i > 0, 0: i >= 0, 1: i < nlat - 1}
    mesh = pl.DeviceIdType.MESH
    dirs = [(a, b) for a in (-1, 1) for b in (-1, 1)] + [(-1, 0), (1, 0), (0, -1), (0, 1)]
    pl.semaphore_wait(pltpu.get_barrier_semaphore(), count)
    src_rows = {1: pl.ds(rows - width, width), -1: pl.ds(0, width), 0: pl.ds(0, rows)}
    dst_rows = {1: pl.ds(0, width), -1: pl.ds(width + rows, width), 0: pl.ds(width, rows)}
    src_cols = {1: pl.ds(cols - edge, edge), -1: pl.ds(0, edge), 0: pl.ds(0, cols)}
    dst_cols = {1: pl.ds(0, edge), -1: pl.ds(edge + cols, edge), 0: pl.ds(edge, cols)}
    order = sorted(range(1, nlon), key=lambda d: -min(d, nlon - d))
    for d in order:
        t = (j + d) % nlon
        pltpu.make_async_remote_copy(
            src_ref=p_ref.at[pl.ds(t, 1)],
            dst_ref=inbox.at[pl.ds(j, 1)],
            send_sem=p_send.at[t],
            recv_sem=p_recv.at[j],
            device_id=(i, t),
            device_id_type=mesh,
        ).start()
    sends = [
        pltpu.make_async_remote_copy(
            src_ref=p_ref.at[pl.ds(t, 1)],
            dst_ref=inbox.at[pl.ds(j, 1)],
            send_sem=p_send.at[t],
            recv_sem=p_recv.at[j],
            device_id=(i, t),
            device_id_type=mesh,
        )
        for t in range(nlon)
    ]
    copies = []
    for k, (a, b) in enumerate(dirs):
        copy = pltpu.make_async_remote_copy(
            src_ref=x_ref.at[src_rows[a], src_cols[b]],
            dst_ref=buf.at[dst_rows[a], dst_cols[b]],
            send_sem=send_sem.at[k],
            recv_sem=recv_sem.at[k],
            device_id=((i + a) % nlat, (j + b) % nlon),
            device_id_type=mesh,
        )
        copies.append((a, copy))
        pl.when(has[a])(copy.start)
    for a, copy in copies:
        pl.when(has[a])(copy.wait_send)
        pl.when(has[-a])(copy.wait_recv)
    for t in range(nlon):
        arrival = pltpu.make_async_remote_copy(
            src_ref=p_ref.at[pl.ds(t, 1)],
            dst_ref=inbox.at[pl.ds(t, 1)],
            send_sem=p_send.at[t],
            recv_sem=p_recv.at[t],
            device_id=(i, t),
            device_id_type=mesh,
        )
        pl.when(t != j)(sends[t].wait_send)
        pl.when(t != j)(arrival.wait_recv)


def halo_kernel(width, nlat, nlon, x_ref, p_ref, o_ref, q_ref, buf, inbox, *sems):
    rows, cols = x_ref.shape[0], x_ref.shape[1]
    edge = (buf.shape[1] - cols) // 2
    j = lax.axis_index("lon")
    buf[...] = jnp.zeros(buf.shape, buf.dtype)
    buf[width : width + rows, edge : edge + cols, :] = x_ref[...]
    inbox[pl.ds(j, 1)] = p_ref[pl.ds(j, 1)]
    count = greet(nlat, nlon)
    trade(width, nlat, nlon, count, x_ref, p_ref, buf, inbox, *sems)
    o_ref[...] = buf[:, edge - width : edge + cols + width, :]
    q_ref[...] = inbox[...]


def back_kernel(
    width, nlat, nlon, got_ref, high_ref, slope_ref,
    grad_ref, o_ref, q_ref, buf, inbox, innov_ref, x_src, *sems
):
    rows, cols = x_src.shape[0], x_src.shape[1]
    edge = (buf.shape[1] - cols) // 2
    j = lax.axis_index("lon")
    buf[...] = jnp.zeros(buf.shape, buf.dtype)
    count = greet(nlat, nlon)
    observe_kernel(got_ref, high_ref, innov_ref, grad_ref)
    grads = (grad_ref[...] * gelu_slope(slope_ref[...])).astype(x_src.dtype).reshape(x_src.shape)
    x_src[...] = grads
    trade(width, nlat, nlon, count, x_src, innov_ref, buf, inbox, *sems)
    buf[width : width + rows, edge : edge + cols, :] = x_src[...]
    inbox[pl.ds(j, 1)] = innov_ref[pl.ds(j, 1)]
    o_ref[...] = buf[:, edge - width : edge + cols + width, :]
    q_ref[...] = inbox[...]


def sem_scratch(nlon):
    return [
        pltpu.SemaphoreType.DMA((8,)),
        pltpu.SemaphoreType.DMA((8,)),
        pltpu.SemaphoreType.DMA((nlon,)),
        pltpu.SemaphoreType.DMA((nlon,)),
    ]


def exchange(block, width, payload):
    rows, cols, feats = block.shape
    edge = 16
    nlat = lax.axis_size("lat")
    nlon = lax.axis_size("lon")
    full = (rows + 2 * width, cols + 2 * edge, feats)
    vmem = pl.BlockSpec(memory_space=pltpu.VMEM)
    out, got = pl.pallas_call(
        functools.partial(halo_kernel, width, nlat, nlon),
        out_shape=(
            jax.ShapeDtypeStruct((rows + 2 * width, cols + 2 * width, feats), block.dtype),
            jax.ShapeDtypeStruct(payload.shape, payload.dtype),
        ),
        in_specs=[vmem, vmem],
        out_specs=(vmem, vmem),
        scratch_shapes=[
            pltpu.VMEM(full, block.dtype),
            pltpu.VMEM(payload.shape, payload.dtype),
        ]
        + sem_scratch(nlon),
        compiler_params=pltpu.CompilerParams(collective_id=0, has_side_effects=True),
    )(block, payload)
    return out, got


def observe_and_exchange(output, got, slope, width):
    rows, cols, feats = output.shape
    ncell = rows * cols
    edge = 16
    nlat = lax.axis_size("lat")
    nlon = lax.axis_size("lon")
    owners, nslot = got.shape[0], got.shape[2]
    full = (rows + 2 * width, cols + 2 * edge, feats)
    vmem = pl.BlockSpec(memory_space=pltpu.VMEM)
    innov_shape = (owners, 1, nslot)
    grad, out, innovation = pl.pallas_call(
        functools.partial(back_kernel, width, nlat, nlon),
        out_shape=(
            jax.ShapeDtypeStruct((ncell, feats), jnp.float32),
            jax.ShapeDtypeStruct((rows + 2 * width, cols + 2 * width, feats), jnp.bfloat16),
            jax.ShapeDtypeStruct(innov_shape, jnp.float32),
        ),
        in_specs=[vmem] * 3,
        out_specs=(vmem, vmem, vmem),
        scratch_shapes=[
            pltpu.VMEM(full, jnp.bfloat16),
            pltpu.VMEM(innov_shape, jnp.float32),
            pltpu.VMEM(innov_shape, jnp.float32),
            pltpu.VMEM((rows, cols, feats), jnp.bfloat16),
        ]
        + sem_scratch(nlon),
        compiler_params=pltpu.CompilerParams(collective_id=1, has_side_effects=True),
    )(got, output.reshape(ncell, feats), slope.reshape(ncell, feats))
    grads = out
    return grad.reshape(rows, cols, feats), grads, innovation


def inside(field, tile_rows, halo):
    rows = field.shape[0]
    first = lax.axis_index("lat") * tile_rows - halo
    where = first + lax.broadcasted_iota(jnp.int32, (rows, 1, 1), 0)
    keep = (where >= 0) & (where < lax.axis_size("lat") * tile_rows)
    return jnp.where(keep, field, jnp.zeros_like(field))


def trim(field, width):
    return field[width : field.shape[0] - width, width : field.shape[1] - width]


def shards(
    state,
    kernel_in,
    kernel_mid,
    kernel_out,
    lift,
    obs_cells,
    obs_chan,
    obs_weights,
    obs_value,
    obs_count,
):
    rows, cols = (state.shape[0], state.shape[1])
    crows = rows // 2
    mat_in = banded(kernel_in, LEV)
    mat_mid = banded(kernel_mid, LEV)
    mat_out = banded(kernel_out, LEV)
    lift_full = block_diagonal(lift, LEV)
    packed = pack(obs_cells, obs_chan, obs_weights, obs_value, obs_count)
    padded, got = exchange(state, 7, packed)
    pre_first = conv_valid(padded, mat_in, rows + 12, cols + 12)
    act_first = jax.nn.gelu(pre_first, approximate=True).astype(jnp.bfloat16)
    pooled = (block_sum(act_first.astype(jnp.float32)) * 0.25).astype(jnp.bfloat16)
    pooled = inside(pooled, crows, 3)
    pre_mid = conv_valid(pooled, mat_mid, crows + 4, cols // 2 + 4)
    act_mid = jax.nn.gelu(trim(pre_mid, 1), approximate=True).astype(jnp.bfloat16)
    lifted = jnp.einsum("ijg,gf->ijf", act_mid, lift_full, preferred_element_type=jnp.float32)
    merged = (trim(act_first, 5).astype(jnp.float32) + trim(widen(lifted), 1)).astype(jnp.bfloat16)
    merged = inside(merged, rows, 1)
    pre_last = conv_valid(merged, mat_out, rows, cols)
    slope_first = gelu_slope(trim(pre_first, 5))
    slope_mid = gelu_slope(pre_mid)
    output = state.astype(jnp.float32) + jax.nn.gelu(pre_last, approximate=True)
    grad_out, grads, innovation = observe_and_exchange(output, got, pre_last, 5)
    innovation = innovation.reshape(obs_value.shape)
    grad_merged = adjoint_valid(grads, mat_out, rows + 8, cols + 8)
    grad_coarse = block_sum(grad_merged).astype(jnp.bfloat16)
    back_mid = jnp.einsum("ijf,gf->ijg", grad_coarse, lift_full, preferred_element_type=jnp.float32)
    grad_mid = inside((back_mid * slope_mid).astype(jnp.bfloat16), crows, 2)
    grad_pooled = adjoint_valid(grad_mid, mat_mid, crows + 2, cols // 2 + 2)
    grad_first = (
        (trim(grad_merged, 3) + trim(widen(grad_pooled), 1) * 0.25) * slope_first
    ).astype(jnp.bfloat16)
    grad_first = inside(grad_first, rows, 1)
    gradient = grad_out + adjoint_valid(grad_first, mat_in, rows, cols)
    return (gradient, innovation)


def solution(mesh):
    placed = (
        P("lat", "lon", None),
        P(),
        P(),
        P(),
        P(),
        P("lat", "lon", None, None),
        P("lat", "lon", None),
        P("lat", "lon", None, None),
        P("lat", "lon", None),
        P("lat", "lon"),
    )
    return jax.shard_map(
        shards,
        mesh=mesh,
        in_specs=placed,
        out_specs=(P("lat", "lon", None), P("lat", "lon", None)),
        check_vma=False,
    )
```
